32 devices in a mesh: band: 8 (over z, y), tok: 4 (over x, core).
Axes of the slice: x: 2, y: 2, z: 4, core: 2. Of those that a mesh axis runs over, the one named last changes fastest.
Arguments:
- pixels: bfloat16 [4, 8, 32, 256, 256], P('tok', None, 'band'), may hold values from -6 to 6
- wave_table: float32 [64], replicated, may hold values from 0.4 to 12
- wave_index: int32 [4, 8, 32], P('tok'), may hold values from 0 to 63
- patch_count: int32 [4, 8], P('tok', 'band'), may hold values from 49 to 256, as said below
- d_out: bfloat16 [4, 8, 256, 768], P('tok', 'band'), may hold values from -6 to 6
- gen_w: bfloat16 [196608, 128], P(('band', 'tok')), may hold values from -0.5 to 0.5
- gen_b: float32 [128, 768], replicated, may hold values from -0.25 to 0.25
- bias_token: float32 [128], replicated, may hold values from -6 to 6
- hyper_query: float32 [128, 128], replicated, may hold values from -1 to 1
- hyper_key: float32 [128, 128], replicated, may hold values from -1 to 1
- hyper_value: float32 [128, 128], replicated, may hold values from -0.5 to 0.5
- hyper_out: float32 [128, 128], replicated, may hold values from -0.5 to 0.5
- hyper_up: float32 [128, 2048], replicated, may hold values from -0.5 to 0.5
- hyper_down: float32 [2048, 128], replicated, may hold values from -0.125 to 0.125
- hyper_gain1: float32 [128], replicated, may hold values from 0.1 to 1.9
- hyper_gain2: float32 [128], replicated, may hold values from 0.1 to 1.9
- w_qkv: bfloat16 [768, 2304], P(None, 'tok'), may hold values from -0.21875 to 0.21875
- w_out: bfloat16 [768, 768], P(None, 'tok'), may hold values from -1.75 to 1.75
- w_up: bfloat16 [768, 3072], P(None, 'tok'), may hold values from -0.21875 to 0.21875
- w_down: bfloat16 [3072, 768], P('tok'), may hold values from -0.109375 to 0.109375
- ln1_gain: float32 [768], replicated, may hold values from 0.5 to 1.5
- ln2_gain: float32 [768], replicated, may hold values from 0.5 to 1.5
Outputs:
- layer_out: bfloat16 [4, 8, 256, 768], P('tok', 'band')
- pixel_grad: bfloat16 [4, 8, 32, 256, 256], P('tok', None, 'band')
- grad_gen_w: float32 [196608, 128], P(('band', 'tok'))
- grad_gen_b: float32 [128, 768], replicated
- grad_bias_token: float32 [128], replicated
- grad_hyper_query: float32 [128, 128], replicated
- grad_hyper_key: float32 [128, 128], replicated
- grad_hyper_value: float32 [128, 128], replicated
- grad_hyper_out: float32 [128, 128], replicated
- grad_hyper_up: float32 [128, 2048], replicated
- grad_hyper_down: float32 [2048, 128], replicated
- grad_hyper_gain1: float32 [128], replicated
- grad_hyper_gain2: float32 [128], replicated
- grad_w_qkv: float32 [768, 2304], P(None, ('band', 'tok'))
- grad_w_out: float32 [768, 768], P(None, ('band', 'tok'))
- grad_w_up: float32 [768, 3072], P(None, ('band', 'tok'))
- grad_w_down: float32 [3072, 768], P(('band', 'tok'))
- grad_ln1_gain: float32 [768], P(('band', 'tok'))
- grad_ln2_gain: float32 [768], P(('band', 'tok'))
The draws below stay inside these ranges and needn't reach their ends.
Inputs may be any that keep to these rules, and one draw needn't show every extreme that they name: `patch_count`: each entry is 49, 196 or 256; every draw has an image with 49 and one with 256.
All inputs are finite; a program needn't handle non-finite values.
Results may differ from the reference program's by a relative error of at most 0.028.
Values may be sent and summed in bfloat16 or wider, within the bound.
A program may use at most 384 MiB of HBM per device.

```python
import math
import jax
import jax.numpy as jnp
from jax import lax

D = 768
HEADS = 12
HD = 64
FF = 3072
PIX = 256
WD = 128
HHEADS = 4
HFF = 2048
BANDS = 32
WAVES = 64
SLOT = 256
PATCH_FEW = 49
PATCH_MID = 196
IMG_GROUP = 8
GROUPS = 4
KW = 196608


def draw_patch_count(key, part):
    image_total = GROUPS * IMG_GROUP
    key_pick, key_large, key_small = jax.random.split(key, 3)
    selection = jax.random.randint(key_pick, (image_total,), 0, 3)
    large_spot = jax.random.randint(key_large, (), 0, image_total)
    small_spot = (large_spot + 1 + jax.random.randint(key_small, (), 0, image_total - 1)) % image_total
    positions = jnp.arange(image_total)
    selection = jnp.where(positions == large_spot, 2, selection)
    selection = jnp.where(positions == small_spot, 0, selection)
    counts = jnp.where(selection == 0, PATCH_FEW, jnp.where(selection == 1, PATCH_MID, SLOT))
    return counts.reshape(GROUPS, IMG_GROUP).astype(jnp.int32)


def plant(entries, rng, low, top_value):
    place = [jax.random.randint(jax.random.fold_in(rng, axis), (), 0, length) for axis, length in enumerate(entries.shape)]
    widest = entries.shape.index(max(entries.shape))
    neighbour = place[:widest] + [(place[widest] + 1) % entries.shape[widest]] + place[widest + 1:]
    return entries.at[tuple(place)].set(low).at[tuple(neighbour)].set(top_value)


def block_levels(key, shape, cuts, least, high):
    level, own = 1.0, jax.random.fold_in(key, 6)
    for position, shards_of in cuts:
        draws = jnp.exp(jax.random.uniform(jax.random.fold_in(own, position), (shards_of,), jnp.float32, least / len(cuts), high / len(cuts)))
        level = level * jnp.repeat(draws, shape[position] // shards_of).reshape([-1 if axis == position else 1 for axis in range(len(shape))])
    return level


def bell_draw(key, extent, scale, bound, pieces=(), kind=jnp.bfloat16):
    factor_of = block_levels(key, extent, pieces, -0.22, 0.18) if pieces else 1.0
    array = jax.random.normal(key, extent, jnp.float32) * scale * factor_of
    return jnp.minimum(jnp.maximum(array, -bound), bound).astype(kind)


def setup_inputs(seed: int = 0) -> dict:
    key_of = jax.random.split(jax.random.key(seed), 23)
    return {
        "pixels": bell_draw(key_of[0], (GROUPS, IMG_GROUP, BANDS, SLOT, PIX), 1.0, 6.0, ((0, 4), (2, 8))),
        "wave_table": jnp.clip(jnp.exp(jax.random.uniform(key_of[1], (WAVES,), jnp.float32, math.log(0.4), math.log(12.0))), 0.4, 12.0),
        "wave_index": plant(jax.random.randint(key_of[2], (GROUPS, IMG_GROUP, BANDS), 0, WAVES), jax.random.fold_in(key_of[2], 1), 0, WAVES - 1).astype(jnp.int32),
        "patch_count": draw_patch_count(jax.random.fold_in(key_of[22], 71), 0),
        "d_out": bell_draw(key_of[4], (GROUPS, IMG_GROUP, SLOT, D), 1.0, 6.0, ((0, 4), (1, 8))),
        "gen_w": bell_draw(key_of[5], (KW, WD), WD ** -0.5, 0.5, ((0, 32),)),
        "gen_b": bell_draw(key_of[6], (WD, D), (4 * WD) ** -0.5, 0.25, (), jnp.float32),
        "bias_token": bell_draw(key_of[7], (WD,), 1.0, 6.0, (), jnp.float32),
        "hyper_query": bell_draw(key_of[8], (WD, WD), (WD // 4) ** -0.5, 1.0, (), jnp.float32),
        "hyper_key": bell_draw(key_of[9], (WD, WD), (WD // 4) ** -0.5, 1.0, (), jnp.float32),
        "hyper_value": bell_draw(key_of[10], (WD, WD), WD ** -0.5, 0.5, (), jnp.float32),
        "hyper_out": bell_draw(key_of[11], (WD, WD), WD ** -0.5, 0.5, (), jnp.float32),
        "hyper_up": bell_draw(key_of[12], (WD, HFF), WD ** -0.5, 0.5, (), jnp.float32),
        "hyper_down": bell_draw(key_of[13], (HFF, WD), HFF ** -0.5, 0.125, (), jnp.float32),
        "hyper_gain1": jnp.clip(1.0 + 0.18 * jax.random.normal(key_of[14], (WD,), jnp.float32), 0.1, 1.9),
        "hyper_gain2": jnp.clip(1.0 + 0.18 * jax.random.normal(key_of[15], (WD,), jnp.float32), 0.1, 1.9),
        "w_qkv": bell_draw(key_of[16], (D, 3 * D), D ** -0.5, 0.21875, ((1, 4),)),
        "w_out": bell_draw(key_of[17], (D, D), (D // 64) ** -0.5, 1.75, ((1, 4),)),
        "w_up": bell_draw(key_of[18], (D, FF), D ** -0.5, 0.21875, ((1, 4),)),
        "w_down": bell_draw(key_of[19], (FF, D), FF ** -0.5, 0.109375, ((0, 4),)),
        "ln1_gain": jnp.clip(1.0 + 0.1 * jax.random.normal(key_of[20], (D,), jnp.float32), 0.5, 1.5),
        "ln2_gain": jnp.clip(1.0 + 0.1 * jax.random.normal(key_of[21], (D,), jnp.float32), 0.5, 1.5),
    }


EPS_BLOCK = 1e-06
EPS_HYPER = 1e-05
PRECISE = lax.Precision.HIGHEST

@jax.custom_vjp
def low(v):
    return lax.optimization_barrier(v.astype(jnp.bfloat16)).astype(jnp.float32)

@jax.custom_vjp
def low_back(v):
    return v

def low_keep(v):
    return (low(v), None)

def low_pass(kept, grad):
    return (grad,)

def back_keep(v):
    return (v, None)

def back_low(kept, grad):
    return (low(grad),)
low.defvjp(low_keep, low_pass)
low_back.defvjp(back_keep, back_low)

def layer_norm(values, scaling, epsilon):
    center = values - lax.optimization_barrier(jnp.mean(values, axis=-1, keepdims=True))
    spread = lax.optimization_barrier(jnp.mean(center * center, axis=-1, keepdims=True))
    return center * lax.rsqrt(spread + epsilon) * scaling

def wave_features(lengths, model_dim):
    middle = model_dim // 2
    angular = 1.0 / 10000.0 ** (jnp.arange(middle, dtype=jnp.float32) / middle)
    phases = (100.0 * lengths)[..., None] * angular
    return jnp.concatenate([jnp.sin(phases), jnp.cos(phases)], axis=-1)

def hyper_layer(features, params):
    bias_token, hyper_query, hyper_key, hyper_value, hyper_out, hyper_up, hyper_down, hyper_gain1, hyper_gain2 = params
    images = features.shape[0]
    model_dim = features.shape[-1]
    head_size = model_dim // HHEADS
    tokens = jnp.concatenate([features, jnp.broadcast_to(bias_token, (images, 1, model_dim))], axis=1)
    length = tokens.shape[1]
    queries = jnp.einsum('nsc,ce->nse', tokens, hyper_query, precision=PRECISE).reshape(images, length, HHEADS, head_size)
    keys_all = jnp.einsum('nsc,ce->nse', tokens, hyper_key, precision=PRECISE).reshape(images, length, HHEADS, head_size)
    values_all = jnp.einsum('nsc,ce->nse', tokens, hyper_value, precision=PRECISE).reshape(images, length, HHEADS, head_size)
    scores = jnp.einsum('nshe,nthe->nhst', queries, keys_all, precision=PRECISE) / math.sqrt(head_size)
    weights = jax.nn.softmax(scores, axis=-1)
    blended = jnp.einsum('nhst,nthe->nshe', weights, values_all, precision=PRECISE).reshape(images, length, model_dim)
    segment_one = layer_norm(tokens + jnp.einsum('nse,ef->nsf', blended, hyper_out, precision=PRECISE), hyper_gain1, EPS_HYPER)
    expanded = jax.nn.gelu(jnp.einsum('nse,ef->nsf', segment_one, hyper_up, precision=PRECISE), approximate=False)
    second = layer_norm(segment_one + jnp.einsum('nsf,fe->nse', expanded, hyper_down, precision=PRECISE), hyper_gain2, EPS_HYPER)
    return (second[:, :-1, :], second[:, -1, :])

def block_forward(pixel_part, length_part, count_part, params):
    gen_w, gen_b, hyper_params, w_qkv, w_out, w_up, w_down, ln1_gain, ln2_gain = params
    batch_images = pixel_part.shape[0]
    factor = 1.0 / math.sqrt(BANDS * PIX)
    band_feats, bias_feats = hyper_layer(wave_features(length_part, WD), hyper_params)
    band_low = low(band_feats)
    raw_kernel = jnp.einsum('ibc,kc->ibk', band_low, gen_w, precision=PRECISE)
    kernel = low(low_back(raw_kernel * factor)).reshape(batch_images, BANDS, PIX, D)
    convolved = jnp.einsum('ibsp,ibpd->isd', pixel_part, kernel, precision=PRECISE)
    bias_rows = jnp.dot(bias_feats, gen_b, precision=PRECISE)
    embedded = low_back(convolved) + bias_rows[:, None, :]
    usable = jnp.arange(SLOT)[None, :] < count_part[:, None]
    normed_one = low(layer_norm(embedded, ln1_gain, EPS_BLOCK))
    qkv_rows = jnp.einsum('isd,de->ise', normed_one, w_qkv, precision=PRECISE)
    queries = low(low_back(qkv_rows[:, :, :D])).reshape(batch_images, SLOT, HEADS, HD)
    keys_all = low(low_back(qkv_rows[:, :, D:2 * D])).reshape(batch_images, SLOT, HEADS, HD)
    values_all = low(low_back(qkv_rows[:, :, 2 * D:])).reshape(batch_images, SLOT, HEADS, HD)
    scores = low_back(jnp.einsum('iqhe,ikhe->ihqk', queries, keys_all, precision=PRECISE) / math.sqrt(HD))
    scores = jnp.where(usable[:, None, None, :], scores, -1e+30)
    attn_probs = low(jax.nn.softmax(scores, axis=-1))
    attended = low(low_back(jnp.einsum('ihqk,ikhe->iqhe', attn_probs, values_all, precision=PRECISE).reshape(batch_images, SLOT, D)))
    middle = embedded + low_back(jnp.einsum('isd,de->ise', attended, w_out, precision=PRECISE))
    normed_two = low(layer_norm(middle, ln2_gain, EPS_BLOCK))
    hidden = low_back(jnp.einsum('isd,df->isf', normed_two, w_up, precision=PRECISE))
    active = low(jax.nn.gelu(hidden, approximate=False))
    output = middle + low_back(jnp.einsum('isf,fd->isd', active, w_down, precision=PRECISE))
    return jnp.where(usable[:, :, None], output, 0.0)

def reference(pixels, wave_table, wave_index, patch_count, d_out, gen_w, gen_b, bias_token, hyper_query, hyper_key, hyper_value, hyper_out, hyper_up, hyper_down, hyper_gain1, hyper_gain2, w_qkv, w_out, w_up, w_down, ln1_gain, ln2_gain):
    blocks = GROUPS * IMG_GROUP // 4
    pixel_blocks = pixels.astype(jnp.float32).reshape(blocks, 4, BANDS, SLOT, PIX)
    length_blocks = wave_table[wave_index].reshape(blocks, 4, BANDS)
    count_blocks = patch_count.reshape(blocks, 4)
    cotangent = d_out.astype(jnp.float32).reshape(blocks, 4, SLOT, D)
    hyper_params = (bias_token, hyper_query, hyper_key, hyper_value, hyper_out, hyper_up, hyper_down, hyper_gain1, hyper_gain2)
    params = (gen_w.astype(jnp.float32), gen_b, hyper_params, w_qkv.astype(jnp.float32), w_out.astype(jnp.float32), w_up.astype(jnp.float32), w_down.astype(jnp.float32), ln1_gain, ln2_gain)

    def forward(pixel_all, weights):

        def one_block(inputs):
            return block_forward(inputs[0], inputs[1], inputs[2], weights)
        return lax.map(jax.checkpoint(one_block), (pixel_all, length_blocks, count_blocks))
    result, pullback = jax.vjp(forward, pixel_blocks, params)
    pixel_grad, gradients = pullback(cotangent)
    gen_grad, bias_gen_grad, hyper_grads, qkv_grad, out_grad, up_grad, down_grad, gain_one, gain_two = gradients
    return (result.reshape(GROUPS, IMG_GROUP, SLOT, D).astype(jnp.bfloat16), pixel_grad.reshape(GROUPS, IMG_GROUP, BANDS, SLOT, PIX).astype(jnp.bfloat16), gen_grad, bias_gen_grad, hyper_grads[0], hyper_grads[1], hyper_grads[2], hyper_grads[3], hyper_grads[4], hyper_grads[5], hyper_grads[6], hyper_grads[7], hyper_grads[8], qkv_grad, out_grad, up_grad, down_grad, gain_one, gain_two)
```

```python
import math

import jax
import jax.numpy as jnp
from jax import lax
from jax.sharding import PartitionSpec as P

HD = 64
HHEADS = 4


EPS_BLOCK = 1e-06
EPS_HYPER = 1e-05
PRECISE = lax.Precision.HIGHEST


def layer_norm(values, scaling, epsilon):
    center = values - jnp.mean(values, axis=-1, keepdims=True)
    spread = jnp.mean(center * center, axis=-1, keepdims=True)
    return center * lax.rsqrt(spread + epsilon) * scaling


def block_norm(values, scaling):
    return layer_norm(values, scaling, EPS_BLOCK)


def exact_gelu(values):
    return jax.nn.gelu(values, approximate=False)


def wave_features(lengths, model_dim):
    middle = model_dim // 2
    angular = 1.0 / 10000.0 ** (jnp.arange(middle, dtype=jnp.float32) / middle)
    phases = (100.0 * lengths)[..., None] * angular
    return jnp.concatenate([jnp.sin(phases), jnp.cos(phases)], axis=-1)


def hyper_layer(features, params):
    (
        bias_token,
        hyper_query,
        hyper_key,
        hyper_value,
        hyper_out,
        hyper_up,
        hyper_down,
        hyper_gain1,
        hyper_gain2,
    ) = params
    images = features.shape[0]
    model_dim = features.shape[-1]
    head_size = model_dim // HHEADS
    tokens = jnp.concatenate(
        [features, jnp.broadcast_to(bias_token, (images, 1, model_dim))], axis=1
    )
    length = tokens.shape[1]
    queries = jnp.einsum("nsc,ce->nse", tokens, hyper_query, precision=PRECISE).reshape(
        images, length, HHEADS, head_size
    )
    keys_all = jnp.einsum("nsc,ce->nse", tokens, hyper_key, precision=PRECISE).reshape(
        images, length, HHEADS, head_size
    )
    values_all = jnp.einsum("nsc,ce->nse", tokens, hyper_value, precision=PRECISE).reshape(
        images, length, HHEADS, head_size
    )
    scores = jnp.einsum("nshe,nthe->nhst", queries, keys_all, precision=PRECISE) / math.sqrt(
        head_size
    )
    weights = jax.nn.softmax(scores, axis=-1)
    blended = jnp.einsum("nhst,nthe->nshe", weights, values_all, precision=PRECISE).reshape(
        images, length, model_dim
    )
    segment_one = layer_norm(
        tokens + jnp.einsum("nse,ef->nsf", blended, hyper_out, precision=PRECISE),
        hyper_gain1,
        EPS_HYPER,
    )
    expanded = jax.nn.gelu(
        jnp.einsum("nse,ef->nsf", segment_one, hyper_up, precision=PRECISE), approximate=False
    )
    second = layer_norm(
        segment_one + jnp.einsum("nsf,fe->nse", expanded, hyper_down, precision=PRECISE),
        hyper_gain2,
        EPS_HYPER,
    )
    return (second[:, :-1, :], second[:, -1, :])


def contract_rows(left_side, right_side):
    return lax.dot_general(
        left_side, right_side, (((0,), (0,)), ((), ())), preferred_element_type=jnp.float32
    )


def contract_cols(left_side, right_side):
    return lax.dot_general(
        left_side, right_side, (((1,), (1,)), ((), ())), preferred_element_type=jnp.float32
    )


def attention_scores(queries, keys_low, usable):
    head_size = queries.shape[-1]
    scores = jnp.einsum(
        "iqhe,ikhe->ihqk", queries, keys_low, preferred_element_type=jnp.float32
    ) / math.sqrt(head_size)
    return jnp.where(usable[:, None, None, :], scores, -1e30)


def block_forward(embedded, usable, weights_full, ln1_gain, ln2_gain):
    w_qkv_full, w_out_full, w_up_full, w_down_full = weights_full
    images, slot_count, model_dim = embedded.shape
    row_count = images * slot_count
    head_count = model_dim // HD
    flat_rows = embedded.reshape(row_count, model_dim)
    normed_one = block_norm(flat_rows, ln1_gain).astype(jnp.bfloat16)
    qkv_low = jnp.dot(normed_one, w_qkv_full, preferred_element_type=jnp.float32).astype(
        jnp.bfloat16
    )
    sections = qkv_low.reshape(images, slot_count, 3, head_count, HD)
    queries = sections[:, :, 0]
    keys_low = sections[:, :, 1]
    values_low = sections[:, :, 2]
    scores = attention_scores(queries, keys_low, usable)
    highest = jnp.max(scores, axis=-1, keepdims=True)
    lifted = jnp.exp(scores - highest)
    totals = jnp.sum(lifted, axis=-1, keepdims=True)
    attn_probs = (lifted / totals).astype(jnp.bfloat16)
    log_mass = highest + jnp.log(totals)
    attended = (
        jnp.einsum("ihqk,ikhe->iqhe", attn_probs, values_low, preferred_element_type=jnp.float32)
        .astype(jnp.bfloat16)
        .reshape(row_count, model_dim)
    )
    middle = flat_rows + jnp.dot(attended, w_out_full, preferred_element_type=jnp.float32)
    normed_two = block_norm(middle, ln2_gain).astype(jnp.bfloat16)
    hidden = jnp.dot(normed_two, w_up_full, preferred_element_type=jnp.float32)
    active = exact_gelu(hidden).astype(jnp.bfloat16)
    output = middle + jnp.dot(active, w_down_full, preferred_element_type=jnp.float32)
    return (
        flat_rows,
        normed_one,
        queries,
        keys_low,
        values_low,
        log_mass,
        attended,
        middle,
        normed_two,
        hidden,
        active,
        output,
    )


def block_backward(stored, usable, grad_rows, weights_full, ln1_gain, ln2_gain):
    (
        flat_rows,
        normed_one,
        queries,
        keys_low,
        values_low,
        log_mass,
        attended,
        middle,
        normed_two,
        hidden,
        active,
        output,
    ) = stored
    w_qkv_full, w_out_full, w_up_full, w_down_full = weights_full
    images, slot_count, head_count, head_size = queries.shape
    row_count, model_dim = flat_rows.shape
    grad_low = grad_rows.astype(jnp.bfloat16)
    grad_down = contract_rows(active, grad_low)
    d_active = contract_cols(grad_low, w_down_full)
    gelu_back = jax.vjp(exact_gelu, hidden)[1]
    d_hidden = gelu_back(d_active)[0].astype(jnp.bfloat16)
    grad_up_turned = contract_rows(d_hidden, normed_two)
    d_normed_two = contract_cols(d_hidden, w_up_full)
    norm_back_two = jax.vjp(block_norm, middle, ln2_gain)[1]
    d_middle_norm, grad_gain_two = norm_back_two(d_normed_two)
    d_middle = grad_rows + d_middle_norm
    d_middle_low = d_middle.astype(jnp.bfloat16)
    grad_out_turned = contract_rows(d_middle_low, attended)
    d_attended = (
        contract_cols(d_middle_low, w_out_full)
        .astype(jnp.bfloat16)
        .reshape(images, slot_count, head_count, head_size)
    )
    scores = attention_scores(queries, keys_low, usable)
    attn_float = jnp.exp(scores - log_mass)
    attn_probs = attn_float.astype(jnp.bfloat16)
    d_values = jnp.einsum(
        "ihqk,iqhe->ikhe", attn_probs, d_attended, preferred_element_type=jnp.float32
    ).astype(jnp.bfloat16)
    d_probs = jnp.einsum(
        "iqhe,ikhe->ihqk", d_attended, values_low, preferred_element_type=jnp.float32
    )
    d_scores = (
        attn_float * (d_probs - jnp.sum(attn_float * d_probs, axis=-1, keepdims=True))
    ).astype(jnp.bfloat16)
    d_queries = (
        jnp.einsum("ihqk,ikhe->iqhe", d_scores, keys_low, preferred_element_type=jnp.float32)
        / math.sqrt(head_size)
    ).astype(jnp.bfloat16)
    d_keys = (
        jnp.einsum("ihqk,iqhe->ikhe", d_scores, queries, preferred_element_type=jnp.float32)
        / math.sqrt(head_size)
    ).astype(jnp.bfloat16)
    d_qkv = jnp.stack([d_queries, d_keys, d_values], axis=2).reshape(row_count, 3 * model_dim)
    grad_qkv_turned = contract_rows(d_qkv, normed_one)
    d_normed_one = contract_cols(d_qkv, w_qkv_full)
    norm_back_one = jax.vjp(block_norm, flat_rows, ln1_gain)[1]
    d_flat, grad_gain_one = norm_back_one(d_normed_one)
    return (
        d_middle + d_flat,
        (grad_qkv_turned, grad_out_turned, grad_up_turned, grad_down, grad_gain_one, grad_gain_two),
    )


def body(
    pixels,
    wave_table,
    wave_index,
    patch_count,
    d_out,
    gen_w,
    gen_b,
    bias_token,
    hyper_query,
    hyper_key,
    hyper_value,
    hyper_out,
    hyper_up,
    hyper_down,
    hyper_gain1,
    hyper_gain2,
    w_qkv,
    w_out,
    w_up,
    w_down,
    ln1_gain,
    ln2_gain,
):
    group_images, band_share, slot_count, pixel_count = pixels.shape[1:]
    own_images = patch_count.shape[1]
    model_dim = w_out.shape[0]
    hyper_dim = gen_w.shape[1]
    all_bands = wave_index.shape[2]
    owners = lax.axis_size("band")
    slice_pixels = pixel_count // owners
    factor = 1.0 / math.sqrt(all_bands * pixel_count)
    band_place = lax.axis_index("band")
    hyper_params = (
        bias_token,
        hyper_query,
        hyper_key,
        hyper_value,
        hyper_out,
        hyper_up,
        hyper_down,
        hyper_gain1,
        hyper_gain2,
    )
    pixel_turned = pixels[0].reshape(
        group_images, band_share, slot_count, owners, slice_pixels
    ).transpose(3, 0, 4, 1, 2)
    pixel_slices = lax.all_to_all(pixel_turned, "band", 0, 0, tiled=True)
    pixel_slices = pixel_slices.transpose(1, 2, 0, 3, 4).reshape(
        group_images, slice_pixels * all_bands, slot_count
    )
    gen_part = lax.all_gather(gen_w, "tok", axis=0, tiled=True)
    gen_grid = gen_part.reshape(slice_pixels, model_dim, hyper_dim)
    weights_full = (
        lax.all_gather(w_qkv, "tok", axis=1, tiled=True),
        lax.all_gather(w_out, "tok", axis=1, tiled=True),
        lax.all_gather(w_up, "tok", axis=1, tiled=True),
        lax.all_gather(w_down, "tok", axis=0, tiled=True),
    )
    catalog = lax.broadcasted_iota(jnp.int32, (1, 1, wave_table.shape[0]), 2)
    picked = (wave_index[0][:, :, None] == catalog).astype(jnp.float32)
    lengths_all = jnp.sum(picked * wave_table, axis=-1)
    hyper_input = wave_features(lengths_all, hyper_dim)
    band_feats = hyper_layer(hyper_input, hyper_params)[0]
    band_low = band_feats.astype(jnp.bfloat16).reshape(-1, hyper_dim)
    own_input = lax.dynamic_slice_in_dim(hyper_input, band_place * own_images, own_images, 0)

    def run_hyper(params):
        return hyper_layer(own_input, params)

    (_, bias_own), hyper_back = jax.vjp(run_hyper, hyper_params)
    kernels = (
        jnp.einsum("pdc,nc->pnd", gen_grid, band_low, preferred_element_type=jnp.float32) * factor
    ).astype(jnp.bfloat16)
    kernel_grid = kernels.reshape(slice_pixels, group_images, all_bands, model_dim)
    kernel_rows = kernel_grid.transpose(1, 0, 2, 3).reshape(
        group_images, slice_pixels * all_bands, model_dim
    )
    product = jnp.einsum(
        "iks,ikd->isd", pixel_slices, kernel_rows, preferred_element_type=jnp.float32
    )
    convolved = lax.psum_scatter(
        product.reshape(group_images * slot_count, model_dim).astype(jnp.bfloat16),
        "band",
        scatter_dimension=0,
        tiled=True,
    ).astype(jnp.float32)
    bias_rows = jnp.dot(bias_own, gen_b, precision=PRECISE)
    embedded = convolved.reshape(own_images, slot_count, model_dim) + bias_rows[:, None, :]
    usable = lax.broadcasted_iota(jnp.int32, (own_images, slot_count), 1) < patch_count[0][:, None]
    stored = block_forward(embedded, usable, weights_full, ln1_gain, ln2_gain)
    row_mask = usable.reshape(-1, 1)
    layer_out = (
        jnp.where(row_mask, stored[-1], 0.0)
        .astype(jnp.bfloat16)
        .reshape(1, own_images, slot_count, model_dim)
    )
    grad_rows = jnp.where(row_mask, d_out[0].reshape(-1, model_dim).astype(jnp.float32), 0.0)
    d_embed, block_terms = block_backward(
        stored, usable, grad_rows, weights_full, ln1_gain, ln2_gain
    )
    d_embed_low = d_embed.astype(jnp.bfloat16).reshape(own_images, slot_count, model_dim)
    d_bias = jnp.sum(d_embed.reshape(own_images, slot_count, model_dim), axis=1)
    d_bias_feat = jnp.dot(d_bias, gen_b.T, precision=PRECISE)
    grad_gen_b = jnp.dot(bias_own.T, d_bias, precision=PRECISE)
    d_gathered = lax.all_gather(d_embed_low, "band", axis=0, tiled=True)
    grad_slices = jnp.einsum(
        "ikd,isd->iks", kernel_rows, d_gathered, preferred_element_type=jnp.float32
    ).astype(jnp.bfloat16)
    grad_slices = grad_slices.reshape(
        group_images, slice_pixels, owners, band_share, slot_count
    ).transpose(2, 0, 1, 3, 4)
    grad_slices = lax.all_to_all(grad_slices, "band", 0, 0, tiled=True)
    pixel_grad = grad_slices.transpose(1, 3, 4, 0, 2).reshape(pixels.shape)
    d_kernel = jnp.einsum(
        "iks,isd->ikd", pixel_slices, d_gathered, preferred_element_type=jnp.float32
    ).astype(jnp.bfloat16)
    d_kernel = (
        d_kernel.reshape(group_images, slice_pixels, all_bands, model_dim)
        .transpose(1, 0, 2, 3)
        .reshape(slice_pixels, group_images * all_bands, model_dim)
    )
    d_band_part = (
        jnp.einsum("pnd,pdc->nc", d_kernel, gen_grid, preferred_element_type=jnp.float32) * factor
    )
    d_band_own = lax.psum_scatter(d_band_part, "band", scatter_dimension=0, tiled=True)
    gen_part_grad = (
        jnp.einsum("pnd,nc->pdc", d_kernel, band_low, preferred_element_type=jnp.float32) * factor
    )
    grad_gen_w = lax.psum_scatter(
        gen_part_grad.reshape(-1, hyper_dim).astype(jnp.bfloat16),
        "tok",
        scatter_dimension=0,
        tiled=True,
    ).astype(jnp.float32)
    (
        grad_token,
        grad_query,
        grad_key,
        grad_value,
        grad_mix,
        grad_expand,
        grad_shrink,
        grad_first_gain,
        grad_second_gain,
    ) = hyper_back((d_band_own.reshape(own_images, all_bands, hyper_dim), d_bias_feat))[0]
    qkv_turned, out_turned, up_turned, grad_down, gain_one, gain_two = block_terms

    def spread(term):
        return lax.psum_scatter(
            term.astype(jnp.bfloat16), ("band", "tok"), scatter_dimension=0, tiled=True
        ).astype(jnp.float32)

    block_sums = (
        spread(qkv_turned),
        spread(out_turned),
        spread(up_turned),
        spread(grad_down),
        lax.psum_scatter(gain_one, ("band", "tok"), scatter_dimension=0, tiled=True),
        lax.psum_scatter(gain_two, ("band", "tok"), scatter_dimension=0, tiled=True),
    )
    hyper_sums = lax.psum(
        (
            grad_token,
            grad_query,
            grad_key,
            grad_value,
            grad_mix,
            grad_expand,
            grad_shrink,
            grad_first_gain,
            grad_second_gain,
            grad_gen_b,
        ),
        ("band", "tok"),
    )
    return (
        layer_out,
        pixel_grad,
        grad_gen_w,
        hyper_sums[9],
        hyper_sums[0],
        hyper_sums[1],
        hyper_sums[2],
        hyper_sums[3],
        hyper_sums[4],
        hyper_sums[5],
        hyper_sums[6],
        hyper_sums[7],
        hyper_sums[8],
        block_sums[0].T,
        block_sums[1].T,
        block_sums[2].T,
        block_sums[3],
        block_sums[4],
        block_sums[5],
    )


def solution(mesh):
    placed = (
        P("tok", None, "band", None, None),
        P(),
        P("tok", None, None),
        P("tok", "band"),
        P("tok", "band", None, None),
        P(("band", "tok"), None),
        P(),
        P(),
        P(),
        P(),
        P(),
        P(),
        P(),
        P(),
        P(),
        P(),
        P(None, "tok"),
        P(None, "tok"),
        P(None, "tok"),
        P("tok", None),
        P(),
        P(),
    )
    return jax.shard_map(
        body,
        mesh=mesh,
        in_specs=placed,
        out_specs=(
            P("tok", "band", None, None),
            P("tok", None, "band", None, None),
            P(("band", "tok"), None),
            P(),
            P(),
            P(),
            P(),
            P(),
            P(),
            P(),
            P(),
            P(),
            P(),
            P(None, ("band", "tok")),
            P(None, ("band", "tok")),
            P(None, ("band", "tok")),
            P(("band", "tok"), None),
            P(("band", "tok")),
            P(("band", "tok")),
        ),
        check_vma=False,
    )
```

```python
import functools
import math

import jax
import jax.numpy as jnp
from jax import lax
from jax.experimental import pallas as pl
from jax.experimental.pallas import tpu as pltpu
from jax.sharding import PartitionSpec as P

HD = 64
HHEADS = 4


EPS_BLOCK = 1e-06
EPS_HYPER = 1e-05
PRECISE = lax.Precision.HIGHEST


MESH = pl.DeviceIdType.MESH


def mesh_bits():
    tok_bits = (lax.axis_size("tok") - 1).bit_length()
    band_bits = (lax.axis_size("band") - 1).bit_length()
    dims = [("band", b) for b in reversed(range(band_bits))]
    dims += [("tok", b) for b in reversed(range(tok_bits))]
    return dims, band_bits, tok_bits


def own_bit(axis, bit):
    return lax.rem(lax.div(lax.axis_index(axis), 1 << bit), 2)


def partner_of(axis, bit):
    place = lax.axis_index(axis)
    mine = own_bit(axis, bit)
    other = place + (1 - 2 * mine) * (1 << bit)
    band, tok = lax.axis_index("band"), lax.axis_index("tok")
    return (other, tok) if axis == "band" else (band, other)


def halving_order(which, band_bits, tok_bits):
    tok = [("tok", b) for b in range(tok_bits)]
    band = [("band", b) for b in range(band_bits)]
    if which == 2:
        return tok
    if which == 0:
        return tok + band
    return tok[:1] + band[:1] + tok[1:] + band[1:]


def pick(remaining, axis_bit, value):
    place = remaining.index(axis_bit)
    return tuple([slice(None)] * place + [value])


def add_block(dest, left, right):
    lead = dest.shape[:-2]

    def one(index):
        spot = []
        for size in reversed(lead):
            spot.insert(0, lax.rem(index, size))
            index = lax.div(index, size)
        spot = tuple(spot)
        dest[spot] = (left(spot) + right(spot)).astype(dest.dtype)

    pl.loop(0, math.prod(lead))(one)


def wide_blocks(shapes, piece):
    blocks, start = [], 0
    for index, (rows, columns) in enumerate(shapes):
        for part in range(columns // 128):
            row = 0
            while row < rows:
                inside = start % piece
                size = min(rows - row, piece - inside)
                blocks.append((index, row, part, start // piece, inside, size))
                row += size
                start += size
    return blocks, start


def segment_spot(segment, count):
    return tuple((segment >> (count - 1 - bit)) & 1 for bit in range(count))


class Sums:
    def __init__(
        self, streams, sources, outputs, own, landing, send_sem, recv_sem, own_sem, buffer=None
    ):
        self.buffer = buffer
        self.streams, self.sources, self.outputs = streams, sources, outputs
        self.own, self.landing = own, landing
        self.send_sem, self.recv_sem, self.own_sem = send_sem, recv_sem, own_sem
        self.flying, self.local = {}, {}

    def part(self, stream, value):
        entry = self.streams[stream]
        spot = pick(entry["span"], entry["order"][0], value)
        spot = spot + (slice(None),) * (len(entry["span"]) - len(spot))
        rows = pl.ds(entry["start"], entry["rows"])
        return self.sources[entry["source"]].at[spot + (rows,)]

    def fetch(self, stream):
        entry = self.streams[stream]
        if entry["fetch"]:
            slot = stream % len(self.own)
            whole = (slice(None),) * (len(entry["span"]) - 1)
            target = self.own[slot].at[whole + (pl.ds(0, entry["rows"]),)]
            copy = pltpu.make_async_copy(
                self.part(stream, own_bit(*entry["order"][0])), target, self.own_sem.at[slot]
            )
            copy.start()
            self.local[stream] = (copy, target)

    def send(self, stream, stage, source):
        axis, bit = self.streams[stream]["order"][stage]
        copy = pltpu.make_async_remote_copy(
            src_ref=source,
            dst_ref=self.landing[stream][stage],
            send_sem=self.send_sem.at[stream, stage],
            recv_sem=self.recv_sem.at[stream, stage],
            device_id=partner_of(axis, bit),
            device_id_type=MESH,
        )
        copy.start()
        self.flying[stream, stage] = copy

    def begin(self, stream):
        first = self.streams[stream]["order"][0]
        self.send(stream, 0, self.part(stream, 1 - own_bit(*first)))

    def advance(self, stream, stage):
        entry = self.streams[stream]
        order, span = entry["order"], entry["span"]
        if stage >= len(order):
            return
        remaining = [d for d in span if d not in order[:stage]]
        axis_bit = order[stage]
        after = [d for d in remaining if d != axis_bit]
        self.flying[stream, stage].wait_recv()
        land = self.landing[stream][stage]
        if stage > 0:
            held = self.landing[stream][stage - 1].at[
                pick(remaining, axis_bit, own_bit(*axis_bit))
            ]
        elif stream in self.local:
            self.local[stream][0].wait()
            held = self.local[stream][1]
        else:
            held = self.part(stream, own_bit(*axis_bit))
        if stage == len(order) - 1 and entry["out"] is not None:
            total = land[...].astype(jnp.float32) + held[...].astype(jnp.float32)
            rows = pl.ds(entry["start"], entry["rows"])
            if entry["fetch"]:
                self.outputs[entry["out"]][rows] = total * entry["scale"]
            else:
                buffer, sem = self.buffer
                buffer[...] = total * entry["scale"]
                copy = pltpu.make_async_copy(buffer, self.outputs[entry["out"]].at[rows], sem)
                copy.start()
                copy.wait()
        else:
            add_block(
                land,
                lambda spot: land[spot].astype(jnp.float32),
                lambda spot: held[spot].astype(jnp.float32),
            )
            if stage < len(order) - 1:
                following = order[stage + 1]
                self.send(
                    stream, stage + 1, land.at[pick(after, following, 1 - own_bit(*following))]
                )

    def drain(self):
        for copy in self.flying.values():
            copy.wait_send()


class Spread:
    def __init__(self, dims, order, whole, send_sem, recv_sem):
        self.dims, self.order, self.whole = dims, list(reversed(order)), whole
        self.send_sem, self.recv_sem = send_sem, recv_sem
        self.spot = [own_bit(*d) if d in order else slice(None) for d in dims]
        self.copies = []

    def start(self):
        step = len(self.copies)
        view = self.whole.at[tuple(self.spot)]
        copy = pltpu.make_async_remote_copy(
            src_ref=view,
            dst_ref=view,
            send_sem=self.send_sem.at[step],
            recv_sem=self.recv_sem.at[step],
            device_id=partner_of(*self.order[step]),
            device_id_type=MESH,
        )
        copy.start()
        self.copies.append(copy)

    def finish(self):
        self.copies[-1].wait()
        self.spot[self.dims.index(self.order[len(self.copies) - 1])] = slice(None)


def pack_blocks(blocks, used, packed, wide, stages):
    for index, row, part, segment, inside, size in blocks:
        packed[segment_spot(segment, stages) + (pl.ds(inside, size),)] = wide[index](
            pl.ds(row, size), pl.ds(part * 128, 128)
        ).astype(packed.dtype)
    piece = packed.shape[-2]
    while used < piece << stages:
        size = piece - used % piece
        packed[segment_spot(used // piece, stages) + (pl.ds(used % piece, size),)] = jnp.zeros(
            (size, 128), packed.dtype
        )
        used += size


def unpack_blocks(blocks, whole, wide_out, stages):
    for index, row, part, segment, inside, size in blocks:
        wide_out[index][pl.ds(row, size), pl.ds(part * 128, 128)] = whole[
            segment_spot(segment, stages) + (pl.ds(inside, size),)
        ].astype(jnp.float32)


def reduce_kernel(plan, blocks, used, *refs):
    streams, dims = plan["streams"], plan["dims"]
    count, stages = len(streams), len(dims)
    pos = plan["bulk"]
    inputs = list(refs[:pos])
    wide = refs[pos : pos + plan["wide"]]
    pos += plan["wide"]
    outputs = refs[pos : pos + plan["bulk"]]
    pos += plan["bulk"]
    wide_out = refs[pos : pos + plan["wide"]]
    pos += plan["wide"]
    own = refs[pos : pos + count - 1]
    pos += count - 1
    landing = []
    for stream in streams:
        landing.append(refs[pos : pos + len(stream["order"])])
        pos += len(stream["order"])
    packed, whole, send_sem, recv_sem, own_sem, gather_send, gather_recv = refs[pos:]
    barrier = pltpu.get_barrier_semaphore()
    for axis, bit in dims:
        pl.semaphore_signal(barrier, inc=1, device_id=partner_of(axis, bit), device_id_type=MESH)
    pl.semaphore_wait(barrier, stages)
    sums = Sums(
        streams, inputs + [packed], outputs, own, landing, send_sem, recv_sem, own_sem
    )
    for stream in range(count - 1):
        sums.begin(stream)
        sums.fetch(stream)
    pack_blocks(
        blocks, used, packed, [lambda r, c, ref=ref: ref[r, c] for ref in wide], stages
    )
    sums.begin(count - 1)
    for stage in range(stages):
        for stream in range(count):
            sums.advance(stream, stage)
    spread = Spread(dims, streams[-1]["order"], whole, gather_send, gather_recv)
    whole[tuple(spread.spot)] = landing[count - 1][stages - 1][...]
    for _ in range(stages):
        spread.start()
        spread.finish()
    unpack_blocks(blocks, whole, wide_out, stages)
    sums.drain()


def stream_entry(source, out, start, rows, order, dims, fetch, scale=1.0):
    return {
        "source": source,
        "out": out,
        "start": start,
        "rows": rows,
        "order": order,
        "span": [d for d in dims if d in order],
        "fetch": fetch,
        "scale": scale,
    }


def landing_shapes(entry, lanes):
    stages = len(entry["order"])
    return [
        pltpu.VMEM((2,) * (stages - 1 - stage) + (entry["rows"], lanes), jnp.bfloat16)
        for stage in range(stages)
    ]


def wide_plan(shapes, devices):
    used = sum(math.prod(shape) for shape in shapes) // 128
    piece = -(-used // (16 * devices)) * 16
    return wide_blocks(shapes, piece)[0], used, piece


def row_chunks(rows, chunks):
    size = -(-rows // chunks // 8) * 8
    return [(start, min(size, rows - start)) for start in range(0, rows, size)]


def reduce_all(arrays, whiches, chunks, wide, collective_id):
    dims, band_bits, tok_bits = mesh_bits()
    low, everything = jnp.bfloat16, len(dims)
    split, outs, own, landing, streams = [], [], [], [], []
    for k, array in enumerate(arrays):
        order = halving_order(whiches[k], band_bits, tok_bits)
        stages = len(order)
        rows, lanes = array.shape[0] >> stages, array.shape[1]
        split.append(array.reshape((2,) * stages + (rows, lanes)))
        outs.append(jax.ShapeDtypeStruct((rows, lanes), jnp.float32))
        for start, size in row_chunks(rows, chunks[k]):
            streams.append(stream_entry(k, k, start, size, order, dims, True))
            own.append(pltpu.VMEM((2,) * (stages - 1) + (size, lanes), low))
            landing += landing_shapes(streams[-1], lanes)
    blocks, used, piece = wide_plan([part.shape for part in wide], 1 << everything)
    order = halving_order(0, band_bits, tok_bits)
    streams.append(stream_entry(len(arrays), None, 0, piece, order, dims, False))
    landing += landing_shapes(streams[-1], 128)
    outs += [jax.ShapeDtypeStruct(part.shape, jnp.float32) for part in wide]
    count = len(streams)
    plan = {"streams": streams, "dims": dims, "bulk": len(arrays), "wide": len(wide)}
    sent = sum(a.size for a in arrays)
    space = (2,) * everything + (piece, 128)
    return pl.pallas_call(
        functools.partial(reduce_kernel, plan, blocks, used),
        out_shape=outs,
        in_specs=[pl.BlockSpec(memory_space=pl.ANY)] * len(arrays)
        + [pl.BlockSpec(memory_space=pltpu.VMEM)] * len(wide),
        out_specs=[pl.BlockSpec(memory_space=pltpu.VMEM)] * len(outs),
        scratch_shapes=own
        + landing
        + [
            pltpu.VMEM(space, low),
            pltpu.VMEM(space, low),
            pltpu.SemaphoreType.DMA((count, everything)),
            pltpu.SemaphoreType.DMA((count, everything)),
            pltpu.SemaphoreType.DMA((count,)),
            pltpu.SemaphoreType.DMA((everything,)),
            pltpu.SemaphoreType.DMA((everything,)),
        ],
        compiler_params=pltpu.CompilerParams(
            collective_id=collective_id, has_side_effects=True, vmem_limit_bytes=60 << 20
        ),
        cost_estimate=pl.CostEstimate(flops=2 * sent, bytes_accessed=40 * sent, transcendentals=0),
    )(*split, *wide)


def turn_kernel(in_ref, out_ref, lines):
    bands = in_ref.shape[1]
    halves, rows = lines.shape[:2]
    for band in range(bands):
        turned = in_ref[0, band].astype(jnp.float32).T
        for half in range(halves):
            lines[half, pl.ds(band, rows // bands, stride=bands), :] = turned[
                :, half * 128 : (half + 1) * 128
            ]
    for half in range(halves):
        out_ref[:, 0, :, pl.ds(half * 128, 128)] = (
            lines[half].astype(out_ref.dtype).reshape(*out_ref.shape[:1], -1, 128)
        )


def turn_pixels(pixels, owners):
    images, bands, slot, pixel_count = pixels.shape
    share = pixel_count // owners * bands
    return pl.pallas_call(
        turn_kernel,
        grid=(images,),
        out_shape=jax.ShapeDtypeStruct((owners, images, share, slot), pixels.dtype),
        in_specs=[pl.BlockSpec((1, bands, slot, pixel_count), lambda i: (i, 0, 0, 0))],
        out_specs=pl.BlockSpec((owners, 1, share, slot), lambda i: (0, i, 0, 0)),
        scratch_shapes=[pltpu.VMEM((slot // 128, pixel_count * bands, 128), jnp.float32)],
        compiler_params=pltpu.CompilerParams(vmem_limit_bytes=20 << 20),
    )(pixels)


def unturn_kernel(in_ref, out_ref, lines):
    bands = out_ref.shape[1]
    halves, rows = lines.shape[:2]
    for half in range(halves):
        lines[half] = (
            in_ref[:, 0, :, pl.ds(half * 128, 128)].astype(jnp.float32).reshape(rows, 128)
        )
    for band in range(bands):
        for half in range(halves):
            piece = lines[half, pl.ds(band, rows // bands, stride=bands), :]
            out_ref[0, band, pl.ds(half * 128, 128), :] = piece.T.astype(out_ref.dtype)


def unturn_pixels(blocks, shape):
    owners, images, share, slot = blocks.shape
    bands, pixel_count = shape[1], shape[3]
    return pl.pallas_call(
        unturn_kernel,
        grid=(images,),
        out_shape=jax.ShapeDtypeStruct(shape, blocks.dtype),
        in_specs=[pl.BlockSpec((owners, 1, share, slot), lambda i: (0, i, 0, 0))],
        out_specs=pl.BlockSpec((1, bands, slot, pixel_count), lambda i: (i, 0, 0, 0)),
        scratch_shapes=[pltpu.VMEM((slot // 128, pixel_count * bands, 128), jnp.float32)],
        compiler_params=pltpu.CompilerParams(vmem_limit_bytes=20 << 20),
    )(blocks)


def at_band(place):
    return (place, lax.axis_index("tok"))


def pair_place():
    band = lax.axis_index("band")
    return lax.div(band, 2), lax.rem(band, 2)


def first_half(shape):
    return lax.rem(lax.broadcasted_iota(jnp.int32, shape, len(shape) - 2), 8) < 4


def make_kernels(gen_ref, even_ref, odd_ref, kern_ref, factor):
    pixel_share, model_dim = gen_ref.shape[:2]
    pairs, _, owners, _, _ = kern_ref.shape
    width = 256

    @pl.loop(0, pixel_share // 4)
    def _(quad):
        @pl.loop(0, model_dim // width)
        def _(part):
            columns = pl.ds(pl.multiple_of(part * width, width), width)
            pieces = []
            for offset in range(4):
                rows = (even_ref, odd_ref)[offset % 2][...]
                piece = lax.dot_general(
                    rows,
                    gen_ref[quad * 4 + offset, columns, :],
                    (((1,), (1,)), ((), ())),
                    preferred_element_type=jnp.float32,
                )
                pieces.append((piece * factor).reshape(pairs * owners, 8, width))
            top = first_half(pieces[0].shape)
            even, odd = [], []
            for a, b in ((pieces[0], pieces[1]), (pieces[2], pieces[3])):
                even.append(jnp.where(top, a, b))
                odd.append(pltpu.roll(jnp.where(top, b, a), 4, 1))
            rows = pl.ds(pl.multiple_of(quad * 16, 16), 16)
            for parity, both in ((0, even), (1, odd)):
                block = jnp.concatenate(both, axis=1).astype(jnp.bfloat16)
                kern_ref[:, parity, :, rows, columns] = block.reshape(pairs, owners, 16, width)


def embed_kernel(
    factor,
    gen_hbm,
    pix_hbm,
    even_ref,
    odd_ref,
    out_ref,
    gen_ref,
    pix_ref,
    kern_ref,
    y_out,
    y_in,
    z_out,
    z_in,
    kept,
    load_sem,
    y_send,
    y_recv,
    z_send,
    z_recv,
):
    pairs = kern_ref.shape[0]
    depth, side = pairs, lax.rem(lax.axis_index("band"), 2)
    place = lax.div(lax.axis_index("band"), 2)
    loads = [
        pltpu.make_async_copy(gen_hbm, gen_ref, load_sem.at[0]),
        pltpu.make_async_copy(pix_hbm, pix_ref, load_sem.at[1]),
    ]
    for load in loads:
        load.start()
    barrier = pltpu.get_barrier_semaphore()
    pl.semaphore_signal(
        barrier, inc=1, device_id=at_band(place * 2 + 1 - side), device_id_type=MESH
    )
    for step in range(depth - 1):
        target = lax.rem(place + 1 + step, depth)
        pl.semaphore_signal(
            barrier, inc=1, device_id=at_band(target * 2 + side), device_id_type=MESH
        )
    loads[0].wait()
    make_kernels(gen_ref, even_ref, odd_ref, kern_ref, factor)
    loads[1].wait()
    pl.semaphore_wait(barrier, depth)
    width = 256

    def conv(pair, parity, store):
        slot, inner = kern_ref.shape[3], pix_ref.shape[3]
        owners = kern_ref.shape[2]
        left = pix_ref[:, pair * 2 + parity].reshape(owners * slot, inner).T

        @pl.loop(0, kern_ref.shape[4] // width)
        def _(part):
            columns = pl.ds(pl.multiple_of(part * width, width), width)
            right = kern_ref[pair, parity, :, :, columns].reshape(owners * slot, width)
            store(
                columns,
                jnp.dot(left, right, preferred_element_type=jnp.float32),
            )

    def y_copy(step):
        return pltpu.make_async_remote_copy(
            src_ref=y_out.at[step],
            dst_ref=y_in.at[step],
            send_sem=y_send.at[step],
            recv_sem=y_recv.at[step],
            device_id=at_band(place * 2 + 1 - side),
            device_id_type=MESH,
        )

    def z_copy(step):
        return pltpu.make_async_remote_copy(
            src_ref=z_out.at[step],
            dst_ref=z_in.at[step],
            send_sem=z_send.at[step],
            recv_sem=z_recv.at[step],
            device_id=at_band(lax.rem(place + 1 + step, depth) * 2 + side),
            device_id_type=MESH,
        )

    @pl.loop(0, depth)
    def _(step):
        def store(columns, value):
            y_out[step, :, columns] = value.astype(y_out.dtype)

        conv(lax.rem(place + 1 + step, depth), 1 - side, store)
        y_copy(step).start()

    @pl.loop(0, depth)
    def _(step):
        def store(columns, value):
            kept[:, columns] = value

        conv(lax.rem(place + 1 + step, depth), side, store)
        y_copy(step).wait_recv()
        total = kept[...] + y_in[step].astype(jnp.float32)

        @pl.when(step < depth - 1)
        def _():
            z_out[step] = total.astype(z_out.dtype)
            z_copy(step).start()

        @pl.when(step == depth - 1)
        def _():
            out_ref[...] = total

    @pl.loop(0, depth - 1)
    def _(step):
        z_copy(step).wait_recv()
        out_ref[...] += z_in[step].astype(jnp.float32)

    @pl.loop(0, depth)
    def _(step):
        y_copy(step).wait_send()

    @pl.loop(0, depth - 1)
    def _(step):
        z_copy(step).wait_send()


def embed_parts(gen_grid, pix, even, odd, model_dim, factor, collective_id):
    owners, images, share, slot = pix.shape
    depth = owners // 2
    low = jnp.bfloat16
    return pl.pallas_call(
        functools.partial(embed_kernel, factor),
        out_shape=jax.ShapeDtypeStruct((slot, model_dim), jnp.float32),
        in_specs=[pl.BlockSpec(memory_space=pl.ANY)] * 2
        + [pl.BlockSpec(memory_space=pltpu.VMEM)] * 2,
        out_specs=pl.BlockSpec(memory_space=pltpu.VMEM),
        scratch_shapes=[
            pltpu.VMEM(gen_grid.shape, low),
            pltpu.VMEM(pix.shape, low),
            pltpu.VMEM((images // 2, 2, owners, share, model_dim), low),
            pltpu.VMEM((depth, slot, model_dim), low),
            pltpu.VMEM((depth, slot, model_dim), low),
            pltpu.VMEM((depth - 1, slot, model_dim), low),
            pltpu.VMEM((depth - 1, slot, model_dim), low),
            pltpu.VMEM((slot, model_dim), jnp.float32),
            pltpu.SemaphoreType.DMA((2,)),
            pltpu.SemaphoreType.DMA((depth,)),
            pltpu.SemaphoreType.DMA((depth,)),
            pltpu.SemaphoreType.DMA((depth - 1,)),
            pltpu.SemaphoreType.DMA((depth - 1,)),
        ],
        compiler_params=pltpu.CompilerParams(
            collective_id=collective_id, has_side_effects=True, vmem_limit_bytes=60 << 20
        ),
        cost_estimate=pl.CostEstimate(
            flops=10**10, bytes_accessed=12 * 10**7, transcendentals=0
        ),
    )(gen_grid, pix, even, odd)


def tail_kernel(factor, plan, *refs):
    streams, dims, blocks, used = plan["streams"], plan["dims"], plan["blocks"], plan["used"]
    count, stages = len(streams), len(dims)
    bulk = plan["bulk"]
    refs = list(refs)

    def take(number):
        taken = refs[:number]
        del refs[:number]
        return taken

    gen_hbm, pix_hbm = take(2)
    weights_in = take(bulk)
    low_ref, even_ref, odd_ref, feature_ref, token_ref, bias_grad_ref = take(6)
    params = take(8)
    gen_b_grad, gain_lines = take(2)
    (pixel_land,) = take(1)
    outputs = take(bulk + 1)
    wide_out = take(8)
    gen_ref, pix_ref, kern_ref, gath, stage_ref, part_ref, part_in, wide_ref = take(8)
    expand_ref, shrink_ref = wide_out[4:6]
    own = take(2)
    landing = [take(len(stream["order"])) for stream in streams]
    packed, whole = take(2)
    load_sem, near_send, far_send, relay_send, block_recv, part_send, part_recv = take(7)
    send_sem, recv_sem, own_sem, gather_send, gather_recv = take(5)
    pixel_send, pixel_recv, pixel_own = take(3)
    sum_in, sum_send, sum_recv, share_send, share_recv, out_buffer, out_sem = take(7)

    depth = kern_ref.shape[0]
    owners, share = kern_ref.shape[2], kern_ref.shape[3]
    slot, model_dim = low_ref.shape
    place, side = pair_place()
    mine = place * 2 + side
    beside = place * 2 + 1 - side
    dk_ref = kern_ref.reshape(depth, gen_ref.shape[0] // 2, 2, owners * 8, model_dim)
    tok_dims = [d for d in dims if d[0] == "tok"]
    loads = [
        pltpu.make_async_copy(gen_hbm, gen_ref, load_sem.at[0]),
        pltpu.make_async_copy(pix_hbm, pix_ref, load_sem.at[1]),
        pltpu.make_async_copy(params[4], expand_ref, load_sem.at[2]),
        pltpu.make_async_copy(params[5], shrink_ref, load_sem.at[3]),
    ]
    for load in loads:
        load.start()
    barrier = pltpu.get_barrier_semaphore()
    for step in range(1, owners):
        pl.semaphore_signal(
            barrier,
            inc=1,
            device_id=at_band(lax.rem(mine + step, owners)),
            device_id_type=MESH,
        )
    for axis, bit in tok_dims:
        pl.semaphore_signal(barrier, inc=1, device_id=partner_of(axis, bit), device_id_type=MESH)
    pl.semaphore_wait(barrier, owners - 1 + len(tok_dims))

    def block_copy(source, block, target, sem):
        return pltpu.make_async_remote_copy(
            src_ref=source,
            dst_ref=gath.at[block],
            send_sem=sem,
            recv_sem=block_recv.at[block],
            device_id=at_band(target),
            device_id_type=MESH,
        )

    near = block_copy(low_ref, mine, beside, near_send)
    far = [
        block_copy(
            low_ref, mine, lax.rem(place + step, depth) * 2 + side, far_send.at[step - 1]
        )
        for step in range(1, depth)
    ]
    for copy in far[:1] + [near] + far[1:]:
        copy.start()
    bits = (2,) * len(tok_dims)
    segments = gen_ref.reshape(bits + (gen_ref.shape[0] * model_dim >> len(bits), gen_ref.shape[2]))
    sums = Sums(
        streams,
        weights_in + [segments, packed],
        outputs,
        own,
        landing,
        send_sem,
        recv_sem,
        own_sem,
        (out_buffer, out_sem),
    )
    heavy = [s for s in range(count) if streams[s]["source"] < bulk]
    slices = [s for s in range(count) if streams[s]["source"] == bulk]
    light = count - 1
    for stream in heavy:
        sums.begin(stream)
    for stream in heavy[:2]:
        sums.fetch(stream)
    gath[mine] = low_ref[...]
    loads[0].wait()
    make_kernels(gen_ref, even_ref, odd_ref, kern_ref, factor)
    for stream in heavy:
        sums.advance(stream, 0)
        if stream + 2 < len(heavy):
            sums.fetch(stream + 2)
    loads[1].wait()
    width = 256

    def relay(step):
        block = lax.rem(place + step, depth) * 2 + side
        return block_copy(gath.at[block], block, beside, relay_send.at[step - 1])

    def pixel_copy(image, step):
        target = lax.rem(mine + step, owners)
        return pltpu.make_async_remote_copy(
            src_ref=pix_ref.at[target, image],
            dst_ref=pixel_land.at[mine, image],
            send_sem=pixel_send.at[image, step - 1],
            recv_sem=pixel_recv.at[image, step - 1],
            device_id=at_band(target),
            device_id_type=MESH,
        )

    def pixel_local(image):
        return pltpu.make_async_copy(
            pix_ref.at[mine, image], pixel_land.at[mine, image], pixel_own.at[image]
        )

    def pair_work(pair):
        for parity in range(2):
            image = pair * 2 + parity
            rows = kern_ref[pair, parity].reshape(owners * share, model_dim)
            turned = lax.dot_general(
                rows, gath[image], (((1,), (1,)), ((), ())), preferred_element_type=jnp.float32
            )
            stage_ref[parity] = turned.astype(stage_ref.dtype).reshape(owners, share, slot)

        @pl.loop(0, model_dim // width)
        def _(part):
            columns = pl.ds(pl.multiple_of(part * width, width), width)
            both = []
            for parity in range(2):
                left = pix_ref[:, pair * 2 + parity].reshape(owners * share, slot)
                both.append(
                    jnp.dot(
                        left,
                        gath[pair * 2 + parity, :, columns],
                        preferred_element_type=jnp.float32,
                    ).reshape(owners * share // 8, 8, width)
                )
            even, odd = both[0], pltpu.roll(both[1], 4, 1)
            top = first_half(even.shape)
            for parity, value in (
                (0, jnp.where(top, even, odd)),
                (1, jnp.where(top, odd, even)),
            ):
                value = value.reshape(owners, share // 8, 8, width).transpose(1, 0, 2, 3)
                value = value.reshape(share // 8, owners * 8, width)
                dk_ref[pair, :, parity, :, columns] = value.astype(dk_ref.dtype)

        for parity in range(2):
            image = pair * 2 + parity
            pix_ref[:, image] = stage_ref[parity]
            pixel_local(image).start()

    def pixel_send_pair(pair):
        for parity in range(2):

            @pl.loop(1, owners)
            def _(step):
                pixel_copy(pair * 2 + parity, step).start()

    @pl.loop(0, depth)
    def _(step):
        pair = lax.rem(place + depth - step, depth)

        @pl.when(step > 0)
        def _():
            block_copy(low_ref, pair * 2 + side, beside, near_send).wait_recv()
            relay(depth - step).start()

        block_copy(low_ref, pair * 2 + 1 - side, beside, near_send).wait_recv()
        pair_work(pair)

    def pair_at(step):
        return lax.rem(place + depth - step, depth)

    waiting = [pair_at(step) for step in range(depth)]
    pixel_send_pair(waiting.pop(0))
    part_ref[...] = jnp.zeros_like(part_ref)

    @pl.loop(0, dk_ref.shape[1])
    def _(duo):
        for parity in range(2):
            rows = dk_ref[:, duo, parity].reshape(depth * owners * 8, model_dim)
            part_ref[parity] += jnp.dot(
                rows, gen_ref[duo * 2 + parity], preferred_element_type=jnp.float32
            ).reshape(depth, owners * 8, -1)
            weight = lax.dot_general(
                rows,
                (even_ref, odd_ref)[parity][...],
                (((0,), (0,)), ((), ())),
                preferred_element_type=jnp.float32,
            )
            gen_ref[duo * 2 + parity] = weight.astype(gen_ref.dtype)

    part_ref[...] = part_ref[...] * factor

    def part_copy(step):
        target = lax.rem(mine + step, owners)
        return pltpu.make_async_remote_copy(
            src_ref=part_ref.at[:, lax.div(target, 2)],
            dst_ref=part_in.at[step - 1],
            send_sem=part_send.at[step - 1],
            recv_sem=part_recv.at[step - 1],
            device_id=at_band(target),
            device_id_type=MESH,
        )

    copies = [part_copy(step) for step in range(1, owners)]
    for copy in copies:
        copy.start()
    for stream in slices:
        sums.begin(stream)
    early = len(heavy) // 2
    for stream in heavy[:early]:
        sums.advance(stream, 1)
    total = part_ref[:, place]
    for step, copy in enumerate(copies):
        copy.wait_recv()
        total += part_in[step]
    pixel_send_pair(waiting.pop(0))
    rows = total.shape[1]
    bands = rows // 2
    even_part = total[0].reshape(owners, 8, -1)
    odd_part = total[1].reshape(owners, 8, -1)
    low_rows = even_part + pltpu.roll(odd_part, 4, 1)
    low_rows = jnp.where(side == 0, low_rows, pltpu.roll(low_rows, 4, 1))
    low_rows = low_rows.reshape(rows, -1)
    chooser = (
        lax.broadcasted_iota(jnp.int32, (bands, rows), 1)
        == lax.div(lax.broadcasted_iota(jnp.int32, (bands, rows), 0), 4) * 8
        + lax.rem(lax.broadcasted_iota(jnp.int32, (bands, rows), 0), 4)
    ).astype(jnp.float32)
    d_band = precise_dot(chooser, low_rows)
    hyper_dim = d_band.shape[1]
    first_row = lax.broadcasted_iota(jnp.int32, (8, hyper_dim), 0) == 0
    tokens = jnp.concatenate(
        [feature_ref[...], jnp.where(first_row, token_ref[...], 0.0)], axis=0
    )
    cotangent = jnp.concatenate(
        [d_band, jnp.where(first_row, bias_grad_ref[...], 0.0)], axis=0
    )
    width = 512
    attention = tuple(params[place][...] for place in (0, 1, 2, 3, 6))
    segment, segment_back = jax.vjp(
        lambda t, p: hyper_attention(t, p, 1), tokens, attention
    )
    loads[2].wait()
    loads[3].wait()
    hyper_wide(segment, expand_ref, shrink_ref, wide_ref, width)
    norm_back = jax.vjp(
        lambda v, g: layer_norm(v, g, EPS_HYPER), wide_ref[...], params[7][...]
    )[1]
    d_total, second_grad = norm_back(cotangent)
    hyper_wide_back(segment, d_total, expand_ref, shrink_ref, wide_ref, width)
    token_grad, param_grads = segment_back(wide_ref[...])
    small = [param_grads[0], param_grads[1], param_grads[2], param_grads[3]]
    line_row = lax.broadcasted_iota(jnp.int32, gain_lines.shape, 0)
    lines = gain_lines[...]
    for row, value in enumerate((token_grad[bands : bands + 1], param_grads[4], second_grad)):
        lines = jnp.where(line_row == row, value, lines)

    def of_value(value):
        return lambda r, c: value[
            r.start : r.start + r.size, c.start : c.start + c.size
        ]

    def of_ref(ref):
        return lambda r, c: ref[r, c]

    wide = [of_value(value) for value in small]
    wide += [of_ref(expand_ref), of_ref(shrink_ref), of_ref(gen_b_grad), of_value(lines)]
    pack_blocks(blocks, used, packed, wide, stages)
    sums.begin(light)
    sums.advance(light, 0)
    for stream in slices:
        sums.advance(stream, 0)
    for stream in heavy[early:]:
        sums.advance(stream, 1)
    while len(waiting) > 1:
        pixel_send_pair(waiting.pop(0))
    sums.advance(light, len(tok_dims) - 1)
    piece = packed.shape[-2]
    quarter = landing[light][-1].reshape(owners, piece, 128)

    def sum_copy(step):
        target = lax.rem(mine + step, owners)
        return pltpu.make_async_remote_copy(
            src_ref=quarter.at[target],
            dst_ref=sum_in.at[step - 1],
            send_sem=sum_send.at[step - 1],
            recv_sem=sum_recv.at[step - 1],
            device_id=at_band(target),
            device_id_type=MESH,
        )

    own_tok = tuple(own_bit(*d) for d in tok_dims)
    spread_view = whole.reshape((owners,) + bits + (piece, 128))

    def share_copy(block, target, step):
        return pltpu.make_async_remote_copy(
            src_ref=spread_view.at[(block,) + own_tok],
            dst_ref=spread_view.at[(block,) + own_tok],
            send_sem=share_send.at[step - 1],
            recv_sem=share_recv.at[step - 1],
            device_id=at_band(target),
            device_id_type=MESH,
        )

    moves = [sum_copy(step) for step in range(1, owners)]
    for copy in moves:
        copy.start()
    pixel_send_pair(waiting.pop(0))
    for stream in heavy:
        sums.advance(stream, 2)
    light_total = quarter[mine].astype(jnp.float32)
    for step, copy in enumerate(moves):
        copy.wait_recv()
        light_total += sum_in[step].astype(jnp.float32)
    spread_view[(mine,) + own_tok] = light_total.astype(whole.dtype)
    shares = [
        share_copy(mine, lax.rem(mine + step, owners), step) for step in range(1, owners)
    ]
    for copy in shares:
        copy.start()
    for stage in range(3, stages):
        for stream in heavy:
            sums.advance(stream, stage)
    for step in range(1, owners):
        source = lax.rem(mine + owners - step, owners)
        share_copy(source, source, step).wait_recv()
    spread = Spread(dims, streams[light]["order"], whole, gather_send, gather_recv)
    for step in range(len(tok_dims)):
        spread.start()
        if step == 0:
            for stream in slices:
                sums.advance(stream, 1)
        spread.finish()
    for copy in moves + shares:
        copy.wait_send()
    unpack_blocks(blocks, whole, wide_out, stages)

    @pl.loop(0, depth * 2)
    def _(image):
        pixel_local(image).wait()

        @pl.loop(1, owners)
        def _(step):
            source = lax.rem(mine + owners - step, owners)
            pltpu.make_async_remote_copy(
                src_ref=pix_ref.at[source, image],
                dst_ref=pixel_land.at[source, image],
                send_sem=pixel_send.at[image, step - 1],
                recv_sem=pixel_recv.at[image, step - 1],
                device_id=at_band(source),
                device_id_type=MESH,
            ).wait()

    for copy in copies + [near] + far + [relay(step) for step in range(1, depth)]:
        copy.wait_send()
    sums.drain()


def tail_call(
    gen_grid,
    pix,
    low_own,
    even,
    odd,
    weights,
    features,
    token,
    bias_grad,
    params,
    gen_b_grad,
    gain_lines,
    factor,
    collective_id,
):
    dims, band_bits, tok_bits = mesh_bits()
    everything = len(dims)
    low = jnp.bfloat16
    owners, images, share, slot = pix.shape
    depth = owners // 2
    pixel_share, model_dim, hyper_dim = gen_grid.shape
    rows = owners * 8
    split, outs, landing, streams = [], [], [], []
    order = halving_order(0, band_bits, tok_bits)
    tallest = 0
    for k, weight in enumerate(weights):
        height = weight.shape[0] >> everything
        split.append(weight.reshape((2,) * everything + (height, weight.shape[1])))
        outs.append(jax.ShapeDtypeStruct((height, weight.shape[1]), jnp.float32))
        for start, size in row_chunks(height, 2 if height > 32 else 1):
            streams.append(stream_entry(k, k, start, size, order, dims, True))
            landing += landing_shapes(streams[-1], weight.shape[1])
            tallest = max(tallest, size)
    bulk = len(weights)
    tok_order = halving_order(2, band_bits, tok_bits)
    height = pixel_share * model_dim >> tok_bits
    outs.append(jax.ShapeDtypeStruct((height, hyper_dim), jnp.float32))
    for start, size in row_chunks(height, 4):
        out_rows = size
        streams.append(stream_entry(bulk, bulk, start, size, tok_order, dims, False, factor))
        landing += landing_shapes(streams[-1], hyper_dim)
    wide_shapes = [p.shape for p in params[:6]] + [gen_b_grad.shape, gain_lines.shape]
    blocks, used, piece = wide_plan(wide_shapes, 1 << everything)
    light = stream_entry(bulk + 1, None, 0, piece, tok_order, dims, False)
    light["span"] = dims
    streams.append(light)
    landing += [
        pltpu.VMEM((2,) * (everything - 1 - stage) + (piece, 128), low)
        for stage in range(tok_bits)
    ]
    count = len(streams)
    plan = {"streams": streams, "dims": dims, "bulk": bulk, "blocks": blocks, "used": used}
    space = (2,) * everything + (piece, 128)
    own = pltpu.VMEM((2,) * (everything - 1) + (tallest, model_dim), low)
    dma = pltpu.SemaphoreType.DMA
    return pl.pallas_call(
        functools.partial(tail_kernel, factor, plan),
        out_shape=[jax.ShapeDtypeStruct(pix.shape, low)]
        + outs
        + [jax.ShapeDtypeStruct(shape, jnp.float32) for shape in wide_shapes],
        in_specs=[pl.BlockSpec(memory_space=pl.ANY)] * (2 + bulk)
        + [pl.BlockSpec(memory_space=pltpu.VMEM)] * 10
        + [pl.BlockSpec(memory_space=pl.ANY)] * 2
        + [pl.BlockSpec(memory_space=pltpu.VMEM)] * 4,
        out_specs=[pl.BlockSpec(memory_space=pl.ANY)]
        + [pl.BlockSpec(memory_space=pltpu.VMEM)] * bulk
        + [pl.BlockSpec(memory_space=pl.ANY)]
        + [pl.BlockSpec(memory_space=pltpu.VMEM)] * len(wide_shapes),
        scratch_shapes=[
            pltpu.VMEM(gen_grid.shape, low),
            pltpu.VMEM(pix.shape, low),
            pltpu.VMEM((images // 2, 2, owners, share, model_dim), low),
            pltpu.VMEM((images, slot, model_dim), low),
            pltpu.VMEM((2, owners, share, slot), low),
            pltpu.VMEM((2, depth, rows, hyper_dim), jnp.float32),
            pltpu.VMEM((owners - 1, 2, rows, hyper_dim), jnp.float32),
            pltpu.VMEM((features.shape[0] + 8, hyper_dim), jnp.float32),
            own,
            own,
        ]
        + landing
        + [
            pltpu.VMEM(space, low),
            pltpu.VMEM(space, low),
            dma((4,)),
            dma,
            dma((depth - 1,)),
            dma((depth - 1,)),
            dma((owners,)),
            dma((owners - 1,)),
            dma((owners - 1,)),
            dma((count, everything)),
            dma((count, everything)),
            dma((2,)),
            dma((everything,)),
            dma((everything,)),
            dma((images, owners - 1)),
            dma((images, owners - 1)),
            dma((images,)),
            pltpu.VMEM((owners - 1, piece, 128), low),
            dma((owners - 1,)),
            dma((owners - 1,)),
            dma((owners - 1,)),
            dma((owners - 1,)),
            pltpu.VMEM((out_rows, hyper_dim), jnp.float32),
            dma,
        ],
        compiler_params=pltpu.CompilerParams(
            collective_id=collective_id, has_side_effects=True, vmem_limit_bytes=63 << 20
        ),
        cost_estimate=pl.CostEstimate(
            flops=2 * 10**10, bytes_accessed=3 * 10**8, transcendentals=0
        ),
    )(
        gen_grid,
        pix,
        *split,
        low_own,
        even,
        odd,
        features,
        token,
        bias_grad,
        *params,
        gen_b_grad,
        gain_lines,
    )


def layer_norm(values, scaling, epsilon):
    center = values - jnp.mean(values, axis=-1, keepdims=True)
    spread = jnp.mean(center * center, axis=-1, keepdims=True)
    return center * lax.rsqrt(spread + epsilon) * scaling


def block_norm(values, scaling):
    return layer_norm(values, scaling, EPS_BLOCK)


def exact_gelu(values):
    return jax.nn.gelu(values, approximate=False)


def wave_features(lengths, model_dim):
    middle = model_dim // 2
    angular = 1.0 / 10000.0 ** (jnp.arange(middle, dtype=jnp.float32) / middle)
    phases = (100.0 * lengths)[..., None] * angular
    return jnp.concatenate([jnp.sin(phases), jnp.cos(phases)], axis=-1)


def hyper_layer(features, params):
    (
        bias_token,
        hyper_query,
        hyper_key,
        hyper_value,
        hyper_out,
        hyper_up,
        hyper_down,
        hyper_gain1,
        hyper_gain2,
    ) = params
    images = features.shape[0]
    model_dim = features.shape[-1]
    head_size = model_dim // HHEADS
    tokens = jnp.concatenate(
        [features, jnp.broadcast_to(bias_token, (images, 1, model_dim))], axis=1
    )
    length = tokens.shape[1]
    queries = jnp.einsum("nsc,ce->nse", tokens, hyper_query, precision=PRECISE).reshape(
        images, length, HHEADS, head_size
    )
    keys_all = jnp.einsum("nsc,ce->nse", tokens, hyper_key, precision=PRECISE).reshape(
        images, length, HHEADS, head_size
    )
    values_all = jnp.einsum("nsc,ce->nse", tokens, hyper_value, precision=PRECISE).reshape(
        images, length, HHEADS, head_size
    )
    scores = jnp.einsum("nshe,nthe->nhst", queries, keys_all, precision=PRECISE) / math.sqrt(
        head_size
    )
    weights = jax.nn.softmax(scores, axis=-1)
    blended = jnp.einsum("nhst,nthe->nshe", weights, values_all, precision=PRECISE).reshape(
        images, length, model_dim
    )
    segment_one = layer_norm(
        tokens + jnp.einsum("nse,ef->nsf", blended, hyper_out, precision=PRECISE),
        hyper_gain1,
        EPS_HYPER,
    )
    expanded = jax.nn.gelu(
        jnp.einsum("nse,ef->nsf", segment_one, hyper_up, precision=PRECISE), approximate=False
    )
    second = layer_norm(
        segment_one + jnp.einsum("nsf,fe->nse", expanded, hyper_down, precision=PRECISE),
        hyper_gain2,
        EPS_HYPER,
    )
    return (second[:, :-1, :], second[:, -1, :])


def precise_dot(left, right, contract=(1, 0)):
    return lax.dot_general(
        left,
        right,
        (((contract[0],), (contract[1],)), ((), ())),
        precision=PRECISE,
        preferred_element_type=jnp.float32,
    )


def hyper_attention(tokens, params, images):
    query, key, value, mix, first = params
    rows, hyper_dim = tokens.shape
    bands = (rows - 8 * -(-images // 8)) // images
    head = hyper_dim // HHEADS

    def owner(index):
        return jnp.where(index < images * bands, lax.div(index, bands), index - images * bands)

    same = owner(lax.broadcasted_iota(jnp.int32, (rows, rows), 0)) == owner(
        lax.broadcasted_iota(jnp.int32, (rows, rows), 1)
    )
    lane = lax.div(lax.broadcasted_iota(jnp.int32, (1, hyper_dim), 1), head)
    queries = precise_dot(tokens, query) * (1.0 / math.sqrt(head))
    keys_all = precise_dot(tokens, key)
    values_all = precise_dot(tokens, value)
    blended = None
    for place in range(HHEADS):
        chosen = (lane == place).astype(jnp.float32)
        scores = precise_dot(queries * chosen, keys_all, (1, 1))
        scores = jnp.where(same, scores, -1e30)
        highest = lax.stop_gradient(jnp.max(scores, axis=-1, keepdims=True))
        lifted = jnp.exp(scores - highest)
        weights = lifted / jnp.sum(lifted, axis=-1, keepdims=True)
        part = precise_dot(weights, values_all * chosen)
        blended = part if blended is None else blended + part
    return layer_norm(tokens + precise_dot(blended, mix), first, EPS_HYPER)


def hyper_wide(segment, expand_ref, shrink_ref, total_ref, width):
    total_ref[...] = segment

    @pl.loop(0, expand_ref.shape[1] // width)
    def _(part):
        columns = pl.ds(pl.multiple_of(part * width, width), width)
        wide = precise_dot(segment, expand_ref[:, columns])
        active = 0.5 * wide * (1.0 + lax.erf(wide * math.sqrt(0.5)))
        total_ref[...] += precise_dot(active, shrink_ref[columns, :])


def hyper_wide_back(segment, d_total, expand_ref, shrink_ref, d_segment_ref, width):
    d_segment_ref[...] = d_total

    @pl.loop(0, expand_ref.shape[1] // width)
    def _(part):
        columns = pl.ds(pl.multiple_of(part * width, width), width)
        wide = precise_dot(segment, expand_ref[:, columns])
        bell = 0.5 * (1.0 + lax.erf(wide * math.sqrt(0.5)))
        slope = bell + wide * jnp.exp(-0.5 * wide * wide) * (1.0 / math.sqrt(2.0 * math.pi))
        d_wide = precise_dot(d_total, shrink_ref[columns, :], (1, 1)) * slope
        d_segment_ref[...] += precise_dot(d_wide, expand_ref[:, columns], (1, 1))
        shrink_ref[columns, :] = precise_dot(wide * bell, d_total, (0, 0))
        expand_ref[:, columns] = precise_dot(segment, d_wide, (0, 0))


def contract_rows(left_side, right_side):
    return lax.dot_general(
        left_side, right_side, (((0,), (0,)), ((), ())), preferred_element_type=jnp.float32
    )


def contract_cols(left_side, right_side):
    return lax.dot_general(
        left_side, right_side, (((1,), (1,)), ((), ())), preferred_element_type=jnp.float32
    )


def attention_scores(queries, keys_low, usable):
    head_size = queries.shape[-1]
    scores = jnp.einsum(
        "iqhe,ikhe->ihqk", queries, keys_low, preferred_element_type=jnp.float32
    ) / math.sqrt(head_size)
    return jnp.where(usable[:, None, None, :], scores, -1e30)


def block_forward(embedded, usable, weights_full, ln1_gain, ln2_gain):
    w_qkv_full, w_out_full, w_up_full, w_down_full = weights_full
    images, slot_count, model_dim = embedded.shape
    row_count = images * slot_count
    head_count = model_dim // HD
    flat_rows = embedded.reshape(row_count, model_dim)
    normed_one = block_norm(flat_rows, ln1_gain).astype(jnp.bfloat16)
    qkv_low = jnp.dot(normed_one, w_qkv_full, preferred_element_type=jnp.float32).astype(
        jnp.bfloat16
    )
    sections = qkv_low.reshape(images, slot_count, 3, head_count, HD)
    queries = sections[:, :, 0]
    keys_low = sections[:, :, 1]
    values_low = sections[:, :, 2]
    scores = attention_scores(queries, keys_low, usable)
    highest = jnp.max(scores, axis=-1, keepdims=True)
    lifted = jnp.exp(scores - highest)
    totals = jnp.sum(lifted, axis=-1, keepdims=True)
    attn_probs = (lifted / totals).astype(jnp.bfloat16)
    log_mass = highest + jnp.log(totals)
    attended = (
        jnp.einsum("ihqk,ikhe->iqhe", attn_probs, values_low, preferred_element_type=jnp.float32)
        .astype(jnp.bfloat16)
        .reshape(row_count, model_dim)
    )
    middle = flat_rows + jnp.dot(attended, w_out_full, preferred_element_type=jnp.float32)
    normed_two = block_norm(middle, ln2_gain).astype(jnp.bfloat16)
    hidden = jnp.dot(normed_two, w_up_full, preferred_element_type=jnp.float32)
    active = exact_gelu(hidden).astype(jnp.bfloat16)
    output = middle + jnp.dot(active, w_down_full, preferred_element_type=jnp.float32)
    return (
        flat_rows,
        normed_one,
        queries,
        keys_low,
        values_low,
        log_mass,
        attended,
        middle,
        normed_two,
        hidden,
        active,
        output,
    )


def block_backward(stored, usable, grad_rows, weights_full, ln1_gain, ln2_gain):
    (
        flat_rows,
        normed_one,
        queries,
        keys_low,
        values_low,
        log_mass,
        attended,
        middle,
        normed_two,
        hidden,
        active,
        output,
    ) = stored
    w_qkv_full, w_out_full, w_up_full, w_down_full = weights_full
    images, slot_count, head_count, head_size = queries.shape
    row_count, model_dim = flat_rows.shape
    grad_low = grad_rows.astype(jnp.bfloat16)
    grad_down = contract_rows(active, grad_low)
    d_active = contract_cols(grad_low, w_down_full)
    gelu_back = jax.vjp(exact_gelu, hidden)[1]
    d_hidden = gelu_back(d_active)[0].astype(jnp.bfloat16)
    grad_up_turned = contract_rows(d_hidden, normed_two)
    d_normed_two = contract_cols(d_hidden, w_up_full)
    norm_back_two = jax.vjp(block_norm, middle, ln2_gain)[1]
    d_middle_norm, grad_gain_two = norm_back_two(d_normed_two)
    d_middle = grad_rows + d_middle_norm
    d_middle_low = d_middle.astype(jnp.bfloat16)
    grad_out_turned = contract_rows(d_middle_low, attended)
    d_attended = (
        contract_cols(d_middle_low, w_out_full)
        .astype(jnp.bfloat16)
        .reshape(images, slot_count, head_count, head_size)
    )
    scores = attention_scores(queries, keys_low, usable)
    attn_float = jnp.exp(scores - log_mass)
    attn_probs = attn_float.astype(jnp.bfloat16)
    d_values = jnp.einsum(
        "ihqk,iqhe->ikhe", attn_probs, d_attended, preferred_element_type=jnp.float32
    ).astype(jnp.bfloat16)
    d_probs = jnp.einsum(
        "iqhe,ikhe->ihqk", d_attended, values_low, preferred_element_type=jnp.float32
    )
    d_scores = (
        attn_float * (d_probs - jnp.sum(attn_float * d_probs, axis=-1, keepdims=True))
    ).astype(jnp.bfloat16)
    d_queries = (
        jnp.einsum("ihqk,ikhe->iqhe", d_scores, keys_low, preferred_element_type=jnp.float32)
        / math.sqrt(head_size)
    ).astype(jnp.bfloat16)
    d_keys = (
        jnp.einsum("ihqk,iqhe->ikhe", d_scores, queries, preferred_element_type=jnp.float32)
        / math.sqrt(head_size)
    ).astype(jnp.bfloat16)
    d_qkv = jnp.stack([d_queries, d_keys, d_values], axis=2).reshape(row_count, 3 * model_dim)
    grad_qkv_turned = contract_rows(d_qkv, normed_one)
    d_normed_one = contract_cols(d_qkv, w_qkv_full)
    norm_back_one = jax.vjp(block_norm, flat_rows, ln1_gain)[1]
    d_flat, grad_gain_one = norm_back_one(d_normed_one)
    return (
        d_middle + d_flat,
        (grad_qkv_turned, grad_out_turned, grad_up_turned, grad_down, grad_gain_one, grad_gain_two),
    )


def body(
    pixels,
    wave_table,
    wave_index,
    patch_count,
    d_out,
    gen_w,
    gen_b,
    bias_token,
    hyper_query,
    hyper_key,
    hyper_value,
    hyper_out,
    hyper_up,
    hyper_down,
    hyper_gain1,
    hyper_gain2,
    w_qkv,
    w_out,
    w_up,
    w_down,
    ln1_gain,
    ln2_gain,
):
    group_images, band_share, slot_count, pixel_count = pixels.shape[1:]
    own_images = patch_count.shape[1]
    model_dim = w_out.shape[0]
    hyper_dim = gen_w.shape[1]
    all_bands = wave_index.shape[2]
    owners = lax.axis_size("band")
    slice_pixels = pixel_count // owners
    factor = 1.0 / math.sqrt(all_bands * pixel_count)
    band_place = lax.axis_index("band")
    hyper_params = (
        bias_token,
        hyper_query,
        hyper_key,
        hyper_value,
        hyper_out,
        hyper_up,
        hyper_down,
        hyper_gain1,
        hyper_gain2,
    )
    paired = (
        band_share == 4
        and own_images == 1
        and group_images == owners
        and owners % 2 == 0
        and slice_pixels % 4 == 0
        and model_dim % 256 == 0
    )
    if paired:
        pixel_lined = lax.all_to_all(turn_pixels(pixels[0], owners), "band", 0, 0, tiled=True)
    else:
        pixel_turned = (
            pixels[0]
            .reshape(group_images, band_share, slot_count, owners, slice_pixels)
            .transpose(3, 0, 4, 1, 2)
        )
        pixel_blocks = lax.all_to_all(pixel_turned, "band", 0, 0, tiled=True)
    gen_part = lax.all_gather(gen_w, "tok", axis=0, tiled=True)
    gen_grid = gen_part.reshape(slice_pixels, model_dim, hyper_dim)
    weights_full = (
        lax.all_gather(w_qkv, "tok", axis=1, tiled=True),
        lax.all_gather(w_out, "tok", axis=1, tiled=True),
        lax.all_gather(w_up, "tok", axis=1, tiled=True),
        lax.all_gather(w_down, "tok", axis=0, tiled=True),
    )
    catalog = lax.broadcasted_iota(jnp.int32, (1, 1, wave_table.shape[0]), 2)
    picked = (wave_index[0][:, :, None] == catalog).astype(jnp.float32)
    lengths_all = jnp.sum(picked * wave_table, axis=-1)
    hyper_input = wave_features(lengths_all, hyper_dim)
    band_feats = hyper_layer(hyper_input, hyper_params)[0]
    band_low = band_feats.astype(jnp.bfloat16).reshape(-1, hyper_dim)
    own_input = lax.dynamic_slice_in_dim(hyper_input, band_place * own_images, own_images, 0)

    def run_hyper(params):
        return hyper_layer(own_input, params)

    (_, bias_own), hyper_back = jax.vjp(run_hyper, hyper_params)
    if paired:
        ordered = (
            band_feats.astype(jnp.bfloat16)
            .reshape(group_images // 2, 2, owners, band_share, hyper_dim)
            .transpose(0, 2, 1, 3, 4)
        )
        even_rows = ordered.reshape(-1, hyper_dim)
        odd_rows = ordered[:, :, ::-1].reshape(-1, hyper_dim)
        convolved = embed_parts(
            gen_grid, pixel_lined, even_rows, odd_rows, model_dim, factor, 1
        )
    else:
        pixel_slices = pixel_blocks.transpose(1, 2, 0, 3, 4).reshape(
            group_images, slice_pixels * all_bands, slot_count
        )
        kernels = (
            jnp.einsum("pdc,nc->pnd", gen_grid, band_low, preferred_element_type=jnp.float32) * factor
        ).astype(jnp.bfloat16)
        kernel_grid = kernels.reshape(slice_pixels, group_images, all_bands, model_dim)
        kernel_rows = kernel_grid.transpose(1, 0, 2, 3).reshape(
            group_images, slice_pixels * all_bands, model_dim
        )
        product = jnp.einsum(
            "iks,ikd->isd", pixel_slices, kernel_rows, preferred_element_type=jnp.float32
        )
        convolved = lax.psum_scatter(
            product.reshape(group_images * slot_count, model_dim).astype(jnp.bfloat16),
            "band",
            scatter_dimension=0,
            tiled=True,
        ).astype(jnp.float32)
    bias_rows = jnp.dot(bias_own, gen_b, precision=PRECISE)
    embedded = convolved.reshape(own_images, slot_count, model_dim) + bias_rows[:, None, :]
    usable = lax.broadcasted_iota(jnp.int32, (own_images, slot_count), 1) < patch_count[0][:, None]
    stored = block_forward(embedded, usable, weights_full, ln1_gain, ln2_gain)
    row_mask = usable.reshape(-1, 1)
    layer_out = (
        jnp.where(row_mask, stored[-1], 0.0)
        .astype(jnp.bfloat16)
        .reshape(1, own_images, slot_count, model_dim)
    )
    grad_rows = jnp.where(row_mask, d_out[0].reshape(-1, model_dim).astype(jnp.float32), 0.0)
    d_embed, block_terms = block_backward(
        stored, usable, grad_rows, weights_full, ln1_gain, ln2_gain
    )
    d_embed_low = d_embed.astype(jnp.bfloat16).reshape(own_images, slot_count, model_dim)
    d_bias = jnp.sum(d_embed.reshape(own_images, slot_count, model_dim), axis=1)
    d_bias_feat = jnp.dot(d_bias, gen_b.T, precision=PRECISE)
    grad_gen_b = jnp.dot(bias_own.T, d_bias, precision=PRECISE)
    qkv_turned, out_turned, up_turned, grad_down, gain_one, gain_two = block_terms
    weight_terms = [
        term.astype(jnp.bfloat16) for term in (qkv_turned, out_turned, up_turned, grad_down)
    ]
    gain_rows = model_dim // hyper_dim
    gain_lines = [gain_one.reshape(-1, hyper_dim), gain_two.reshape(-1, hyper_dim)]
    fill = -(3 + 2 * gain_rows) % 16
    gain_lines.append(jnp.zeros((fill, hyper_dim), jnp.float32))
    if paired:
        (
            grad_blocks,
            qkv_sum,
            out_sum,
            up_sum,
            down_sum,
            grad_gen_w,
            query_sum,
            key_sum,
            value_sum,
            mix_sum,
            expand_sum,
            shrink_sum,
            gen_b_sum,
            line_sum,
        ) = tail_call(
            gen_grid,
            pixel_lined,
            d_embed_low.reshape(slot_count, model_dim),
            even_rows,
            odd_rows,
            weight_terms,
            own_input[0],
            bias_token[None],
            d_bias_feat,
            [
                hyper_query,
                hyper_key,
                hyper_value,
                hyper_out,
                hyper_up,
                hyper_down,
                hyper_gain1[None],
                hyper_gain2[None],
            ],
            grad_gen_b,
            jnp.concatenate([jnp.zeros((3, hyper_dim), jnp.float32)] + gain_lines),
            factor,
            2,
        )
        pixel_grad = unturn_pixels(grad_blocks, pixels.shape[1:])[None]
    else:
        d_gathered = lax.all_gather(d_embed_low, "band", axis=0, tiled=True)
        grad_slices = jnp.einsum(
            "ikd,isd->iks", kernel_rows, d_gathered, preferred_element_type=jnp.float32
        ).astype(jnp.bfloat16)
        grad_slices = grad_slices.reshape(
            group_images, slice_pixels, owners, band_share, slot_count
        ).transpose(2, 0, 1, 3, 4)
        d_kernel = jnp.einsum(
            "iks,isd->ikd", pixel_slices, d_gathered, preferred_element_type=jnp.float32
        ).astype(jnp.bfloat16)
        d_kernel = (
            d_kernel.reshape(group_images, slice_pixels, all_bands, model_dim)
            .transpose(1, 0, 2, 3)
            .reshape(slice_pixels, group_images * all_bands, model_dim)
        )
        d_band_part = (
            jnp.einsum("pnd,pdc->nc", d_kernel, gen_grid, preferred_element_type=jnp.float32) * factor
        )
        d_band_own = lax.psum_scatter(d_band_part, "band", scatter_dimension=0, tiled=True)
        gen_part_grad = (
            jnp.einsum("pnd,nc->pdc", d_kernel, band_low, preferred_element_type=jnp.float32) * factor
        )
        gen_low = gen_part_grad.reshape(-1, hyper_dim).astype(jnp.bfloat16)
        grad_slices = lax.all_to_all(grad_slices, "band", 0, 0, tiled=True)
        pixel_grad = grad_slices.transpose(1, 3, 4, 0, 2).reshape(pixels.shape)
        (
            grad_token,
            grad_query,
            grad_key,
            grad_value,
            grad_mix,
            grad_expand,
            grad_shrink,
            grad_first_gain,
            grad_second_gain,
        ) = hyper_back((d_band_own.reshape(own_images, all_bands, hyper_dim), d_bias_feat))[0]
        lines = jnp.concatenate(
            [grad_token[None], grad_first_gain[None], grad_second_gain[None]] + gain_lines
        )
        (
            qkv_sum,
            out_sum,
            up_sum,
            down_sum,
            grad_gen_w,
            query_sum,
            key_sum,
            value_sum,
            mix_sum,
            expand_sum,
            shrink_sum,
            gen_b_sum,
            line_sum,
        ) = reduce_all(
            weight_terms + [gen_low],
            [1, 0, 1, 1, 2],
            [2, 1, 2, 2, 2],
            [
                grad_query,
                grad_key,
                grad_value,
                grad_mix,
                grad_expand,
                grad_shrink,
                grad_gen_b,
                lines,
            ],
            3,
        )
    devices = owners * lax.axis_size("tok")
    place = band_place * lax.axis_size("tok") + lax.axis_index("tok")
    gain_share = model_dim // devices

    def own_gain(whole):
        return lax.dynamic_slice_in_dim(whole.reshape(-1), place * gain_share, gain_share, 0)

    return (
        layer_out,
        pixel_grad,
        grad_gen_w,
        gen_b_sum,
        line_sum[0],
        query_sum,
        key_sum,
        value_sum,
        mix_sum,
        expand_sum,
        shrink_sum,
        line_sum[1],
        line_sum[2],
        qkv_sum.T,
        out_sum.T,
        up_sum.T,
        down_sum,
        own_gain(line_sum[3 : 3 + gain_rows]),
        own_gain(line_sum[3 + gain_rows : 3 + 2 * gain_rows]),
    )


def solution(mesh):
    placed = (
        P("tok", None, "band", None, None),
        P(),
        P("tok", None, None),
        P("tok", "band"),
        P("tok", "band", None, None),
        P(("band", "tok"), None),
        P(),
        P(),
        P(),
        P(),
        P(),
        P(),
        P(),
        P(),
        P(),
        P(),
        P(None, "tok"),
        P(None, "tok"),
        P(None, "tok"),
        P("tok", None),
        P(),
        P(),
    )
    return jax.shard_map(
        body,
        mesh=mesh,
        in_specs=placed,
        out_specs=(
            P("tok", "band", None, None),
            P("tok", None, "band", None, None),
            P(("band", "tok"), None),
            P(),
            P(),
            P(),
            P(),
            P(),
            P(),
            P(),
            P(),
            P(),
            P(),
            P(None, ("band", "tok")),
            P(None, ("band", "tok")),
            P(None, ("band", "tok")),
            P(("band", "tok"), None),
            P(("band", "tok")),
            P(("band", "tok")),
        ),
        check_vma=False,
    )
```

```python
import functools
import math

import jax
import jax.numpy as jnp
from jax import lax
from jax.experimental import pallas as pl
from jax.experimental.pallas import tpu as pltpu
from jax.sharding import PartitionSpec as P

HD = 64
HHEADS = 4


EPS_BLOCK = 1e-06
EPS_HYPER = 1e-05
PRECISE = lax.Precision.HIGHEST


MESH = pl.DeviceIdType.MESH


def mesh_bits():
    tok_bits = (lax.axis_size("tok") - 1).bit_length()
    band_bits = (lax.axis_size("band") - 1).bit_length()
    dims = [("band", b) for b in reversed(range(band_bits))]
    dims += [("tok", b) for b in reversed(range(tok_bits))]
    return dims, band_bits, tok_bits


def own_bit(axis, bit):
    return lax.rem(lax.div(lax.axis_index(axis), 1 << bit), 2)


def partner_of(axis, bit):
    place = lax.axis_index(axis)
    mine = own_bit(axis, bit)
    other = place + (1 - 2 * mine) * (1 << bit)
    band, tok = lax.axis_index("band"), lax.axis_index("tok")
    return (other, tok) if axis == "band" else (band, other)


def halving_order(which, band_bits, tok_bits):
    tok = [("tok", b) for b in range(tok_bits)]
    band = [("band", b) for b in range(band_bits)]
    if which == 2:
        return tok
    if which == 0:
        return tok + band
    return tok[:1] + band[:1] + tok[1:] + band[1:]


def pick(remaining, axis_bit, value):
    place = remaining.index(axis_bit)
    return tuple([slice(None)] * place + [value])


def add_block(dest, left, right):
    lead = dest.shape[:-2]

    def one(index):
        spot = []
        for size in reversed(lead):
            spot.insert(0, lax.rem(index, size))
            index = lax.div(index, size)
        spot = tuple(spot)
        dest[spot] = (left(spot) + right(spot)).astype(dest.dtype)

    pl.loop(0, math.prod(lead))(one)


def wide_blocks(shapes, piece):
    blocks, start = [], 0
    for index, (rows, columns) in enumerate(shapes):
        for part in range(columns // 128):
            row = 0
            while row < rows:
                inside = start % piece
                size = min(rows - row, piece - inside)
                blocks.append((index, row, part, start // piece, inside, size))
                row += size
                start += size
    return blocks, start


def segment_spot(segment, count):
    return tuple((segment >> (count - 1 - bit)) & 1 for bit in range(count))


class Sums:
    def __init__(
        self, streams, sources, outputs, own, landing, send_sem, recv_sem, own_sem, buffer=None
    ):
        self.buffer = buffer
        self.streams, self.sources, self.outputs = streams, sources, outputs
        self.own, self.landing = own, landing
        self.send_sem, self.recv_sem, self.own_sem = send_sem, recv_sem, own_sem
        self.flying, self.local = {}, {}

    def part(self, stream, value):
        entry = self.streams[stream]
        spot = pick(entry["span"], entry["order"][0], value)
        spot = spot + (slice(None),) * (len(entry["span"]) - len(spot))
        rows = pl.ds(entry["start"], entry["rows"])
        return self.sources[entry["source"]].at[spot + (rows,)]

    def fetch(self, stream):
        entry = self.streams[stream]
        if entry["fetch"]:
            slot = stream % len(self.own)
            whole = (slice(None),) * (len(entry["span"]) - 1)
            target = self.own[slot].at[whole + (pl.ds(0, entry["rows"]),)]
            copy = pltpu.make_async_copy(
                self.part(stream, own_bit(*entry["order"][0])), target, self.own_sem.at[slot]
            )
            copy.start()
            self.local[stream] = (copy, target)

    def send(self, stream, stage, source):
        axis, bit = self.streams[stream]["order"][stage]
        copy = pltpu.make_async_remote_copy(
            src_ref=source,
            dst_ref=self.landing[stream][stage],
            send_sem=self.send_sem.at[stream, stage],
            recv_sem=self.recv_sem.at[stream, stage],
            device_id=partner_of(axis, bit),
            device_id_type=MESH,
        )
        copy.start()
        self.flying[stream, stage] = copy

    def begin(self, stream):
        first = self.streams[stream]["order"][0]
        self.send(stream, 0, self.part(stream, 1 - own_bit(*first)))

    def advance(self, stream, stage):
        entry = self.streams[stream]
        order, span = entry["order"], entry["span"]
        if stage >= len(order):
            return
        remaining = [d for d in span if d not in order[:stage]]
        axis_bit = order[stage]
        after = [d for d in remaining if d != axis_bit]
        self.flying[stream, stage].wait_recv()
        land = self.landing[stream][stage]
        if stage > 0:
            held = self.landing[stream][stage - 1].at[
                pick(remaining, axis_bit, own_bit(*axis_bit))
            ]
        elif stream in self.local:
            self.local[stream][0].wait()
            held = self.local[stream][1]
        else:
            held = self.part(stream, own_bit(*axis_bit))
        if stage == len(order) - 1 and entry["out"] is not None:
            total = land[...].astype(jnp.float32) + held[...].astype(jnp.float32)
            rows = pl.ds(entry["base"] + entry["start"], entry["rows"])
            if entry["fetch"]:
                self.outputs[entry["out"]][rows] = total * entry["scale"]
            else:
                buffer, sem = self.buffer
                buffer[...] = total * entry["scale"]
                copy = pltpu.make_async_copy(buffer, self.outputs[entry["out"]].at[rows], sem)
                copy.start()
                copy.wait()
        else:
            add_block(
                land,
                lambda spot: land[spot].astype(jnp.float32),
                lambda spot: held[spot].astype(jnp.float32),
            )
            if stage < len(order) - 1:
                following = order[stage + 1]
                self.send(
                    stream, stage + 1, land.at[pick(after, following, 1 - own_bit(*following))]
                )

    def drain(self):
        for copy in self.flying.values():
            copy.wait_send()


class Spread:
    def __init__(self, dims, order, whole, send_sem, recv_sem):
        self.dims, self.order, self.whole = dims, list(reversed(order)), whole
        self.send_sem, self.recv_sem = send_sem, recv_sem
        self.spot = [own_bit(*d) if d in order else slice(None) for d in dims]
        self.copies = []

    def start(self):
        step = len(self.copies)
        view = self.whole.at[tuple(self.spot)]
        copy = pltpu.make_async_remote_copy(
            src_ref=view,
            dst_ref=view,
            send_sem=self.send_sem.at[step],
            recv_sem=self.recv_sem.at[step],
            device_id=partner_of(*self.order[step]),
            device_id_type=MESH,
        )
        copy.start()
        self.copies.append(copy)

    def finish(self):
        self.copies[-1].wait()
        self.spot[self.dims.index(self.order[len(self.copies) - 1])] = slice(None)


def pack_blocks(blocks, used, packed, wide, stages):
    for index, row, part, segment, inside, size in blocks:
        packed[segment_spot(segment, stages) + (pl.ds(inside, size),)] = wide[index](
            pl.ds(row, size), pl.ds(part * 128, 128)
        ).astype(packed.dtype)
    piece = packed.shape[-2]
    while used < piece << stages:
        size = piece - used % piece
        packed[segment_spot(used // piece, stages) + (pl.ds(used % piece, size),)] = jnp.zeros(
            (size, 128), packed.dtype
        )
        used += size


def unpack_blocks(blocks, whole, wide_out, stages):
    for index, row, part, segment, inside, size in blocks:
        wide_out[index][pl.ds(row, size), pl.ds(part * 128, 128)] = whole[
            segment_spot(segment, stages) + (pl.ds(inside, size),)
        ].astype(jnp.float32)


def reduce_kernel(plan, blocks, used, *refs):
    streams, dims = plan["streams"], plan["dims"]
    count, stages = len(streams), len(dims)
    pos = plan["bulk"]
    inputs = list(refs[:pos])
    wide = refs[pos : pos + plan["wide"]]
    pos += plan["wide"]
    outputs = refs[pos : pos + plan["bulk"]]
    pos += plan["bulk"]
    wide_out = refs[pos : pos + plan["wide"]]
    pos += plan["wide"]
    own = refs[pos : pos + count - 1]
    pos += count - 1
    landing = []
    for stream in streams:
        landing.append(refs[pos : pos + len(stream["order"])])
        pos += len(stream["order"])
    packed, whole, send_sem, recv_sem, own_sem, gather_send, gather_recv = refs[pos:]
    barrier = pltpu.get_barrier_semaphore()
    for axis, bit in dims:
        pl.semaphore_signal(barrier, inc=1, device_id=partner_of(axis, bit), device_id_type=MESH)
    pl.semaphore_wait(barrier, stages)
    sums = Sums(
        streams, inputs + [packed], outputs, own, landing, send_sem, recv_sem, own_sem
    )
    for stream in range(count - 1):
        sums.begin(stream)
        sums.fetch(stream)
    pack_blocks(
        blocks, used, packed, [lambda r, c, ref=ref: ref[r, c] for ref in wide], stages
    )
    sums.begin(count - 1)
    for stage in range(stages):
        for stream in range(count):
            sums.advance(stream, stage)
    spread = Spread(dims, streams[-1]["order"], whole, gather_send, gather_recv)
    whole[tuple(spread.spot)] = landing[count - 1][stages - 1][...]
    for _ in range(stages):
        spread.start()
        spread.finish()
    unpack_blocks(blocks, whole, wide_out, stages)
    sums.drain()


def stream_entry(source, out, start, rows, order, dims, fetch, scale=1.0):
    return {
        "source": source,
        "out": out,
        "start": start,
        "rows": rows,
        "order": order,
        "span": [d for d in dims if d in order],
        "fetch": fetch,
        "base": 0,
        "scale": scale,
    }


def landing_shapes(entry, lanes):
    stages = len(entry["order"])
    return [
        pltpu.VMEM((2,) * (stages - 1 - stage) + (entry["rows"], lanes), jnp.bfloat16)
        for stage in range(stages)
    ]


def wide_plan(shapes, devices):
    used = sum(math.prod(shape) for shape in shapes) // 128
    piece = -(-used // (16 * devices)) * 16
    return wide_blocks(shapes, piece)[0], used, piece


def row_chunks(rows, chunks):
    size = -(-rows // chunks // 8) * 8
    return [(start, min(size, rows - start)) for start in range(0, rows, size)]


def reduce_all(arrays, whiches, chunks, wide, collective_id):
    dims, band_bits, tok_bits = mesh_bits()
    low, everything = jnp.bfloat16, len(dims)
    split, outs, own, landing, streams = [], [], [], [], []
    for k, array in enumerate(arrays):
        order = halving_order(whiches[k], band_bits, tok_bits)
        stages = len(order)
        rows, lanes = array.shape[0] >> stages, array.shape[1]
        split.append(array.reshape((2,) * stages + (rows, lanes)))
        outs.append(jax.ShapeDtypeStruct((rows, lanes), jnp.float32))
        for start, size in row_chunks(rows, chunks[k]):
            streams.append(stream_entry(k, k, start, size, order, dims, True))
            own.append(pltpu.VMEM((2,) * (stages - 1) + (size, lanes), low))
            landing += landing_shapes(streams[-1], lanes)
    blocks, used, piece = wide_plan([part.shape for part in wide], 1 << everything)
    order = halving_order(0, band_bits, tok_bits)
    streams.append(stream_entry(len(arrays), None, 0, piece, order, dims, False))
    landing += landing_shapes(streams[-1], 128)
    outs += [jax.ShapeDtypeStruct(part.shape, jnp.float32) for part in wide]
    count = len(streams)
    plan = {"streams": streams, "dims": dims, "bulk": len(arrays), "wide": len(wide)}
    sent = sum(a.size for a in arrays)
    space = (2,) * everything + (piece, 128)
    return pl.pallas_call(
        functools.partial(reduce_kernel, plan, blocks, used),
        out_shape=outs,
        in_specs=[pl.BlockSpec(memory_space=pl.ANY)] * len(arrays)
        + [pl.BlockSpec(memory_space=pltpu.VMEM)] * len(wide),
        out_specs=[pl.BlockSpec(memory_space=pltpu.VMEM)] * len(outs),
        scratch_shapes=own
        + landing
        + [
            pltpu.VMEM(space, low),
            pltpu.VMEM(space, low),
            pltpu.SemaphoreType.DMA((count, everything)),
            pltpu.SemaphoreType.DMA((count, everything)),
            pltpu.SemaphoreType.DMA((count,)),
            pltpu.SemaphoreType.DMA((everything,)),
            pltpu.SemaphoreType.DMA((everything,)),
        ],
        compiler_params=pltpu.CompilerParams(
            collective_id=collective_id, has_side_effects=True, vmem_limit_bytes=60 << 20
        ),
        cost_estimate=pl.CostEstimate(flops=2 * sent, bytes_accessed=40 * sent, transcendentals=0),
    )(*split, *wide)


def turn_kernel(in_ref, out_ref, lines):
    bands = in_ref.shape[1]
    halves, rows = lines.shape[:2]
    for band in range(bands):
        turned = in_ref[0, band].astype(jnp.float32).T
        for half in range(halves):
            lines[half, pl.ds(band, rows // bands, stride=bands), :] = turned[
                :, half * 128 : (half + 1) * 128
            ]
    for half in range(halves):
        out_ref[:, 0, :, pl.ds(half * 128, 128)] = (
            lines[half].astype(out_ref.dtype).reshape(*out_ref.shape[:1], -1, 128)
        )


def turn_pixels(pixels, owners):
    images, bands, slot, pixel_count = pixels.shape
    share = pixel_count // owners * bands
    return pl.pallas_call(
        turn_kernel,
        grid=(images,),
        out_shape=jax.ShapeDtypeStruct((owners, images, share, slot), pixels.dtype),
        in_specs=[pl.BlockSpec((1, bands, slot, pixel_count), lambda i: (i, 0, 0, 0))],
        out_specs=pl.BlockSpec((owners, 1, share, slot), lambda i: (0, i, 0, 0)),
        scratch_shapes=[pltpu.VMEM((slot // 128, pixel_count * bands, 128), jnp.float32)],
        compiler_params=pltpu.CompilerParams(vmem_limit_bytes=20 << 20),
    )(pixels)


def unturn_kernel(blocks, heights, *refs):
    in_ref, weight_ref, whole_ref, out_ref = refs[:4]
    weight_out = refs[4 : 4 + len(heights)]
    wide_out = refs[4 + len(heights) : -1]
    lines = refs[-1]
    bands = out_ref.shape[1]
    halves, rows = lines.shape[:2]
    for half in range(halves):
        lines[half] = (
            in_ref[:, 0, :, pl.ds(half * 128, 128)].astype(jnp.float32).reshape(rows, 128)
        )
    for band in range(bands):
        for half in range(halves):
            piece = lines[half, pl.ds(band, rows // bands, stride=bands), :]
            out_ref[0, band, pl.ds(half * 128, 128), :] = piece.T.astype(out_ref.dtype)

    @pl.when(pl.program_id(0) == 0)
    def _():
        base = 0
        for number, height in enumerate(heights):
            part = weight_ref[pl.ds(base, height), :]
            weight_out[number][...] = part.T if number < len(heights) - 1 else part
            base += height
        unpack_blocks(blocks, whole_ref, wide_out, len(whole_ref.shape) - 2)


def unturn_pixels(pixel_blocks, shape, weight_sums, heights, whole, wide_shapes):
    owners, images, share, slot = pixel_blocks.shape
    bands, pixel_count = shape[1], shape[3]
    model_dim = weight_sums.shape[1]
    blocks = wide_plan(wide_shapes, math.prod(whole.shape[:-2]))[0]

    def fixed(array_shape):
        return pl.BlockSpec(array_shape, lambda i: (0,) * len(array_shape))

    given = [(model_dim, height) for height in heights[:-1]] + [(heights[-1], model_dim)]
    given += wide_shapes
    return pl.pallas_call(
        functools.partial(unturn_kernel, blocks, heights),
        grid=(images,),
        out_shape=[jax.ShapeDtypeStruct(shape, pixel_blocks.dtype)]
        + [jax.ShapeDtypeStruct(s, jnp.float32) for s in given],
        in_specs=[
            pl.BlockSpec((owners, 1, share, slot), lambda i: (0, i, 0, 0)),
            fixed(weight_sums.shape),
            fixed(whole.shape),
        ],
        out_specs=[pl.BlockSpec((1, bands, slot, pixel_count), lambda i: (i, 0, 0, 0))]
        + [fixed(s) for s in given],
        scratch_shapes=[pltpu.VMEM((slot // 128, pixel_count * bands, 128), jnp.float32)],
        compiler_params=pltpu.CompilerParams(vmem_limit_bytes=40 << 20),
    )(pixel_blocks, weight_sums, whole)


def at_band(place):
    return (place, lax.axis_index("tok"))


def pair_place():
    band = lax.axis_index("band")
    return lax.div(band, 2), lax.rem(band, 2)


def first_half(shape):
    return lax.rem(lax.broadcasted_iota(jnp.int32, shape, len(shape) - 2), 8) < 4


def make_kernels(gen_ref, even_ref, odd_ref, kern_ref, factor):
    pixel_share, model_dim = gen_ref.shape[:2]
    pairs, _, owners, _, _ = kern_ref.shape
    width = 256

    @pl.loop(0, pixel_share // 4)
    def _(quad):
        @pl.loop(0, model_dim // width)
        def _(part):
            columns = pl.ds(pl.multiple_of(part * width, width), width)
            pieces = []
            for offset in range(4):
                rows = (even_ref, odd_ref)[offset % 2][...]
                piece = lax.dot_general(
                    rows,
                    gen_ref[quad * 4 + offset, columns, :],
                    (((1,), (1,)), ((), ())),
                    preferred_element_type=jnp.float32,
                )
                pieces.append((piece * factor).reshape(pairs * owners, 8, width))
            top = first_half(pieces[0].shape)
            even, odd = [], []
            for a, b in ((pieces[0], pieces[1]), (pieces[2], pieces[3])):
                even.append(jnp.where(top, a, b))
                odd.append(pltpu.roll(jnp.where(top, b, a), 4, 1))
            rows = pl.ds(pl.multiple_of(quad * 16, 16), 16)
            for parity, both in ((0, even), (1, odd)):
                block = jnp.concatenate(both, axis=1).astype(jnp.bfloat16)
                kern_ref[:, parity, :, rows, columns] = block.reshape(pairs, owners, 16, width)


def embed_kernel(
    factor,
    gen_hbm,
    pix_hbm,
    even_ref,
    odd_ref,
    out_ref,
    gen_ref,
    pix_ref,
    kern_ref,
    y_out,
    y_in,
    z_out,
    z_in,
    kept,
    load_sem,
    y_send,
    y_recv,
    z_send,
    z_recv,
):
    pairs = kern_ref.shape[0]
    depth, side = pairs, lax.rem(lax.axis_index("band"), 2)
    place = lax.div(lax.axis_index("band"), 2)
    loads = [
        pltpu.make_async_copy(gen_hbm, gen_ref, load_sem.at[0]),
        pltpu.make_async_copy(pix_hbm, pix_ref, load_sem.at[1]),
    ]
    for load in loads:
        load.start()
    barrier = pltpu.get_barrier_semaphore()
    pl.semaphore_signal(
        barrier, inc=1, device_id=at_band(place * 2 + 1 - side), device_id_type=MESH
    )
    for step in range(depth - 1):
        target = lax.rem(place + 1 + step, depth)
        pl.semaphore_signal(
            barrier, inc=1, device_id=at_band(target * 2 + side), device_id_type=MESH
        )
    loads[0].wait()
    make_kernels(gen_ref, even_ref, odd_ref, kern_ref, factor)
    loads[1].wait()
    pl.semaphore_wait(barrier, depth)
    width = 256

    def conv(pair, parity, store):
        slot, inner = kern_ref.shape[3], pix_ref.shape[3]
        owners = kern_ref.shape[2]
        left = pix_ref[:, pair * 2 + parity].reshape(owners * slot, inner).T

        @pl.loop(0, kern_ref.shape[4] // width)
        def _(part):
            columns = pl.ds(pl.multiple_of(part * width, width), width)
            right = kern_ref[pair, parity, :, :, columns].reshape(owners * slot, width)
            store(
                columns,
                jnp.dot(left, right, preferred_element_type=jnp.float32),
            )

    def y_copy(step):
        return pltpu.make_async_remote_copy(
            src_ref=y_out.at[step],
            dst_ref=y_in.at[step],
            send_sem=y_send.at[step],
            recv_sem=y_recv.at[step],
            device_id=at_band(place * 2 + 1 - side),
            device_id_type=MESH,
        )

    def z_copy(step):
        return pltpu.make_async_remote_copy(
            src_ref=z_out.at[step],
            dst_ref=z_in.at[step],
            send_sem=z_send.at[step],
            recv_sem=z_recv.at[step],
            device_id=at_band(lax.rem(place + 1 + step, depth) * 2 + side),
            device_id_type=MESH,
        )

    @pl.loop(0, depth)
    def _(step):
        def store(columns, value):
            y_out[step, :, columns] = value.astype(y_out.dtype)

        conv(lax.rem(place + 1 + step, depth), 1 - side, store)
        y_copy(step).start()

    @pl.loop(0, depth)
    def _(step):
        def store(columns, value):
            kept[:, columns] = value

        conv(lax.rem(place + 1 + step, depth), side, store)
        y_copy(step).wait_recv()
        total = kept[...] + y_in[step].astype(jnp.float32)

        @pl.when(step < depth - 1)
        def _():
            z_out[step] = total.astype(z_out.dtype)
            z_copy(step).start()

        @pl.when(step == depth - 1)
        def _():
            out_ref[...] = total

    @pl.loop(0, depth - 1)
    def _(step):
        z_copy(step).wait_recv()
        out_ref[...] += z_in[step].astype(jnp.float32)

    @pl.loop(0, depth)
    def _(step):
        y_copy(step).wait_send()

    @pl.loop(0, depth - 1)
    def _(step):
        z_copy(step).wait_send()


def embed_parts(gen_grid, pix, even, odd, model_dim, factor, collective_id):
    owners, images, share, slot = pix.shape
    depth = owners // 2
    low = jnp.bfloat16
    return pl.pallas_call(
        functools.partial(embed_kernel, factor),
        out_shape=jax.ShapeDtypeStruct((slot, model_dim), jnp.float32),
        in_specs=[pl.BlockSpec(memory_space=pl.ANY)] * 2
        + [pl.BlockSpec(memory_space=pltpu.VMEM)] * 2,
        out_specs=pl.BlockSpec(memory_space=pltpu.VMEM),
        scratch_shapes=[
            pltpu.VMEM(gen_grid.shape, low),
            pltpu.VMEM(pix.shape, low),
            pltpu.VMEM((images // 2, 2, owners, share, model_dim), low),
            pltpu.VMEM((depth, slot, model_dim), low),
            pltpu.VMEM((depth, slot, model_dim), low),
            pltpu.VMEM((depth - 1, slot, model_dim), low),
            pltpu.VMEM((depth - 1, slot, model_dim), low),
            pltpu.VMEM((slot, model_dim), jnp.float32),
            pltpu.SemaphoreType.DMA((2,)),
            pltpu.SemaphoreType.DMA((depth,)),
            pltpu.SemaphoreType.DMA((depth,)),
            pltpu.SemaphoreType.DMA((depth - 1,)),
            pltpu.SemaphoreType.DMA((depth - 1,)),
        ],
        compiler_params=pltpu.CompilerParams(
            collective_id=collective_id, has_side_effects=True, vmem_limit_bytes=60 << 20
        ),
        cost_estimate=pl.CostEstimate(
            flops=10**10, bytes_accessed=12 * 10**7, transcendentals=0
        ),
    )(gen_grid, pix, even, odd)


def tail_kernel(factor, plan, *refs):
    streams, dims, blocks, used = plan["streams"], plan["dims"], plan["blocks"], plan["used"]
    count, stages = len(streams), len(dims)
    bulk = plan["bulk"]
    refs = list(refs)

    def take(number):
        taken = refs[:number]
        del refs[:number]
        return taken

    gen_hbm, pix_hbm = take(2)
    weights_in = take(bulk)
    low_ref, even_ref, odd_ref, feature_ref, token_ref, bias_grad_ref = take(6)
    params = take(8)
    gen_b_grad, gain_lines = take(2)
    (pixel_land,) = take(1)
    outputs = take(2)
    (whole,) = take(1)
    gen_ref, pix_ref, kern_ref, gath, stage_ref, part_ref, part_in, wide_ref = take(8)
    expand_ref, shrink_ref = take(2)
    own = take(2)
    landing = [take(len(stream["order"])) for stream in streams]
    (packed,) = take(1)
    load_sem, near_send, far_send, relay_send, onward_send = take(5)
    block_recv, part_send, part_recv = take(3)
    send_sem, recv_sem, own_sem, gather_send, gather_recv = take(5)
    pixel_send, pixel_recv, pixel_own = take(3)
    sum_in, sum_send, sum_recv, share_send, share_recv, out_buffer, out_sem = take(7)

    depth = kern_ref.shape[0]
    owners, share = kern_ref.shape[2], kern_ref.shape[3]
    slot, model_dim = low_ref.shape
    place, side = pair_place()
    mine = place * 2 + side
    beside = place * 2 + 1 - side
    dk_ref = kern_ref.reshape(depth, gen_ref.shape[0] // 2, 2, owners * 8, model_dim)
    tok_dims = [d for d in dims if d[0] == "tok"]
    loads = [
        pltpu.make_async_copy(gen_hbm, gen_ref, load_sem.at[0]),
        pltpu.make_async_copy(pix_hbm, pix_ref, load_sem.at[1]),
        pltpu.make_async_copy(params[4], expand_ref, load_sem.at[2]),
        pltpu.make_async_copy(params[5], shrink_ref, load_sem.at[3]),
    ]
    for load in loads:
        load.start()
    barrier = pltpu.get_barrier_semaphore()
    for step in range(1, owners):
        pl.semaphore_signal(
            barrier,
            inc=1,
            device_id=at_band(lax.rem(mine + step, owners)),
            device_id_type=MESH,
        )
    for axis, bit in tok_dims:
        pl.semaphore_signal(barrier, inc=1, device_id=partner_of(axis, bit), device_id_type=MESH)
    pl.semaphore_wait(barrier, owners - 1 + len(tok_dims))

    def block_copy(source, block, target, sem):
        return pltpu.make_async_remote_copy(
            src_ref=source,
            dst_ref=gath.at[block],
            send_sem=sem,
            recv_sem=block_recv.at[block],
            device_id=at_band(target),
            device_id_type=MESH,
        )

    near = block_copy(low_ref, mine, beside, near_send)
    has_right, has_left = place + 1 < depth, place > 0

    def to_right():
        return block_copy(low_ref, mine, mine + 2, far_send.at[0])

    def to_left():
        return block_copy(low_ref, mine, mine - 2, far_send.at[1])

    @pl.when(has_right)
    def _():
        to_right().start()

    @pl.when(has_left)
    def _():
        to_left().start()

    near.start()
    bits = (2,) * len(tok_dims)
    segments = gen_ref.reshape(bits + (gen_ref.shape[0] * model_dim >> len(bits), gen_ref.shape[2]))
    sums = Sums(
        streams,
        weights_in + [segments, packed],
        outputs,
        own,
        landing,
        send_sem,
        recv_sem,
        own_sem,
        (out_buffer, out_sem),
    )
    heavy = [s for s in range(count) if streams[s]["source"] < bulk]
    slices = [s for s in range(count) if streams[s]["source"] == bulk]
    light = count - 1
    for stream in heavy:
        sums.begin(stream)
    for stream in heavy[:2]:
        sums.fetch(stream)
    gath[mine] = low_ref[...]
    loads[0].wait()
    make_kernels(gen_ref, even_ref, odd_ref, kern_ref, factor)
    loads[1].wait()
    width = 256

    def pair_at(step):
        number = step - 1
        left, right = place, depth - 1 - place
        both = jnp.minimum(left, right)
        turn = jnp.where(lax.rem(number, 2) == 0, -1, 1) * (lax.div(number, 2) + 1)
        rest = jnp.where(right > left, 1, -1) * (number - both + 1)
        offset = jnp.where(number < 2 * both, turn, rest)
        return jnp.where(step == 0, place, place + offset)

    def relay(step):
        block = pair_at(step) * 2 + side
        return block_copy(gath.at[block], block, beside, relay_send.at[step - 1])

    def onward(step, act):
        pair = pair_at(step)
        block = pair * 2 + side
        ahead = jnp.where(pair < place, mine + 2, mine - 2)

        @pl.when(jnp.where(pair < place, place + 1 < depth, place > 0))
        def _():
            act(block_copy(gath.at[block], block, ahead, onward_send.at[step - 1]))

    def pixel_copy(image, step):
        target = lax.rem(mine + step, owners)
        return pltpu.make_async_remote_copy(
            src_ref=pix_ref.at[target, image],
            dst_ref=pixel_land.at[mine, image],
            send_sem=pixel_send.at[image, step - 1],
            recv_sem=pixel_recv.at[image, step - 1],
            device_id=at_band(target),
            device_id_type=MESH,
        )

    def pixel_local(image):
        return pltpu.make_async_copy(
            pix_ref.at[mine, image], pixel_land.at[mine, image], pixel_own.at[image]
        )

    def pair_work(pair):
        for parity in range(2):
            image = pair * 2 + parity
            rows = kern_ref[pair, parity].reshape(owners * share, model_dim)
            turned = lax.dot_general(
                rows, gath[image], (((1,), (1,)), ((), ())), preferred_element_type=jnp.float32
            )
            stage_ref[parity] = turned.astype(stage_ref.dtype).reshape(owners, share, slot)

        @pl.loop(0, model_dim // width)
        def _(part):
            columns = pl.ds(pl.multiple_of(part * width, width), width)
            both = []
            for parity in range(2):
                left = pix_ref[:, pair * 2 + parity].reshape(owners * share, slot)
                both.append(
                    jnp.dot(
                        left,
                        gath[pair * 2 + parity, :, columns],
                        preferred_element_type=jnp.float32,
                    ).reshape(owners * share // 8, 8, width)
                )
            even, odd = both[0], pltpu.roll(both[1], 4, 1)
            top = first_half(even.shape)
            for parity, value in (
                (0, jnp.where(top, even, odd)),
                (1, jnp.where(top, odd, even)),
            ):
                value = value.reshape(owners, share // 8, 8, width).transpose(1, 0, 2, 3)
                value = value.reshape(share // 8, owners * 8, width)
                dk_ref[pair, :, parity, :, columns] = value.astype(dk_ref.dtype)

        for parity in range(2):
            image = pair * 2 + parity
            pix_ref[:, image] = stage_ref[parity]
            pixel_local(image).start()

    def pixel_send_pair(pair):
        for parity in range(2):

            @pl.loop(1, owners)
            def _(step):
                pixel_copy(pair * 2 + parity, step).start()

    done = 0
    for step in range(1, depth):
        block_copy(low_ref, pair_at(step) * 2 + side, beside, near_send).wait_recv()
        onward(step, lambda copy: copy.start())
        relay(step).start()
        until = len(heavy) if step >= depth - 2 else len(heavy) * step // (depth - 2)
        for stream in heavy[done:until]:
            sums.advance(stream, 0)
            if stream + 2 < len(heavy):
                sums.fetch(stream + 2)
        done = max(done, until)
    hyper_dim = feature_ref.shape[1]
    bands = feature_ref.shape[0]
    first_row = lax.broadcasted_iota(jnp.int32, (8, hyper_dim), 0) == 0
    tokens = jnp.concatenate(
        [feature_ref[...], jnp.where(first_row, token_ref[...], 0.0)], axis=0
    )
    wide_width = 512
    attention = tuple(params[number][...] for number in (0, 1, 2, 3, 6))
    segment, segment_back = jax.vjp(
        lambda t, p: hyper_attention(t, p, 1), tokens, attention
    )
    loads[2].wait()
    loads[3].wait()
    hyper_wide(segment, expand_ref, shrink_ref, wide_ref, wide_width)
    norm_back = jax.vjp(
        lambda v, g: layer_norm(v, g, EPS_HYPER), wide_ref[...], params[7][...]
    )[1]

    @pl.loop(0, depth)
    def _(step):
        pair = pair_at(step)

        @pl.when(step == depth - 1)
        def _():
            pixel_send_pair(place)

        block_copy(low_ref, pair * 2 + 1 - side, beside, near_send).wait_recv()
        pair_work(pair)

    waiting = [pair_at(step) for step in range(1, depth)]
    part_ref[...] = jnp.zeros_like(part_ref)

    def dk_rows(duo, parity):
        return dk_ref[:, duo, parity].reshape(depth * owners * 8, model_dim)

    @pl.loop(0, dk_ref.shape[1])
    def _(duo):
        for parity in range(2):
            part_ref[parity] += jnp.dot(
                dk_rows(duo, parity),
                gen_ref[duo * 2 + parity],
                preferred_element_type=jnp.float32,
            ).reshape(depth, owners * 8, -1)

    part_ref[...] = part_ref[...] * factor

    def part_copy(step):
        target = lax.rem(mine + step, owners)
        return pltpu.make_async_remote_copy(
            src_ref=part_ref.at[:, lax.div(target, 2)],
            dst_ref=part_in.at[step - 1],
            send_sem=part_send.at[step - 1],
            recv_sem=part_recv.at[step - 1],
            device_id=at_band(target),
            device_id_type=MESH,
        )

    copies = [part_copy(step) for step in range(1, owners)]
    for copy in copies:
        copy.start()

    @pl.loop(0, dk_ref.shape[1])
    def _(duo):
        for parity in range(2):
            weight = lax.dot_general(
                dk_rows(duo, parity),
                (even_ref, odd_ref)[parity][...],
                (((0,), (0,)), ((), ())),
                preferred_element_type=jnp.float32,
            )
            gen_ref[duo * 2 + parity] = weight.astype(gen_ref.dtype)

    for stream in slices:
        sums.begin(stream)
    early = len(heavy) // 2
    for stream in heavy[:early]:
        sums.advance(stream, 1)
    total = part_ref[:, place]
    for step, copy in enumerate(copies):
        copy.wait_recv()
        total += part_in[step]
    pixel_send_pair(waiting.pop(0))
    rows = total.shape[1]
    half = jnp.where(side == 0, 0.0, 1.0)
    even_part = total[0].reshape(owners, 8, -1)
    odd_part = total[1].reshape(owners, 8, -1)
    low_rows = even_part + pltpu.roll(odd_part, 4, 1)
    low_rows = jnp.where(side == 0, low_rows, pltpu.roll(low_rows, 4, 1))
    low_rows = low_rows.reshape(rows, -1)
    chooser = (
        lax.broadcasted_iota(jnp.int32, (bands, rows), 1)
        == lax.div(lax.broadcasted_iota(jnp.int32, (bands, rows), 0), 4) * 8
        + lax.rem(lax.broadcasted_iota(jnp.int32, (bands, rows), 0), 4)
    ).astype(jnp.float32)
    d_band = precise_dot(chooser, low_rows)
    cotangent = jnp.concatenate(
        [d_band, jnp.where(first_row, bias_grad_ref[...], 0.0)], axis=0
    )
    d_total, second_grad = norm_back(cotangent)
    hyper_wide_back(segment, d_total, expand_ref, shrink_ref, wide_ref, wide_width)
    token_grad, param_grads = segment_back(wide_ref[...])
    small = [param_grads[0], param_grads[1], param_grads[2], param_grads[3]]
    line_row = lax.broadcasted_iota(jnp.int32, gain_lines.shape, 0)
    lines = gain_lines[...]
    for row, value in enumerate((token_grad[bands : bands + 1], param_grads[4], second_grad)):
        lines = jnp.where(line_row == row, value, lines)

    def of_value(value):
        return lambda r, c: value[
            r.start : r.start + r.size, c.start : c.start + c.size
        ]

    def of_ref(ref):
        return lambda r, c: ref[r, c]

    wide = [of_value(value) for value in small]
    wide += [of_ref(expand_ref), of_ref(shrink_ref), of_ref(gen_b_grad), of_value(lines)]
    pack_blocks(blocks, used, packed, wide, stages)
    sums.begin(light)
    sums.advance(light, 0)
    for stream in slices:
        sums.advance(stream, 0)
    for stream in heavy[early:]:
        sums.advance(stream, 1)
    while len(waiting) > 1:
        pixel_send_pair(waiting.pop(0))
    sums.advance(light, len(tok_dims) - 1)
    piece = packed.shape[-2]
    quarter = landing[light][-1].reshape(owners, piece, 128)

    def sum_copy(step):
        target = lax.rem(mine + step, owners)
        return pltpu.make_async_remote_copy(
            src_ref=quarter.at[target],
            dst_ref=sum_in.at[step - 1],
            send_sem=sum_send.at[step - 1],
            recv_sem=sum_recv.at[step - 1],
            device_id=at_band(target),
            device_id_type=MESH,
        )

    own_tok = tuple(own_bit(*d) for d in tok_dims)
    spread_view = whole.reshape((owners,) + bits + (piece, 128))

    def share_copy(block, target, step):
        return pltpu.make_async_remote_copy(
            src_ref=spread_view.at[(block,) + own_tok],
            dst_ref=spread_view.at[(block,) + own_tok],
            send_sem=share_send.at[step - 1],
            recv_sem=share_recv.at[step - 1],
            device_id=at_band(target),
            device_id_type=MESH,
        )

    moves = [sum_copy(step) for step in range(1, owners)]
    for copy in moves:
        copy.start()
    pixel_send_pair(waiting.pop(0))
    for stream in heavy:
        sums.advance(stream, 2)
    light_total = quarter[mine].astype(jnp.float32)
    for step, copy in enumerate(moves):
        copy.wait_recv()
        light_total += sum_in[step].astype(jnp.float32)
    spread_view[(mine,) + own_tok] = light_total.astype(whole.dtype)
    shares = [
        share_copy(mine, lax.rem(mine + step, owners), step) for step in range(1, owners)
    ]
    for copy in shares:
        copy.start()
    for stage in range(3, stages):
        for stream in heavy:
            sums.advance(stream, stage)
    for step in range(1, owners):
        source = lax.rem(mine + owners - step, owners)
        share_copy(source, source, step).wait_recv()
    spread = Spread(dims, streams[light]["order"], whole, gather_send, gather_recv)
    for step in range(len(tok_dims)):
        spread.start()
        if step == 0:
            for stream in slices:
                sums.advance(stream, 1)
        spread.finish()
    for copy in moves + shares:
        copy.wait_send()

    @pl.loop(0, depth * 2)
    def _(image):
        pixel_local(image).wait()

        @pl.loop(1, owners)
        def _(step):
            source = lax.rem(mine + owners - step, owners)
            pltpu.make_async_remote_copy(
                src_ref=pix_ref.at[source, image],
                dst_ref=pixel_land.at[source, image],
                send_sem=pixel_send.at[image, step - 1],
                recv_sem=pixel_recv.at[image, step - 1],
                device_id=at_band(source),
                device_id_type=MESH,
            ).wait()

    for copy in copies + [near] + [relay(step) for step in range(1, depth)]:
        copy.wait_send()
    for step in range(1, depth):
        onward(step, lambda copy: copy.wait_send())

    @pl.when(has_right)
    def _():
        to_right().wait_send()

    @pl.when(has_left)
    def _():
        to_left().wait_send()

    sums.drain()


def tail_call(
    gen_grid,
    pix,
    low_own,
    even,
    odd,
    weights,
    features,
    token,
    bias_grad,
    params,
    gen_b_grad,
    gain_lines,
    factor,
    collective_id,
):
    dims, band_bits, tok_bits = mesh_bits()
    everything = len(dims)
    low = jnp.bfloat16
    owners, images, share, slot = pix.shape
    depth = owners // 2
    pixel_share, model_dim, hyper_dim = gen_grid.shape
    rows = owners * 8
    split, outs, landing, streams = [], [], [], []
    order = halving_order(0, band_bits, tok_bits)
    tallest, base = 0, 0
    for k, weight in enumerate(weights):
        height = weight.shape[0] >> everything
        split.append(weight.reshape((2,) * everything + (height, weight.shape[1])))
        for start, size in row_chunks(height, 2 if height > 32 else 1):
            streams.append(stream_entry(k, 0, start, size, order, dims, True))
            streams[-1]["base"] = base
            landing += landing_shapes(streams[-1], weight.shape[1])
            tallest = max(tallest, size)
        base += height
    outs.append(jax.ShapeDtypeStruct((base, model_dim), jnp.float32))
    bulk = len(weights)
    tok_order = halving_order(2, band_bits, tok_bits)
    height = pixel_share * model_dim >> tok_bits
    outs.append(jax.ShapeDtypeStruct((height, hyper_dim), jnp.float32))
    for start, size in row_chunks(height, 4):
        out_rows = size
        streams.append(stream_entry(bulk, 1, start, size, tok_order, dims, False, factor))
        landing += landing_shapes(streams[-1], hyper_dim)
    wide_shapes = [p.shape for p in params[:6]] + [gen_b_grad.shape, gain_lines.shape]
    blocks, used, piece = wide_plan(wide_shapes, 1 << everything)
    light = stream_entry(bulk + 1, None, 0, piece, tok_order, dims, False)
    light["span"] = dims
    streams.append(light)
    landing += [
        pltpu.VMEM((2,) * (everything - 1 - stage) + (piece, 128), low)
        for stage in range(tok_bits)
    ]
    count = len(streams)
    plan = {"streams": streams, "dims": dims, "bulk": bulk, "blocks": blocks, "used": used}
    space = (2,) * everything + (piece, 128)
    own = pltpu.VMEM((2,) * (everything - 1) + (tallest, model_dim), low)
    dma = pltpu.SemaphoreType.DMA
    return pl.pallas_call(
        functools.partial(tail_kernel, factor, plan),
        out_shape=[jax.ShapeDtypeStruct(pix.shape, low)]
        + outs
        + [jax.ShapeDtypeStruct(space, low)],
        in_specs=[pl.BlockSpec(memory_space=pl.ANY)] * (2 + bulk)
        + [pl.BlockSpec(memory_space=pltpu.VMEM)] * 10
        + [pl.BlockSpec(memory_space=pl.ANY)] * 2
        + [pl.BlockSpec(memory_space=pltpu.VMEM)] * 4,
        out_specs=[pl.BlockSpec(memory_space=pl.ANY)]
        + [
            pl.BlockSpec(memory_space=pltpu.VMEM),
            pl.BlockSpec(memory_space=pl.ANY),
            pl.BlockSpec(memory_space=pltpu.VMEM),
        ],
        scratch_shapes=[
            pltpu.VMEM(gen_grid.shape, low),
            pltpu.VMEM(pix.shape, low),
            pltpu.VMEM((images // 2, 2, owners, share, model_dim), low),
            pltpu.VMEM((images, slot, model_dim), low),
            pltpu.VMEM((2, owners, share, slot), low),
            pltpu.VMEM((2, depth, rows, hyper_dim), jnp.float32),
            pltpu.VMEM((owners - 1, 2, rows, hyper_dim), jnp.float32),
            pltpu.VMEM((features.shape[0] + 8, hyper_dim), jnp.float32),
            pltpu.VMEM(params[4].shape, jnp.float32),
            pltpu.VMEM(params[5].shape, jnp.float32),
            own,
            own,
        ]
        + landing
        + [
            pltpu.VMEM(space, low),
            dma((4,)),
            dma,
            dma((2,)),
            dma((depth - 1,)),
            dma((depth - 1,)),
            dma((owners,)),
            dma((owners - 1,)),
            dma((owners - 1,)),
            dma((count, everything)),
            dma((count, everything)),
            dma((2,)),
            dma((everything,)),
            dma((everything,)),
            dma((images, owners - 1)),
            dma((images, owners - 1)),
            dma((images,)),
            pltpu.VMEM((owners - 1, piece, 128), low),
            dma((owners - 1,)),
            dma((owners - 1,)),
            dma((owners - 1,)),
            dma((owners - 1,)),
            pltpu.VMEM((out_rows, hyper_dim), jnp.float32),
            dma,
        ],
        compiler_params=pltpu.CompilerParams(
            collective_id=collective_id, has_side_effects=True, vmem_limit_bytes=63 << 20
        ),
        cost_estimate=pl.CostEstimate(
            flops=2 * 10**10, bytes_accessed=3 * 10**8, transcendentals=0
        ),
    )(
        gen_grid,
        pix,
        *split,
        low_own,
        even,
        odd,
        features,
        token,
        bias_grad,
        *params,
        gen_b_grad,
        gain_lines,
    )


def layer_norm(values, scaling, epsilon):
    center = values - jnp.mean(values, axis=-1, keepdims=True)
    spread = jnp.mean(center * center, axis=-1, keepdims=True)
    return center * lax.rsqrt(spread + epsilon) * scaling


def block_norm(values, scaling):
    return layer_norm(values, scaling, EPS_BLOCK)


def exact_gelu(values):
    return 0.5 * values * (1.0 + lax.erf(values * math.sqrt(0.5)))


def wave_features(lengths, model_dim):
    middle = model_dim // 2
    angular = 1.0 / 10000.0 ** (jnp.arange(middle, dtype=jnp.float32) / middle)
    phases = (100.0 * lengths)[..., None] * angular
    return jnp.concatenate([jnp.sin(phases), jnp.cos(phases)], axis=-1)


def hyper_layer(features, params):
    (
        bias_token,
        hyper_query,
        hyper_key,
        hyper_value,
        hyper_out,
        hyper_up,
        hyper_down,
        hyper_gain1,
        hyper_gain2,
    ) = params
    images = features.shape[0]
    model_dim = features.shape[-1]
    head_size = model_dim // HHEADS
    tokens = jnp.concatenate(
        [features, jnp.broadcast_to(bias_token, (images, 1, model_dim))], axis=1
    )
    length = tokens.shape[1]
    queries = jnp.einsum("nsc,ce->nse", tokens, hyper_query, precision=PRECISE).reshape(
        images, length, HHEADS, head_size
    )
    keys_all = jnp.einsum("nsc,ce->nse", tokens, hyper_key, precision=PRECISE).reshape(
        images, length, HHEADS, head_size
    )
    values_all = jnp.einsum("nsc,ce->nse", tokens, hyper_value, precision=PRECISE).reshape(
        images, length, HHEADS, head_size
    )
    scores = jnp.einsum("nshe,nthe->nhst", queries, keys_all, precision=PRECISE) / math.sqrt(
        head_size
    )
    weights = jax.nn.softmax(scores, axis=-1)
    blended = jnp.einsum("nhst,nthe->nshe", weights, values_all, precision=PRECISE).reshape(
        images, length, model_dim
    )
    segment_one = layer_norm(
        tokens + jnp.einsum("nse,ef->nsf", blended, hyper_out, precision=PRECISE),
        hyper_gain1,
        EPS_HYPER,
    )
    expanded = jax.nn.gelu(
        jnp.einsum("nse,ef->nsf", segment_one, hyper_up, precision=PRECISE), approximate=False
    )
    second = layer_norm(
        segment_one + jnp.einsum("nsf,fe->nse", expanded, hyper_down, precision=PRECISE),
        hyper_gain2,
        EPS_HYPER,
    )
    return (second[:, :-1, :], second[:, -1, :])


def precise_dot(left, right, contract=(1, 0)):
    return lax.dot_general(
        left,
        right,
        (((contract[0],), (contract[1],)), ((), ())),
        precision=PRECISE,
        preferred_element_type=jnp.float32,
    )


def hyper_attention(tokens, params, images):
    query, key, value, mix, first = params
    rows, hyper_dim = tokens.shape
    bands = (rows - 8 * -(-images // 8)) // images
    head = hyper_dim // HHEADS

    def owner(index):
        return jnp.where(index < images * bands, lax.div(index, bands), index - images * bands)

    same = owner(lax.broadcasted_iota(jnp.int32, (rows, rows), 0)) == owner(
        lax.broadcasted_iota(jnp.int32, (rows, rows), 1)
    )
    lane = lax.div(lax.broadcasted_iota(jnp.int32, (1, hyper_dim), 1), head)
    queries = precise_dot(tokens, query) * (1.0 / math.sqrt(head))
    keys_all = precise_dot(tokens, key)
    values_all = precise_dot(tokens, value)
    blended = None
    for place in range(HHEADS):
        chosen = (lane == place).astype(jnp.float32)
        scores = precise_dot(queries * chosen, keys_all, (1, 1))
        scores = jnp.where(same, scores, -1e30)
        highest = lax.stop_gradient(jnp.max(scores, axis=-1, keepdims=True))
        lifted = jnp.exp(scores - highest)
        weights = lifted / jnp.sum(lifted, axis=-1, keepdims=True)
        part = precise_dot(weights, values_all * chosen)
        blended = part if blended is None else blended + part
    return layer_norm(tokens + precise_dot(blended, mix), first, EPS_HYPER)


def hyper_wide(segment, expand_ref, shrink_ref, total_ref, width):
    total_ref[...] = segment

    @pl.loop(0, expand_ref.shape[1] // width)
    def _(part):
        columns = pl.ds(pl.multiple_of(part * width, width), width)
        wide = precise_dot(segment, expand_ref[:, columns])
        active = 0.5 * wide * (1.0 + lax.erf(wide * math.sqrt(0.5)))
        total_ref[...] += precise_dot(active, shrink_ref[columns, :])


def hyper_wide_back(segment, d_total, expand_ref, shrink_ref, d_segment_ref, width):
    d_segment_ref[...] = d_total

    @pl.loop(0, expand_ref.shape[1] // width)
    def _(part):
        columns = pl.ds(pl.multiple_of(part * width, width), width)
        wide = precise_dot(segment, expand_ref[:, columns])
        bell = 0.5 * (1.0 + lax.erf(wide * math.sqrt(0.5)))
        slope = bell + wide * jnp.exp(-0.5 * wide * wide) * (1.0 / math.sqrt(2.0 * math.pi))
        d_wide = precise_dot(d_total, shrink_ref[columns, :], (1, 1)) * slope
        d_segment_ref[...] += precise_dot(d_wide, expand_ref[:, columns], (1, 1))
        shrink_ref[columns, :] = precise_dot(wide * bell, d_total, (0, 0))
        expand_ref[:, columns] = precise_dot(segment, d_wide, (0, 0))


def contract_rows(left_side, right_side):
    return lax.dot_general(
        left_side, right_side, (((0,), (0,)), ((), ())), preferred_element_type=jnp.float32
    )


def contract_cols(left_side, right_side):
    return lax.dot_general(
        left_side, right_side, (((1,), (1,)), ((), ())), preferred_element_type=jnp.float32
    )


def attention_scores(queries, keys_low, usable):
    head_size = queries.shape[-1]
    scores = jnp.einsum(
        "iqhe,ikhe->ihqk", queries, keys_low, preferred_element_type=jnp.float32
    ) / math.sqrt(head_size)
    return jnp.where(usable[:, None, None, :], scores, -1e30)


def block_forward(embedded, usable, weights_full, ln1_gain, ln2_gain):
    w_qkv_full, w_out_full, w_up_full, w_down_full = weights_full
    images, slot_count, model_dim = embedded.shape
    row_count = images * slot_count
    head_count = model_dim // HD
    flat_rows = embedded.reshape(row_count, model_dim)
    normed_one = block_norm(flat_rows, ln1_gain).astype(jnp.bfloat16)
    qkv_low = jnp.dot(normed_one, w_qkv_full, preferred_element_type=jnp.float32).astype(
        jnp.bfloat16
    )
    sections = qkv_low.reshape(images, slot_count, 3, head_count, HD)
    queries = sections[:, :, 0]
    keys_low = sections[:, :, 1]
    values_low = sections[:, :, 2]
    scores = attention_scores(queries, keys_low, usable)
    highest = jnp.max(scores, axis=-1, keepdims=True)
    lifted = jnp.exp(scores - highest)
    totals = jnp.sum(lifted, axis=-1, keepdims=True)
    attn_probs = (lifted / totals).astype(jnp.bfloat16)
    log_mass = highest + jnp.log(totals)
    attended = (
        jnp.einsum("ihqk,ikhe->iqhe", attn_probs, values_low, preferred_element_type=jnp.float32)
        .astype(jnp.bfloat16)
        .reshape(row_count, model_dim)
    )
    middle = flat_rows + jnp.dot(attended, w_out_full, preferred_element_type=jnp.float32)
    normed_two = block_norm(middle, ln2_gain).astype(jnp.bfloat16)
    hidden = jnp.dot(normed_two, w_up_full, preferred_element_type=jnp.float32)
    active = exact_gelu(hidden).astype(jnp.bfloat16)
    output = middle + jnp.dot(active, w_down_full, preferred_element_type=jnp.float32)
    return (
        flat_rows,
        normed_one,
        queries,
        keys_low,
        values_low,
        log_mass,
        attended,
        middle,
        normed_two,
        hidden,
        active,
        output,
    )


def block_backward(stored, usable, grad_rows, weights_full, ln1_gain, ln2_gain):
    (
        flat_rows,
        normed_one,
        queries,
        keys_low,
        values_low,
        log_mass,
        attended,
        middle,
        normed_two,
        hidden,
        active,
        output,
    ) = stored
    w_qkv_full, w_out_full, w_up_full, w_down_full = weights_full
    images, slot_count, head_count, head_size = queries.shape
    row_count, model_dim = flat_rows.shape
    grad_low = grad_rows.astype(jnp.bfloat16)
    grad_down = contract_rows(active, grad_low)
    d_active = contract_cols(grad_low, w_down_full)
    gelu_back = jax.vjp(exact_gelu, hidden)[1]
    d_hidden = gelu_back(d_active)[0].astype(jnp.bfloat16)
    grad_up_turned = contract_rows(d_hidden, normed_two)
    d_normed_two = contract_cols(d_hidden, w_up_full)
    norm_back_two = jax.vjp(block_norm, middle, ln2_gain)[1]
    d_middle_norm, grad_gain_two = norm_back_two(d_normed_two)
    d_middle = grad_rows + d_middle_norm
    d_middle_low = d_middle.astype(jnp.bfloat16)
    grad_out_turned = contract_rows(d_middle_low, attended)
    d_attended = (
        contract_cols(d_middle_low, w_out_full)
        .astype(jnp.bfloat16)
        .reshape(images, slot_count, head_count, head_size)
    )
    scores = attention_scores(queries, keys_low, usable)
    attn_float = jnp.exp(scores - log_mass)
    attn_probs = attn_float.astype(jnp.bfloat16)
    d_values = jnp.einsum(
        "ihqk,iqhe->ikhe", attn_probs, d_attended, preferred_element_type=jnp.float32
    ).astype(jnp.bfloat16)
    d_probs = jnp.einsum(
        "iqhe,ikhe->ihqk", d_attended, values_low, preferred_element_type=jnp.float32
    )
    d_scores = (
        attn_float * (d_probs - jnp.sum(attn_float * d_probs, axis=-1, keepdims=True))
    ).astype(jnp.bfloat16)
    d_queries = (
        jnp.einsum("ihqk,ikhe->iqhe", d_scores, keys_low, preferred_element_type=jnp.float32)
        / math.sqrt(head_size)
    ).astype(jnp.bfloat16)
    d_keys = (
        jnp.einsum("ihqk,iqhe->ikhe", d_scores, queries, preferred_element_type=jnp.float32)
        / math.sqrt(head_size)
    ).astype(jnp.bfloat16)
    d_qkv = jnp.stack([d_queries, d_keys, d_values], axis=2).reshape(row_count, 3 * model_dim)
    grad_qkv_turned = contract_rows(d_qkv, normed_one)
    d_normed_one = contract_cols(d_qkv, w_qkv_full)
    norm_back_one = jax.vjp(block_norm, flat_rows, ln1_gain)[1]
    d_flat, grad_gain_one = norm_back_one(d_normed_one)
    return (
        d_middle + d_flat,
        (grad_qkv_turned, grad_out_turned, grad_up_turned, grad_down, grad_gain_one, grad_gain_two),
    )


def body(
    pixels,
    wave_table,
    wave_index,
    patch_count,
    d_out,
    gen_w,
    gen_b,
    bias_token,
    hyper_query,
    hyper_key,
    hyper_value,
    hyper_out,
    hyper_up,
    hyper_down,
    hyper_gain1,
    hyper_gain2,
    w_qkv,
    w_out,
    w_up,
    w_down,
    ln1_gain,
    ln2_gain,
):
    group_images, band_share, slot_count, pixel_count = pixels.shape[1:]
    own_images = patch_count.shape[1]
    model_dim = w_out.shape[0]
    hyper_dim = gen_w.shape[1]
    all_bands = wave_index.shape[2]
    owners = lax.axis_size("band")
    slice_pixels = pixel_count // owners
    factor = 1.0 / math.sqrt(all_bands * pixel_count)
    band_place = lax.axis_index("band")
    hyper_params = (
        bias_token,
        hyper_query,
        hyper_key,
        hyper_value,
        hyper_out,
        hyper_up,
        hyper_down,
        hyper_gain1,
        hyper_gain2,
    )
    paired = (
        band_share == 4
        and own_images == 1
        and group_images == owners
        and owners % 2 == 0
        and slice_pixels % 4 == 0
        and model_dim % 256 == 0
    )
    if paired:
        pixel_lined = lax.all_to_all(turn_pixels(pixels[0], owners), "band", 0, 0, tiled=True)
    else:
        pixel_turned = (
            pixels[0]
            .reshape(group_images, band_share, slot_count, owners, slice_pixels)
            .transpose(3, 0, 4, 1, 2)
        )
        pixel_blocks = lax.all_to_all(pixel_turned, "band", 0, 0, tiled=True)
    gen_part = lax.all_gather(gen_w, "tok", axis=0, tiled=True)
    gen_grid = gen_part.reshape(slice_pixels, model_dim, hyper_dim)
    weights_full = (
        lax.all_gather(w_qkv, "tok", axis=1, tiled=True),
        lax.all_gather(w_out, "tok", axis=1, tiled=True),
        lax.all_gather(w_up, "tok", axis=1, tiled=True),
        lax.all_gather(w_down, "tok", axis=0, tiled=True),
    )
    catalog = lax.broadcasted_iota(jnp.int32, (1, 1, wave_table.shape[0]), 2)
    picked = (wave_index[0][:, :, None] == catalog).astype(jnp.float32)
    lengths_all = jnp.sum(picked * wave_table, axis=-1)
    hyper_input = wave_features(lengths_all, hyper_dim)
    band_feats = hyper_layer(hyper_input, hyper_params)[0]
    band_low = band_feats.astype(jnp.bfloat16).reshape(-1, hyper_dim)
    own_input = lax.dynamic_slice_in_dim(hyper_input, band_place * own_images, own_images, 0)

    def run_hyper(params):
        return hyper_layer(own_input, params)

    (_, bias_own), hyper_back = jax.vjp(run_hyper, hyper_params)
    if paired:
        ordered = (
            band_feats.astype(jnp.bfloat16)
            .reshape(group_images // 2, 2, owners, band_share, hyper_dim)
            .transpose(0, 2, 1, 3, 4)
        )
        even_rows = ordered.reshape(-1, hyper_dim)
        odd_rows = ordered[:, :, ::-1].reshape(-1, hyper_dim)
        convolved = embed_parts(
            gen_grid, pixel_lined, even_rows, odd_rows, model_dim, factor, 1
        )
    else:
        pixel_slices = pixel_blocks.transpose(1, 2, 0, 3, 4).reshape(
            group_images, slice_pixels * all_bands, slot_count
        )
        kernels = (
            jnp.einsum("pdc,nc->pnd", gen_grid, band_low, preferred_element_type=jnp.float32) * factor
        ).astype(jnp.bfloat16)
        kernel_grid = kernels.reshape(slice_pixels, group_images, all_bands, model_dim)
        kernel_rows = kernel_grid.transpose(1, 0, 2, 3).reshape(
            group_images, slice_pixels * all_bands, model_dim
        )
        product = jnp.einsum(
            "iks,ikd->isd", pixel_slices, kernel_rows, preferred_element_type=jnp.float32
        )
        convolved = lax.psum_scatter(
            product.reshape(group_images * slot_count, model_dim).astype(jnp.bfloat16),
            "band",
            scatter_dimension=0,
            tiled=True,
        ).astype(jnp.float32)
    bias_rows = jnp.dot(bias_own, gen_b, precision=PRECISE)
    embedded = convolved.reshape(own_images, slot_count, model_dim) + bias_rows[:, None, :]
    usable = lax.broadcasted_iota(jnp.int32, (own_images, slot_count), 1) < patch_count[0][:, None]
    stored = block_forward(embedded, usable, weights_full, ln1_gain, ln2_gain)
    row_mask = usable.reshape(-1, 1)
    layer_out = (
        jnp.where(row_mask, stored[-1], 0.0)
        .astype(jnp.bfloat16)
        .reshape(1, own_images, slot_count, model_dim)
    )
    grad_rows = jnp.where(row_mask, d_out[0].reshape(-1, model_dim).astype(jnp.float32), 0.0)
    d_embed, block_terms = block_backward(
        stored, usable, grad_rows, weights_full, ln1_gain, ln2_gain
    )
    d_embed_low = d_embed.astype(jnp.bfloat16).reshape(own_images, slot_count, model_dim)
    d_bias = jnp.sum(d_embed.reshape(own_images, slot_count, model_dim), axis=1)
    d_bias_feat = jnp.dot(d_bias, gen_b.T, precision=PRECISE)
    grad_gen_b = jnp.dot(bias_own.T, d_bias, precision=PRECISE)
    qkv_turned, out_turned, up_turned, grad_down, gain_one, gain_two = block_terms
    weight_terms = [
        term.astype(jnp.bfloat16) for term in (qkv_turned, out_turned, up_turned, grad_down)
    ]
    gain_rows = model_dim // hyper_dim
    gain_lines = [gain_one.reshape(-1, hyper_dim), gain_two.reshape(-1, hyper_dim)]
    fill = -(3 + 2 * gain_rows) % 16
    gain_lines.append(jnp.zeros((fill, hyper_dim), jnp.float32))
    if paired:
        grad_blocks, weight_sums, grad_gen_w, whole = tail_call(
            gen_grid,
            pixel_lined,
            d_embed_low.reshape(slot_count, model_dim),
            even_rows,
            odd_rows,
            weight_terms,
            own_input[0],
            bias_token[None],
            d_bias_feat,
            [
                hyper_query,
                hyper_key,
                hyper_value,
                hyper_out,
                hyper_up,
                hyper_down,
                hyper_gain1[None],
                hyper_gain2[None],
            ],
            grad_gen_b,
            jnp.concatenate([jnp.zeros((3, hyper_dim), jnp.float32)] + gain_lines),
            factor,
            2,
        )
        devices = owners * lax.axis_size("tok")
        (
            pixel_grad,
            qkv_sum,
            out_sum,
            up_sum,
            down_sum,
            query_sum,
            key_sum,
            value_sum,
            mix_sum,
            expand_sum,
            shrink_sum,
            gen_b_sum,
            line_sum,
        ) = unturn_pixels(
            grad_blocks,
            pixels.shape[1:],
            weight_sums,
            [term.shape[0] // devices for term in weight_terms],
            whole,
            [part.shape for part in hyper_params[1:7]]
            + [gen_b.shape, (3 + 2 * gain_rows + fill, hyper_dim)],
        )
        pixel_grad = pixel_grad[None]
    else:
        d_gathered = lax.all_gather(d_embed_low, "band", axis=0, tiled=True)
        grad_slices = jnp.einsum(
            "ikd,isd->iks", kernel_rows, d_gathered, preferred_element_type=jnp.float32
        ).astype(jnp.bfloat16)
        grad_slices = grad_slices.reshape(
            group_images, slice_pixels, owners, band_share, slot_count
        ).transpose(2, 0, 1, 3, 4)
        d_kernel = jnp.einsum(
            "iks,isd->ikd", pixel_slices, d_gathered, preferred_element_type=jnp.float32
        ).astype(jnp.bfloat16)
        d_kernel = (
            d_kernel.reshape(group_images, slice_pixels, all_bands, model_dim)
            .transpose(1, 0, 2, 3)
            .reshape(slice_pixels, group_images * all_bands, model_dim)
        )
        d_band_part = (
            jnp.einsum("pnd,pdc->nc", d_kernel, gen_grid, preferred_element_type=jnp.float32) * factor
        )
        d_band_own = lax.psum_scatter(d_band_part, "band", scatter_dimension=0, tiled=True)
        gen_part_grad = (
            jnp.einsum("pnd,nc->pdc", d_kernel, band_low, preferred_element_type=jnp.float32) * factor
        )
        gen_low = gen_part_grad.reshape(-1, hyper_dim).astype(jnp.bfloat16)
        grad_slices = lax.all_to_all(grad_slices, "band", 0, 0, tiled=True)
        pixel_grad = grad_slices.transpose(1, 3, 4, 0, 2).reshape(pixels.shape)
        (
            grad_token,
            grad_query,
            grad_key,
            grad_value,
            grad_mix,
            grad_expand,
            grad_shrink,
            grad_first_gain,
            grad_second_gain,
        ) = hyper_back((d_band_own.reshape(own_images, all_bands, hyper_dim), d_bias_feat))[0]
        lines = jnp.concatenate(
            [grad_token[None], grad_first_gain[None], grad_second_gain[None]] + gain_lines
        )
        (
            qkv_sum,
            out_sum,
            up_sum,
            down_sum,
            grad_gen_w,
            query_sum,
            key_sum,
            value_sum,
            mix_sum,
            expand_sum,
            shrink_sum,
            gen_b_sum,
            line_sum,
        ) = reduce_all(
            weight_terms + [gen_low],
            [1, 0, 1, 1, 2],
            [2, 1, 2, 2, 2],
            [
                grad_query,
                grad_key,
                grad_value,
                grad_mix,
                grad_expand,
                grad_shrink,
                grad_gen_b,
                lines,
            ],
            3,
        )
        qkv_sum, out_sum, up_sum = qkv_sum.T, out_sum.T, up_sum.T
    devices = owners * lax.axis_size("tok")
    place = band_place * lax.axis_size("tok") + lax.axis_index("tok")
    gain_share = model_dim // devices

    def own_gain(whole):
        return lax.dynamic_slice_in_dim(whole.reshape(-1), place * gain_share, gain_share, 0)

    return (
        layer_out,
        pixel_grad,
        grad_gen_w,
        gen_b_sum,
        line_sum[0],
        query_sum,
        key_sum,
        value_sum,
        mix_sum,
        expand_sum,
        shrink_sum,
        line_sum[1],
        line_sum[2],
        qkv_sum,
        out_sum,
        up_sum,
        down_sum,
        own_gain(line_sum[3 : 3 + gain_rows]),
        own_gain(line_sum[3 + gain_rows : 3 + 2 * gain_rows]),
    )


def solution(mesh):
    placed = (
        P("tok", None, "band", None, None),
        P(),
        P("tok", None, None),
        P("tok", "band"),
        P("tok", "band", None, None),
        P(("band", "tok"), None),
        P(),
        P(),
        P(),
        P(),
        P(),
        P(),
        P(),
        P(),
        P(),
        P(),
        P(None, "tok"),
        P(None, "tok"),
        P(None, "tok"),
        P("tok", None),
        P(),
        P(),
    )
    return jax.shard_map(
        body,
        mesh=mesh,
        in_specs=placed,
        out_specs=(
            P("tok", "band", None, None),
            P("tok", None, "band", None, None),
            P(("band", "tok"), None),
            P(),
            P(),
            P(),
            P(),
            P(),
            P(),
            P(),
            P(),
            P(),
            P(),
            P(None, ("band", "tok")),
            P(None, ("band", "tok")),
            P(None, ("band", "tok")),
            P(("band", "tok"), None),
            P(("band", "tok")),
            P(("band", "tok")),
        ),
        check_vma=False,
    )
```

```python
import functools
import math

import jax
import jax.numpy as jnp
from jax import lax
from jax.experimental import pallas as pl
from jax.experimental.pallas import tpu as pltpu
from jax.sharding import PartitionSpec as P

HD = 64
HHEADS = 4


EPS_BLOCK = 1e-06
EPS_HYPER = 1e-05
PRECISE = lax.Precision.HIGHEST


MESH = pl.DeviceIdType.MESH


def mesh_bits():
    tok_bits = (lax.axis_size("tok") - 1).bit_length()
    band_bits = (lax.axis_size("band") - 1).bit_length()
    dims = [("band", b) for b in reversed(range(band_bits))]
    dims += [("tok", b) for b in reversed(range(tok_bits))]
    return dims, band_bits, tok_bits


def own_bit(axis, bit):
    return lax.rem(lax.div(lax.axis_index(axis), 1 << bit), 2)


def partner_of(axis, bit):
    place = lax.axis_index(axis)
    mine = own_bit(axis, bit)
    other = place + (1 - 2 * mine) * (1 << bit)
    band, tok = lax.axis_index("band"), lax.axis_index("tok")
    return (other, tok) if axis == "band" else (band, other)


def halving_order(which, band_bits, tok_bits):
    tok = [("tok", b) for b in range(tok_bits)]
    band = [("band", b) for b in range(band_bits)]
    if which == 2:
        return tok
    if which == 0:
        return tok + band
    return tok[:1] + band[:1] + tok[1:] + band[1:]


def pick(remaining, axis_bit, value):
    place = remaining.index(axis_bit)
    return tuple([slice(None)] * place + [value])


def add_block(dest, left, right):
    lead = dest.shape[:-2]

    def one(index):
        spot = []
        for size in reversed(lead):
            spot.insert(0, lax.rem(index, size))
            index = lax.div(index, size)
        spot = tuple(spot)
        dest[spot] = (left(spot) + right(spot)).astype(dest.dtype)

    pl.loop(0, math.prod(lead))(one)


def wide_blocks(shapes, piece):
    blocks, start = [], 0
    for index, (rows, columns) in enumerate(shapes):
        for part in range(columns // 128):
            row = 0
            while row < rows:
                inside = start % piece
                size = min(rows - row, piece - inside)
                blocks.append((index, row, part, start // piece, inside, size))
                row += size
                start += size
    return blocks, start


def segment_spot(segment, count):
    return tuple((segment >> (count - 1 - bit)) & 1 for bit in range(count))


class Sums:
    def __init__(
        self, streams, sources, outputs, own, landing, send_sem, recv_sem, own_sem, buffer=None
    ):
        self.buffer = buffer
        self.streams, self.sources, self.outputs = streams, sources, outputs
        self.own, self.landing = own, landing
        self.send_sem, self.recv_sem, self.own_sem = send_sem, recv_sem, own_sem
        self.flying, self.local = {}, {}

    def part(self, stream, value):
        entry = self.streams[stream]
        spot = pick(entry["span"], entry["order"][0], value)
        spot = spot + (slice(None),) * (len(entry["span"]) - len(spot))
        rows = pl.ds(entry["start"], entry["rows"])
        return self.sources[entry["source"]].at[spot + (rows,)]

    def fetch(self, stream):
        entry = self.streams[stream]
        if entry["fetch"]:
            slot = stream % len(self.own)
            whole = (slice(None),) * (len(entry["span"]) - 1)
            target = self.own[slot].at[whole + (pl.ds(0, entry["rows"]),)]
            copy = pltpu.make_async_copy(
                self.part(stream, own_bit(*entry["order"][0])), target, self.own_sem.at[slot]
            )
            copy.start()
            self.local[stream] = (copy, target)

    def send(self, stream, stage, source):
        axis, bit = self.streams[stream]["order"][stage]
        copy = pltpu.make_async_remote_copy(
            src_ref=source,
            dst_ref=self.landing[stream][stage],
            send_sem=self.send_sem.at[stream, stage],
            recv_sem=self.recv_sem.at[stream, stage],
            device_id=partner_of(axis, bit),
            device_id_type=MESH,
        )
        copy.start()
        self.flying[stream, stage] = copy

    def begin(self, stream):
        first = self.streams[stream]["order"][0]
        self.send(stream, 0, self.part(stream, 1 - own_bit(*first)))

    def advance(self, stream, stage):
        entry = self.streams[stream]
        order, span = entry["order"], entry["span"]
        if stage >= len(order):
            return
        remaining = [d for d in span if d not in order[:stage]]
        axis_bit = order[stage]
        after = [d for d in remaining if d != axis_bit]
        self.flying[stream, stage].wait_recv()
        land = self.landing[stream][stage]
        if stage > 0:
            held = self.landing[stream][stage - 1].at[
                pick(remaining, axis_bit, own_bit(*axis_bit))
            ]
        elif stream in self.local:
            self.local[stream][0].wait()
            held = self.local[stream][1]
        else:
            held = self.part(stream, own_bit(*axis_bit))
        if stage == len(order) - 1 and entry["out"] is not None:
            total = land[...].astype(jnp.float32) + held[...].astype(jnp.float32)
            rows = pl.ds(entry["base"] + entry["start"], entry["rows"])
            if entry["fetch"]:
                self.outputs[entry["out"]][rows] = total * entry["scale"]
            else:
                buffer, sem = self.buffer
                buffer[...] = total * entry["scale"]
                copy = pltpu.make_async_copy(buffer, self.outputs[entry["out"]].at[rows], sem)
                copy.start()
                copy.wait()
        else:
            add_block(
                land,
                lambda spot: land[spot].astype(jnp.float32),
                lambda spot: held[spot].astype(jnp.float32),
            )
            if stage < len(order) - 1:
                following = order[stage + 1]
                self.send(
                    stream, stage + 1, land.at[pick(after, following, 1 - own_bit(*following))]
                )

    def drain(self):
        for copy in self.flying.values():
            copy.wait_send()


class Spread:
    def __init__(self, dims, order, whole, send_sem, recv_sem):
        self.dims, self.order, self.whole = dims, list(reversed(order)), whole
        self.send_sem, self.recv_sem = send_sem, recv_sem
        self.spot = [own_bit(*d) if d in order else slice(None) for d in dims]
        self.copies = []

    def start(self):
        step = len(self.copies)
        view = self.whole.at[tuple(self.spot)]
        copy = pltpu.make_async_remote_copy(
            src_ref=view,
            dst_ref=view,
            send_sem=self.send_sem.at[step],
            recv_sem=self.recv_sem.at[step],
            device_id=partner_of(*self.order[step]),
            device_id_type=MESH,
        )
        copy.start()
        self.copies.append(copy)

    def finish(self):
        self.copies[-1].wait()
        self.spot[self.dims.index(self.order[len(self.copies) - 1])] = slice(None)


def pack_blocks(blocks, used, packed, wide, stages):
    for index, row, part, segment, inside, size in blocks:
        packed[segment_spot(segment, stages) + (pl.ds(inside, size),)] = wide[index](
            pl.ds(row, size), pl.ds(part * 128, 128)
        ).astype(packed.dtype)
    piece = packed.shape[-2]
    while used < piece << stages:
        size = piece - used % piece
        packed[segment_spot(used // piece, stages) + (pl.ds(used % piece, size),)] = jnp.zeros(
            (size, 128), packed.dtype
        )
        used += size


def unpack_blocks(blocks, whole, wide_out, stages):
    for index, row, part, segment, inside, size in blocks:
        wide_out[index][pl.ds(row, size), pl.ds(part * 128, 128)] = whole[
            segment_spot(segment, stages) + (pl.ds(inside, size),)
        ].astype(jnp.float32)


def reduce_kernel(plan, blocks, used, *refs):
    streams, dims = plan["streams"], plan["dims"]
    count, stages = len(streams), len(dims)
    pos = plan["bulk"]
    inputs = list(refs[:pos])
    wide = refs[pos : pos + plan["wide"]]
    pos += plan["wide"]
    outputs = refs[pos : pos + plan["bulk"]]
    pos += plan["bulk"]
    wide_out = refs[pos : pos + plan["wide"]]
    pos += plan["wide"]
    own = refs[pos : pos + count - 1]
    pos += count - 1
    landing = []
    for stream in streams:
        landing.append(refs[pos : pos + len(stream["order"])])
        pos += len(stream["order"])
    packed, whole, send_sem, recv_sem, own_sem, gather_send, gather_recv = refs[pos:]
    barrier = pltpu.get_barrier_semaphore()
    for axis, bit in dims:
        pl.semaphore_signal(barrier, inc=1, device_id=partner_of(axis, bit), device_id_type=MESH)
    pl.semaphore_wait(barrier, stages)
    sums = Sums(
        streams, inputs + [packed], outputs, own, landing, send_sem, recv_sem, own_sem
    )
    for stream in range(count - 1):
        sums.begin(stream)
        sums.fetch(stream)
    pack_blocks(
        blocks, used, packed, [lambda r, c, ref=ref: ref[r, c] for ref in wide], stages
    )
    sums.begin(count - 1)
    for stage in range(stages):
        for stream in range(count):
            sums.advance(stream, stage)
    spread = Spread(dims, streams[-1]["order"], whole, gather_send, gather_recv)
    whole[tuple(spread.spot)] = landing[count - 1][stages - 1][...]
    for _ in range(stages):
        spread.start()
        spread.finish()
    unpack_blocks(blocks, whole, wide_out, stages)
    sums.drain()


def stream_entry(source, out, start, rows, order, dims, fetch, scale=1.0):
    return {
        "source": source,
        "out": out,
        "start": start,
        "rows": rows,
        "order": order,
        "span": [d for d in dims if d in order],
        "fetch": fetch,
        "base": 0,
        "scale": scale,
    }


def landing_shapes(entry, lanes):
    stages = len(entry["order"])
    return [
        pltpu.VMEM((2,) * (stages - 1 - stage) + (entry["rows"], lanes), jnp.bfloat16)
        for stage in range(stages)
    ]


def wide_plan(shapes, devices):
    used = sum(math.prod(shape) for shape in shapes) // 128
    piece = -(-used // (16 * devices)) * 16
    return wide_blocks(shapes, piece)[0], used, piece


def row_chunks(rows, chunks):
    size = -(-rows // chunks // 8) * 8
    return [(start, min(size, rows - start)) for start in range(0, rows, size)]


def reduce_all(arrays, whiches, chunks, wide, collective_id):
    dims, band_bits, tok_bits = mesh_bits()
    low, everything = jnp.bfloat16, len(dims)
    split, outs, own, landing, streams = [], [], [], [], []
    for k, array in enumerate(arrays):
        order = halving_order(whiches[k], band_bits, tok_bits)
        stages = len(order)
        rows, lanes = array.shape[0] >> stages, array.shape[1]
        split.append(array.reshape((2,) * stages + (rows, lanes)))
        outs.append(jax.ShapeDtypeStruct((rows, lanes), jnp.float32))
        for start, size in row_chunks(rows, chunks[k]):
            streams.append(stream_entry(k, k, start, size, order, dims, True))
            own.append(pltpu.VMEM((2,) * (stages - 1) + (size, lanes), low))
            landing += landing_shapes(streams[-1], lanes)
    blocks, used, piece = wide_plan([part.shape for part in wide], 1 << everything)
    order = halving_order(0, band_bits, tok_bits)
    streams.append(stream_entry(len(arrays), None, 0, piece, order, dims, False))
    landing += landing_shapes(streams[-1], 128)
    outs += [jax.ShapeDtypeStruct(part.shape, jnp.float32) for part in wide]
    count = len(streams)
    plan = {"streams": streams, "dims": dims, "bulk": len(arrays), "wide": len(wide)}
    sent = sum(a.size for a in arrays)
    space = (2,) * everything + (piece, 128)
    return pl.pallas_call(
        functools.partial(reduce_kernel, plan, blocks, used),
        out_shape=outs,
        in_specs=[pl.BlockSpec(memory_space=pl.ANY)] * len(arrays)
        + [pl.BlockSpec(memory_space=pltpu.VMEM)] * len(wide),
        out_specs=[pl.BlockSpec(memory_space=pltpu.VMEM)] * len(outs),
        scratch_shapes=own
        + landing
        + [
            pltpu.VMEM(space, low),
            pltpu.VMEM(space, low),
            pltpu.SemaphoreType.DMA((count, everything)),
            pltpu.SemaphoreType.DMA((count, everything)),
            pltpu.SemaphoreType.DMA((count,)),
            pltpu.SemaphoreType.DMA((everything,)),
            pltpu.SemaphoreType.DMA((everything,)),
        ],
        compiler_params=pltpu.CompilerParams(
            collective_id=collective_id, has_side_effects=True, vmem_limit_bytes=60 << 20
        ),
        cost_estimate=pl.CostEstimate(flops=2 * sent, bytes_accessed=40 * sent, transcendentals=0),
    )(*split, *wide)


def turn_kernel(in_ref, out_ref, lines):
    bands = in_ref.shape[1]
    halves, rows = lines.shape[:2]
    for band in range(bands):
        turned = in_ref[0, band].astype(jnp.float32).T
        for half in range(halves):
            lines[half, pl.ds(band, rows // bands, stride=bands), :] = turned[
                :, half * 128 : (half + 1) * 128
            ]
    for half in range(halves):
        out_ref[:, 0, :, pl.ds(half * 128, 128)] = (
            lines[half].astype(out_ref.dtype).reshape(*out_ref.shape[:1], -1, 128)
        )


def turn_pixels(pixels, owners):
    images, bands, slot, pixel_count = pixels.shape
    share = pixel_count // owners * bands
    return pl.pallas_call(
        turn_kernel,
        grid=(images,),
        out_shape=jax.ShapeDtypeStruct((owners, images, share, slot), pixels.dtype),
        in_specs=[pl.BlockSpec((1, bands, slot, pixel_count), lambda i: (i, 0, 0, 0))],
        out_specs=pl.BlockSpec((owners, 1, share, slot), lambda i: (0, i, 0, 0)),
        scratch_shapes=[pltpu.VMEM((slot // 128, pixel_count * bands, 128), jnp.float32)],
        compiler_params=pltpu.CompilerParams(vmem_limit_bytes=60 << 20),
    )(pixels)


def unturn_kernel(blocks, heights, *refs):
    in_ref, weight_ref, whole_ref, out_ref = refs[:4]
    weight_out = refs[4 : 4 + len(heights)]
    wide_out = refs[4 + len(heights) : -1]
    lines = refs[-1]
    bands = out_ref.shape[1]
    halves, rows = lines.shape[:2]
    for half in range(halves):
        lines[half] = (
            in_ref[:, 0, :, pl.ds(half * 128, 128)].astype(jnp.float32).reshape(rows, 128)
        )
    for band in range(bands):
        for half in range(halves):
            piece = lines[half, pl.ds(band, rows // bands, stride=bands), :]
            out_ref[0, band, pl.ds(half * 128, 128), :] = piece.T.astype(out_ref.dtype)

    @pl.when(pl.program_id(0) == 0)
    def _():
        base = 0
        for number, height in enumerate(heights):
            part = weight_ref[pl.ds(base, height), :]
            weight_out[number][...] = part
            base += height
        unpack_blocks(blocks, whole_ref, wide_out, len(whole_ref.shape) - 2)


def unturn_pixels(pixel_blocks, shape, weight_sums, heights, whole, wide_shapes):
    owners, images, share, slot = pixel_blocks.shape
    bands, pixel_count = shape[1], shape[3]
    model_dim = weight_sums.shape[1]
    blocks = wide_plan(wide_shapes, math.prod(whole.shape[:-2]))[0]

    def fixed(array_shape):
        return pl.BlockSpec(array_shape, lambda i: (0,) * len(array_shape))

    given = [(height, model_dim) for height in heights]
    given += wide_shapes
    return pl.pallas_call(
        functools.partial(unturn_kernel, blocks, heights),
        grid=(images,),
        out_shape=[jax.ShapeDtypeStruct(shape, pixel_blocks.dtype)]
        + [jax.ShapeDtypeStruct(s, jnp.float32) for s in given],
        in_specs=[
            pl.BlockSpec((owners, 1, share, slot), lambda i: (0, i, 0, 0)),
            fixed(weight_sums.shape),
            fixed(whole.shape),
        ],
        out_specs=[pl.BlockSpec((1, bands, slot, pixel_count), lambda i: (i, 0, 0, 0))]
        + [fixed(s) for s in given],
        scratch_shapes=[pltpu.VMEM((slot // 128, pixel_count * bands, 128), jnp.float32)],
        compiler_params=pltpu.CompilerParams(vmem_limit_bytes=60 << 20),
    )(pixel_blocks, weight_sums, whole)


def at_band(place):
    return (place, lax.axis_index("tok"))


def pair_place():
    band = lax.axis_index("band")
    return lax.div(band, 2), lax.rem(band, 2)


def first_half(shape):
    return lax.rem(lax.broadcasted_iota(jnp.int32, shape, len(shape) - 2), 8) < 4


def make_kernel(factor, gen_ref, even_ref, odd_ref, kern_ref):
    model_dim = gen_ref.shape[1]
    pairs, _, owners, rows, _ = kern_ref.shape
    width = 256

    @pl.loop(0, model_dim // width)
    def _(part):
        columns = pl.ds(pl.multiple_of(part * width, width), width)
        pieces = []
        for offset in range(4):
            piece = lax.dot_general(
                (even_ref, odd_ref)[offset % 2][...],
                gen_ref[offset, columns, :],
                (((1,), (1,)), ((), ())),
                preferred_element_type=jnp.float32,
            )
            pieces.append((piece * factor).reshape(pairs * owners, 8, width))
        top = first_half(pieces[0].shape)
        even, odd = [], []
        for a, b in ((pieces[0], pieces[1]), (pieces[2], pieces[3])):
            even.append(jnp.where(top, a, b))
            odd.append(pltpu.roll(jnp.where(top, b, a), 4, 1))
        for parity, both in ((0, even), (1, odd)):
            block = jnp.concatenate(both, axis=1).astype(jnp.bfloat16)
            kern_ref[:, parity, :, :, columns] = block.reshape(pairs, owners, rows, width)


def make_kernels(gen_grid, even, odd, images, owners, factor):
    pixel_share, model_dim, hyper_dim = gen_grid.shape
    fixed = pl.BlockSpec(even.shape, lambda q: (0, 0))
    return pl.pallas_call(
        functools.partial(make_kernel, factor),
        grid=(pixel_share // 4,),
        out_shape=jax.ShapeDtypeStruct(
            (images // 2, 2, owners, pixel_share * 4, model_dim), jnp.bfloat16
        ),
        in_specs=[
            pl.BlockSpec((4, model_dim, hyper_dim), lambda q: (q, 0, 0)),
            fixed,
            fixed,
        ],
        out_specs=pl.BlockSpec(
            (images // 2, 2, owners, 16, model_dim), lambda q: (0, 0, 0, q, 0)
        ),
        compiler_params=pltpu.CompilerParams(vmem_limit_bytes=60 << 20),
        cost_estimate=pl.CostEstimate(
            flops=2 * gen_grid.size * even.shape[0],
            bytes_accessed=2 * gen_grid.size + 12 * 10**6,
            transcendentals=0,
        ),
    )(gen_grid, even, odd)


def embed_kernel(
    kern_hbm,
    pix_hbm,
    out_ref,
    pix_ref,
    kern_ref,
    y_out,
    y_in,
    z_out,
    z_in,
    kept,
    load_sem,
    y_send,
    y_recv,
    z_send,
    z_recv,
):
    pairs = kern_ref.shape[0]
    depth, side = pairs, lax.rem(lax.axis_index("band"), 2)
    place = lax.div(lax.axis_index("band"), 2)

    def loads(step, parity, number):
        pair = lax.rem(place + 1 + step, depth)
        image = pair * 2 + parity
        return (
            pltpu.make_async_copy(
                kern_hbm.at[pair, parity], kern_ref.at[pair, parity], load_sem.at[0, number, step]
            ),
            pltpu.make_async_copy(
                pix_hbm.at[:, image], pix_ref.at[:, image], load_sem.at[1, number, step]
            ),
        )

    for number, parity in enumerate((1 - side, side)):

        @pl.loop(0, depth)
        def _(step):
            for load in loads(step, parity, number):
                load.start()

    barrier = pltpu.get_barrier_semaphore()
    pl.semaphore_signal(
        barrier, inc=1, device_id=at_band(place * 2 + 1 - side), device_id_type=MESH
    )
    for step in range(depth - 1):
        target = lax.rem(place + 1 + step, depth)
        pl.semaphore_signal(
            barrier, inc=1, device_id=at_band(target * 2 + side), device_id_type=MESH
        )
    pl.semaphore_wait(barrier, depth)
    width = 256

    def conv(pair, parity, store):
        slot, inner = kern_ref.shape[3], pix_ref.shape[3]
        owners = kern_ref.shape[2]
        left = pix_ref[:, pair * 2 + parity].reshape(owners * slot, inner).T

        @pl.loop(0, kern_ref.shape[4] // width)
        def _(part):
            columns = pl.ds(pl.multiple_of(part * width, width), width)
            right = kern_ref[pair, parity, :, :, columns].reshape(owners * slot, width)
            store(
                columns,
                jnp.dot(left, right, preferred_element_type=jnp.float32),
            )

    def y_copy(step):
        return pltpu.make_async_remote_copy(
            src_ref=y_out.at[step],
            dst_ref=y_in.at[step],
            send_sem=y_send.at[step],
            recv_sem=y_recv.at[step],
            device_id=at_band(place * 2 + 1 - side),
            device_id_type=MESH,
        )

    def z_copy(step):
        return pltpu.make_async_remote_copy(
            src_ref=z_out.at[step],
            dst_ref=z_in.at[step],
            send_sem=z_send.at[step],
            recv_sem=z_recv.at[step],
            device_id=at_band(lax.rem(place + 1 + step, depth) * 2 + side),
            device_id_type=MESH,
        )

    @pl.loop(0, depth)
    def _(step):
        def store(columns, value):
            y_out[step, :, columns] = value.astype(y_out.dtype)

        for load in loads(step, 1 - side, 0):
            load.wait()
        conv(lax.rem(place + 1 + step, depth), 1 - side, store)
        y_copy(step).start()

    @pl.loop(0, depth)
    def _(step):
        def store(columns, value):
            kept[:, columns] = value

        for load in loads(step, side, 1):
            load.wait()
        conv(lax.rem(place + 1 + step, depth), side, store)
        y_copy(step).wait_recv()
        total = kept[...] + y_in[step].astype(jnp.float32)

        @pl.when(step < depth - 1)
        def _():
            z_out[step] = total.astype(z_out.dtype)
            z_copy(step).start()

        @pl.when(step == depth - 1)
        def _():
            out_ref[...] = total

    @pl.loop(0, depth - 1)
    def _(step):
        z_copy(step).wait_recv()
        out_ref[...] += z_in[step].astype(jnp.float32)

    @pl.loop(0, depth)
    def _(step):
        y_copy(step).wait_send()

    @pl.loop(0, depth - 1)
    def _(step):
        z_copy(step).wait_send()


def embed_parts(kernels, pix, model_dim, collective_id):
    owners, images, share, slot = pix.shape
    depth = owners // 2
    low = jnp.bfloat16
    return pl.pallas_call(
        embed_kernel,
        out_shape=jax.ShapeDtypeStruct((slot, model_dim), jnp.float32),
        in_specs=[pl.BlockSpec(memory_space=pl.ANY)] * 2,
        out_specs=pl.BlockSpec(memory_space=pltpu.VMEM),
        scratch_shapes=[
            pltpu.VMEM(pix.shape, low),
            pltpu.VMEM(kernels.shape, low),
            pltpu.VMEM((depth, slot, model_dim), low),
            pltpu.VMEM((depth, slot, model_dim), low),
            pltpu.VMEM((depth - 1, slot, model_dim), low),
            pltpu.VMEM((depth - 1, slot, model_dim), low),
            pltpu.VMEM((slot, model_dim), jnp.float32),
            pltpu.SemaphoreType.DMA((2, 2, depth)),
            pltpu.SemaphoreType.DMA((depth,)),
            pltpu.SemaphoreType.DMA((depth,)),
            pltpu.SemaphoreType.DMA((depth - 1,)),
            pltpu.SemaphoreType.DMA((depth - 1,)),
        ],
        compiler_params=pltpu.CompilerParams(
            collective_id=collective_id, has_side_effects=True, vmem_limit_bytes=60 << 20
        ),
        cost_estimate=pl.CostEstimate(
            flops=10**10, bytes_accessed=12 * 10**7, transcendentals=0
        ),
    )(kernels, pix)


def tail_kernel(factor, plan, *refs):
    streams, dims, blocks, used = plan["streams"], plan["dims"], plan["blocks"], plan["used"]
    count, stages = len(streams), len(dims)
    bulk = plan["bulk"]
    refs = list(refs)

    def take(number):
        taken = refs[:number]
        del refs[:number]
        return taken

    gen_hbm, pix_hbm, kern_hbm = take(3)
    active_hbm, down_hbm, middle_hbm = take(3)
    weights_in = take(bulk)
    low_ref, even_ref, odd_ref, feature_ref, token_ref, bias_grad_ref = take(6)
    params = take(8)
    gen_b_grad, gain_lines = take(2)
    (pixel_land,) = take(1)
    outputs = take(2)
    whole, layer_ref = take(2)
    gen_ref, pix_ref, kern_ref, gath, stage_ref, part_ref, part_in, wide_ref = take(8)
    expand_ref, shrink_ref = take(2)
    own = take(2)
    landing = [take(len(stream["order"])) for stream in streams]
    (packed,) = take(1)
    load_sem, near_send, far_send, relay_send, onward_send = take(5)
    block_recv, part_send, part_recv = take(3)
    send_sem, recv_sem, own_sem, gather_send, gather_recv = take(5)
    pixel_send, pixel_recv, pixel_own = take(3)
    sum_in, sum_send, sum_recv, share_send, share_recv, out_buffer, out_sem = take(7)
    layer_total, layer_sem = take(2)

    depth = kern_ref.shape[0]
    owners, share = kern_ref.shape[2], kern_ref.shape[3]
    slot, model_dim = low_ref.shape
    place, side = pair_place()
    mine = place * 2 + side
    beside = place * 2 + 1 - side
    dk_ref = kern_ref.reshape(depth, gen_ref.shape[0] // 2, 2, owners * 8, model_dim)
    tok_dims = [d for d in dims if d[0] == "tok"]
    loads = [
        pltpu.make_async_copy(gen_hbm, gen_ref, load_sem.at[0]),
        pltpu.make_async_copy(pix_hbm, pix_ref, load_sem.at[1]),
        pltpu.make_async_copy(params[4], expand_ref, load_sem.at[2]),
        pltpu.make_async_copy(params[5], shrink_ref, load_sem.at[3]),
        pltpu.make_async_copy(kern_hbm, kern_ref, load_sem.at[4]),
    ]
    for load in loads:
        load.start()
    barrier = pltpu.get_barrier_semaphore()
    for step in range(1, owners):
        pl.semaphore_signal(
            barrier,
            inc=1,
            device_id=at_band(lax.rem(mine + step, owners)),
            device_id_type=MESH,
        )
    for axis, bit in tok_dims:
        pl.semaphore_signal(barrier, inc=1, device_id=partner_of(axis, bit), device_id_type=MESH)
    pl.semaphore_wait(barrier, owners - 1 + len(tok_dims))

    def block_copy(source, block, target, sem):
        return pltpu.make_async_remote_copy(
            src_ref=source,
            dst_ref=gath.at[block],
            send_sem=sem,
            recv_sem=block_recv.at[block],
            device_id=at_band(target),
            device_id_type=MESH,
        )

    near = block_copy(low_ref, mine, beside, near_send)
    has_right, has_left = place + 1 < depth, place > 0

    def to_right():
        return block_copy(low_ref, mine, mine + 2, far_send.at[0])

    def to_left():
        return block_copy(low_ref, mine, mine - 2, far_send.at[1])

    @pl.when(has_right)
    def _():
        to_right().start()

    @pl.when(has_left)
    def _():
        to_left().start()

    near.start()
    bits = (2,) * len(tok_dims)
    segments = gen_ref.reshape(bits + (gen_ref.shape[0] * model_dim >> len(bits), gen_ref.shape[2]))
    sums = Sums(
        streams,
        weights_in + [segments, packed],
        outputs,
        own,
        landing,
        send_sem,
        recv_sem,
        own_sem,
        (out_buffer, out_sem),
    )
    heavy = [s for s in range(count) if streams[s]["source"] < bulk]
    slices = [s for s in range(count) if streams[s]["source"] == bulk]
    light = count - 1
    for stream in heavy:
        sums.begin(stream)
    for stream in heavy[:2]:
        sums.fetch(stream)
    gath[mine] = low_ref[...]
    width = 256

    def pair_at(step):
        number = step - 1
        left, right = place, depth - 1 - place
        both = jnp.minimum(left, right)
        turn = jnp.where(lax.rem(number, 2) == 0, -1, 1) * (lax.div(number, 2) + 1)
        rest = jnp.where(right > left, 1, -1) * (number - both + 1)
        offset = jnp.where(number < 2 * both, turn, rest)
        return jnp.where(step == 0, place, place + offset)

    def relay(step):
        block = pair_at(step) * 2 + side
        return block_copy(gath.at[block], block, beside, relay_send.at[step - 1])

    def onward(step, act):
        pair = pair_at(step)
        block = pair * 2 + side
        ahead = jnp.where(pair < place, mine + 2, mine - 2)

        @pl.when(jnp.where(pair < place, place + 1 < depth, place > 0))
        def _():
            act(block_copy(gath.at[block], block, ahead, onward_send.at[step - 1]))

    def pixel_copy(image, step):
        target = lax.rem(mine + step, owners)
        return pltpu.make_async_remote_copy(
            src_ref=pix_ref.at[target, image],
            dst_ref=pixel_land.at[mine, image],
            send_sem=pixel_send.at[image, step - 1],
            recv_sem=pixel_recv.at[image, step - 1],
            device_id=at_band(target),
            device_id_type=MESH,
        )

    def pixel_local(image):
        return pltpu.make_async_copy(
            pix_ref.at[mine, image], pixel_land.at[mine, image], pixel_own.at[image]
        )

    def pair_work(pair):
        for parity in range(2):
            image = pair * 2 + parity
            rows = kern_ref[pair, parity].reshape(owners * share, model_dim)
            turned = lax.dot_general(
                rows, gath[image], (((1,), (1,)), ((), ())), preferred_element_type=jnp.float32
            )
            stage_ref[parity] = turned.astype(stage_ref.dtype).reshape(owners, share, slot)

        @pl.loop(0, model_dim // width)
        def _(part):
            columns = pl.ds(pl.multiple_of(part * width, width), width)
            both = []
            for parity in range(2):
                left = pix_ref[:, pair * 2 + parity].reshape(owners * share, slot)
                both.append(
                    jnp.dot(
                        left,
                        gath[pair * 2 + parity, :, columns],
                        preferred_element_type=jnp.float32,
                    ).reshape(owners * share // 8, 8, width)
                )
            even, odd = both[0], pltpu.roll(both[1], 4, 1)
            top = first_half(even.shape)
            for parity, value in (
                (0, jnp.where(top, even, odd)),
                (1, jnp.where(top, odd, even)),
            ):
                value = value.reshape(owners, share // 8, 8, width).transpose(1, 0, 2, 3)
                value = value.reshape(share // 8, owners * 8, width)
                dk_ref[pair, :, parity, :, columns] = value.astype(dk_ref.dtype)

        for parity in range(2):
            image = pair * 2 + parity
            pix_ref[:, image] = stage_ref[parity]
            pixel_local(image).start()

    def pixel_send_pair(pair):
        for parity in range(2):

            @pl.loop(1, owners)
            def _(step):
                pixel_copy(pair * 2 + parity, step).start()

    done = 0
    for step in range(1, depth):
        block_copy(low_ref, pair_at(step) * 2 + side, beside, near_send).wait_recv()
        onward(step, lambda copy: copy.start())
        relay(step).start()
        until = len(heavy) if step >= depth - 2 else len(heavy) * step // (depth - 2)
        for stream in heavy[done:until]:
            sums.advance(stream, 0)
            if stream + 2 < len(heavy):
                sums.fetch(stream + 2)
        done = max(done, until)
    hyper_dim = feature_ref.shape[1]
    bands = feature_ref.shape[0]
    first_row = lax.broadcasted_iota(jnp.int32, (8, hyper_dim), 0) == 0
    tokens = jnp.concatenate(
        [feature_ref[...], jnp.where(first_row, token_ref[...], 0.0)], axis=0
    )
    wide_width = 512
    attention = tuple(params[number][...] for number in (0, 1, 2, 3, 6))
    segment, segment_back = jax.vjp(
        lambda t, p: hyper_attention(t, p, 1), tokens, attention
    )
    loads[2].wait()
    loads[3].wait()
    hyper_wide(segment, expand_ref, shrink_ref, wide_ref, wide_width)
    norm_back = jax.vjp(
        lambda v, g: layer_norm(v, g, EPS_HYPER), wide_ref[...], params[7][...]
    )[1]

    loads[1].wait()
    loads[4].wait()

    @pl.loop(0, depth)
    def _(step):
        pair = pair_at(step)

        @pl.when(step == depth - 1)
        def _():
            pixel_send_pair(place)

        block_copy(low_ref, pair * 2 + 1 - side, beside, near_send).wait_recv()
        pair_work(pair)

    waiting = [pair_at(step) for step in range(1, depth)]

    layer_chunks = down_hbm.shape[0] // model_dim
    high = model_dim // slot

    def layer_copies(chunk):
        half = lax.rem(chunk, 2)
        base = half * (high + 1)
        rows = pl.ds(pl.multiple_of(chunk * model_dim, model_dim), model_dim)
        copies = [
            pltpu.make_async_copy(
                active_hbm.at[:, rows], gath.at[base + high], layer_sem.at[0, half]
            ),
            pltpu.make_async_copy(
                down_hbm.at[rows].reshape(high, slot, model_dim),
                gath.at[pl.ds(base, high)],
                layer_sem.at[1, half],
            ),
        ]
        return copies, base

    def layer_output():
        for step in range(1, depth):
            relay(step).wait_send()
            onward(step, lambda copy: copy.wait_send())
        first = pltpu.make_async_copy(middle_hbm, layer_total, layer_sem.at[2, 0])
        first.start()
        for copy in layer_copies(0)[0]:
            copy.start()
        first.wait()

        @pl.loop(0, layer_chunks)
        def _(chunk):
            @pl.when(chunk + 1 < layer_chunks)
            def _():
                for copy in layer_copies(chunk + 1)[0]:
                    copy.start()

            copies, base = layer_copies(chunk)
            for copy in copies:
                copy.wait()
            layer_total[...] += jnp.dot(
                gath[base + high],
                gath[pl.ds(base, high)].reshape(model_dim, model_dim),
                preferred_element_type=jnp.float32,
            )

        layer_ref[...] = layer_total[...].astype(layer_ref.dtype)
    loads[0].wait()
    part_ref[...] = jnp.zeros_like(part_ref)

    def dk_rows(duo, parity):
        return dk_ref[:, duo, parity].reshape(depth * owners * 8, model_dim)

    @pl.loop(0, dk_ref.shape[1])
    def _(duo):
        for parity in range(2):
            part_ref[parity] += jnp.dot(
                dk_rows(duo, parity),
                gen_ref[duo * 2 + parity],
                preferred_element_type=jnp.float32,
            ).reshape(depth, owners * 8, -1)

    part_ref[...] = part_ref[...] * factor

    def part_copy(step):
        target = lax.rem(mine + step, owners)
        return pltpu.make_async_remote_copy(
            src_ref=part_ref.at[:, lax.div(target, 2)],
            dst_ref=part_in.at[step - 1],
            send_sem=part_send.at[step - 1],
            recv_sem=part_recv.at[step - 1],
            device_id=at_band(target),
            device_id_type=MESH,
        )

    copies = [part_copy(step) for step in range(1, owners)]
    for copy in copies:
        copy.start()
    pixel_send_pair(waiting.pop(0))

    @pl.loop(0, dk_ref.shape[1])
    def _(duo):
        for parity in range(2):
            weight = lax.dot_general(
                dk_rows(duo, parity),
                (even_ref, odd_ref)[parity][...],
                (((0,), (0,)), ((), ())),
                preferred_element_type=jnp.float32,
            )
            gen_ref[duo * 2 + parity] = weight.astype(gen_ref.dtype)

    for stream in slices:
        sums.begin(stream)
    early = len(heavy) // 2
    for stream in heavy[:early]:
        sums.advance(stream, 1)
    total = part_ref[:, place]
    for step, copy in enumerate(copies):
        copy.wait_recv()
        total += part_in[step]
    rows = total.shape[1]
    half = jnp.where(side == 0, 0.0, 1.0)
    even_part = total[0].reshape(owners, 8, -1)
    odd_part = total[1].reshape(owners, 8, -1)
    low_rows = even_part + pltpu.roll(odd_part, 4, 1)
    low_rows = jnp.where(side == 0, low_rows, pltpu.roll(low_rows, 4, 1))
    low_rows = low_rows.reshape(rows, -1)
    chooser = (
        lax.broadcasted_iota(jnp.int32, (bands, rows), 1)
        == lax.div(lax.broadcasted_iota(jnp.int32, (bands, rows), 0), 4) * 8
        + lax.rem(lax.broadcasted_iota(jnp.int32, (bands, rows), 0), 4)
    ).astype(jnp.float32)
    d_band = precise_dot(chooser, low_rows)
    cotangent = jnp.concatenate(
        [d_band, jnp.where(first_row, bias_grad_ref[...], 0.0)], axis=0
    )
    d_total, second_grad = norm_back(cotangent)
    hyper_wide_back(segment, d_total, expand_ref, shrink_ref, wide_ref, wide_width)
    token_grad, param_grads = segment_back(wide_ref[...])
    small = [param_grads[0], param_grads[1], param_grads[2], param_grads[3]]
    line_row = lax.broadcasted_iota(jnp.int32, gain_lines.shape, 0)
    lines = gain_lines[...]
    for row, value in enumerate((token_grad[bands : bands + 1], param_grads[4], second_grad)):
        lines = jnp.where(line_row == row, value, lines)

    def of_value(value):
        return lambda r, c: value[
            r.start : r.start + r.size, c.start : c.start + c.size
        ]

    def of_ref(ref):
        return lambda r, c: ref[r, c]

    wide = [of_value(value) for value in small]
    wide += [of_ref(expand_ref), of_ref(shrink_ref), of_ref(gen_b_grad), of_value(lines)]
    pack_blocks(blocks, used, packed, wide, stages)
    sums.begin(light)
    sums.advance(light, 0)
    for stream in slices:
        sums.advance(stream, 0)
    while len(waiting) > 1:
        pixel_send_pair(waiting.pop(0))
    sums.advance(light, len(tok_dims) - 1)
    for stream in heavy[early:]:
        sums.advance(stream, 1)
    sums.advance(light, len(tok_dims))
    piece = packed.shape[-2]
    quarter = landing[light][-1].reshape(depth, piece, 128)

    def sum_copy(step):
        target = lax.rem(place + step, depth)
        return pltpu.make_async_remote_copy(
            src_ref=quarter.at[target],
            dst_ref=sum_in.at[step - 1],
            send_sem=sum_send.at[step - 1],
            recv_sem=sum_recv.at[step - 1],
            device_id=at_band(target * 2 + side),
            device_id_type=MESH,
        )

    own_tok = tuple(own_bit(*d) for d in tok_dims)
    spread_view = whole.reshape((owners,) + bits + (piece, 128))

    def share_copy(block, target, step):
        return pltpu.make_async_remote_copy(
            src_ref=spread_view.at[(block,) + own_tok],
            dst_ref=spread_view.at[(block,) + own_tok],
            send_sem=share_send.at[step - 1],
            recv_sem=share_recv.at[step - 1],
            device_id=at_band(target),
            device_id_type=MESH,
        )

    moves = [sum_copy(step) for step in range(1, depth)]
    for copy in moves:
        copy.start()
    pixel_send_pair(waiting.pop(0))
    for stream in heavy:
        sums.advance(stream, 2)
    light_total = quarter[place].astype(jnp.float32)
    for step, copy in enumerate(moves):
        copy.wait_recv()
        light_total += sum_in[step].astype(jnp.float32)
    spread_view[(mine,) + own_tok] = light_total.astype(whole.dtype)
    shares = [
        share_copy(mine, lax.rem(place + step, depth) * 2 + side, step)
        for step in range(1, depth)
    ]
    for copy in shares:
        copy.start()
    layer_output()
    for stage in range(3, stages):
        for stream in heavy:
            sums.advance(stream, stage)
    for step in range(1, depth):
        source = lax.rem(place + depth - step, depth) * 2 + side
        share_copy(source, source, step).wait_recv()
    spread = Spread(dims, streams[light]["order"], whole, gather_send, gather_recv)
    for step in range(len(tok_dims) + 1):
        spread.start()
        if step == 0:
            for stream in slices:
                sums.advance(stream, 1)
        spread.finish()
    for copy in moves + shares:
        copy.wait_send()

    @pl.loop(0, depth * 2)
    def _(image):
        pixel_local(image).wait()

        @pl.loop(1, owners)
        def _(step):
            source = lax.rem(mine + owners - step, owners)
            pltpu.make_async_remote_copy(
                src_ref=pix_ref.at[source, image],
                dst_ref=pixel_land.at[source, image],
                send_sem=pixel_send.at[image, step - 1],
                recv_sem=pixel_recv.at[image, step - 1],
                device_id=at_band(source),
                device_id_type=MESH,
            ).wait()

    for copy in copies + [near]:
        copy.wait_send()

    @pl.when(has_right)
    def _():
        to_right().wait_send()

    @pl.when(has_left)
    def _():
        to_left().wait_send()

    sums.drain()


def tail_call(
    gen_grid,
    pix,
    kernels,
    layer_parts,
    low_own,
    even,
    odd,
    weights,
    features,
    token,
    bias_grad,
    params,
    gen_b_grad,
    gain_lines,
    factor,
    collective_id,
):
    dims, band_bits, tok_bits = mesh_bits()
    everything = len(dims)
    low = jnp.bfloat16
    owners, images, share, slot = pix.shape
    depth = owners // 2
    pixel_share, model_dim, hyper_dim = gen_grid.shape
    rows = owners * 8
    split, outs, landing, streams = [], [], [], []
    order = halving_order(0, band_bits, tok_bits)
    tallest, base = 0, 0
    for k, weight in enumerate(weights):
        height = weight.shape[0] >> everything
        split.append(weight.reshape((2,) * everything + (height, weight.shape[1])))
        for start, size in row_chunks(height, 3 if height > 32 else 1):
            streams.append(stream_entry(k, 0, start, size, order, dims, True))
            streams[-1]["base"] = base
            landing += landing_shapes(streams[-1], weight.shape[1])
            tallest = max(tallest, size)
        base += height
    outs.append(jax.ShapeDtypeStruct((base, model_dim), jnp.float32))
    bulk = len(weights)
    tok_order = halving_order(2, band_bits, tok_bits)
    height = pixel_share * model_dim >> tok_bits
    outs.append(jax.ShapeDtypeStruct((height, hyper_dim), jnp.float32))
    for start, size in row_chunks(height, 4):
        out_rows = size
        streams.append(stream_entry(bulk, 1, start, size, tok_order, dims, False, factor))
        landing += landing_shapes(streams[-1], hyper_dim)
    wide_shapes = [p.shape for p in params[:6]] + [gen_b_grad.shape, gain_lines.shape]
    blocks, used, piece = wide_plan(wide_shapes, 1 << everything)
    near_order = tok_order + [("band", 0)]
    light = stream_entry(bulk + 1, None, 0, piece, near_order, dims, False)
    light["span"] = dims
    streams.append(light)
    landing += [
        pltpu.VMEM((2,) * (everything - 1 - stage) + (piece, 128), low)
        for stage in range(len(near_order))
    ]
    count = len(streams)
    plan = {"streams": streams, "dims": dims, "bulk": bulk, "blocks": blocks, "used": used}
    space = (2,) * everything + (piece, 128)
    own = pltpu.VMEM((2,) * (everything - 1) + (tallest, model_dim), low)
    dma = pltpu.SemaphoreType.DMA
    return pl.pallas_call(
        functools.partial(tail_kernel, factor, plan),
        out_shape=[jax.ShapeDtypeStruct(pix.shape, low)]
        + outs
        + [jax.ShapeDtypeStruct(space, low), jax.ShapeDtypeStruct((slot, model_dim), low)],
        in_specs=[pl.BlockSpec(memory_space=pl.ANY)] * (6 + bulk)
        + [pl.BlockSpec(memory_space=pltpu.VMEM)] * 10
        + [pl.BlockSpec(memory_space=pl.ANY)] * 2
        + [pl.BlockSpec(memory_space=pltpu.VMEM)] * 4,
        out_specs=[pl.BlockSpec(memory_space=pl.ANY)]
        + [
            pl.BlockSpec(memory_space=pltpu.VMEM),
            pl.BlockSpec(memory_space=pl.ANY),
            pl.BlockSpec(memory_space=pltpu.VMEM),
            pl.BlockSpec(memory_space=pltpu.VMEM),
        ],
        scratch_shapes=[
            pltpu.VMEM(gen_grid.shape, low),
            pltpu.VMEM(pix.shape, low),
            pltpu.VMEM((images // 2, 2, owners, share, model_dim), low),
            pltpu.VMEM((images, slot, model_dim), low),
            pltpu.VMEM((2, owners, share, slot), low),
            pltpu.VMEM((2, depth, rows, hyper_dim), jnp.float32),
            pltpu.VMEM((owners - 1, 2, rows, hyper_dim), jnp.float32),
            pltpu.VMEM((features.shape[0] + 8, hyper_dim), jnp.float32),
            pltpu.VMEM(params[4].shape, jnp.float32),
            pltpu.VMEM(params[5].shape, jnp.float32),
            own,
            own,
        ]
        + landing
        + [
            pltpu.VMEM(space, low),
            dma((5,)),
            dma,
            dma((2,)),
            dma((depth - 1,)),
            dma((depth - 1,)),
            dma((owners,)),
            dma((owners - 1,)),
            dma((owners - 1,)),
            dma((count, everything)),
            dma((count, everything)),
            dma((2,)),
            dma((everything,)),
            dma((everything,)),
            dma((images, owners - 1)),
            dma((images, owners - 1)),
            dma((images,)),
            pltpu.VMEM((depth - 1, piece, 128), low),
            dma((depth - 1,)),
            dma((depth - 1,)),
            dma((depth - 1,)),
            dma((depth - 1,)),
            pltpu.VMEM((out_rows, hyper_dim), jnp.float32),
            dma,
            pltpu.VMEM((slot, model_dim), jnp.float32),
            dma((3, 2)),
        ],
        compiler_params=pltpu.CompilerParams(
            collective_id=collective_id, has_side_effects=True, vmem_limit_bytes=63 << 20
        ),
        cost_estimate=pl.CostEstimate(
            flops=2 * 10**10, bytes_accessed=3 * 10**8, transcendentals=0
        ),
    )(
        gen_grid,
        pix,
        kernels,
        *layer_parts,
        *split,
        low_own,
        even,
        odd,
        features,
        token,
        bias_grad,
        *params,
        gen_b_grad,
        gain_lines,
    )


def layer_norm(values, scaling, epsilon):
    center = values - jnp.mean(values, axis=-1, keepdims=True)
    spread = jnp.mean(center * center, axis=-1, keepdims=True)
    return center * lax.rsqrt(spread + epsilon) * scaling


def block_norm(values, scaling):
    return layer_norm(values, scaling, EPS_BLOCK)


def exact_gelu(values):
    return 0.5 * values * (1.0 + lax.erf(values * math.sqrt(0.5)))


def wave_features(lengths, model_dim):
    middle = model_dim // 2
    angular = 1.0 / 10000.0 ** (jnp.arange(middle, dtype=jnp.float32) / middle)
    phases = (100.0 * lengths)[..., None] * angular
    return jnp.concatenate([jnp.sin(phases), jnp.cos(phases)], axis=-1)


def hyper_layer(features, params):
    (
        bias_token,
        hyper_query,
        hyper_key,
        hyper_value,
        hyper_out,
        hyper_up,
        hyper_down,
        hyper_gain1,
        hyper_gain2,
    ) = params
    images = features.shape[0]
    model_dim = features.shape[-1]
    head_size = model_dim // HHEADS
    tokens = jnp.concatenate(
        [features, jnp.broadcast_to(bias_token, (images, 1, model_dim))], axis=1
    )
    length = tokens.shape[1]
    queries = jnp.einsum("nsc,ce->nse", tokens, hyper_query, precision=PRECISE).reshape(
        images, length, HHEADS, head_size
    )
    keys_all = jnp.einsum("nsc,ce->nse", tokens, hyper_key, precision=PRECISE).reshape(
        images, length, HHEADS, head_size
    )
    values_all = jnp.einsum("nsc,ce->nse", tokens, hyper_value, precision=PRECISE).reshape(
        images, length, HHEADS, head_size
    )
    scores = jnp.einsum("nshe,nthe->nhst", queries, keys_all, precision=PRECISE) / math.sqrt(
        head_size
    )
    weights = jax.nn.softmax(scores, axis=-1)
    blended = jnp.einsum("nhst,nthe->nshe", weights, values_all, precision=PRECISE).reshape(
        images, length, model_dim
    )
    segment_one = layer_norm(
        tokens + jnp.einsum("nse,ef->nsf", blended, hyper_out, precision=PRECISE),
        hyper_gain1,
        EPS_HYPER,
    )
    expanded = jax.nn.gelu(
        jnp.einsum("nse,ef->nsf", segment_one, hyper_up, precision=PRECISE), approximate=False
    )
    second = layer_norm(
        segment_one + jnp.einsum("nsf,fe->nse", expanded, hyper_down, precision=PRECISE),
        hyper_gain2,
        EPS_HYPER,
    )
    return (second[:, :-1, :], second[:, -1, :])


def precise_dot(left, right, contract=(1, 0)):
    return lax.dot_general(
        left,
        right,
        (((contract[0],), (contract[1],)), ((), ())),
        precision=PRECISE,
        preferred_element_type=jnp.float32,
    )


def hyper_attention(tokens, params, images):
    query, key, value, mix, first = params
    rows, hyper_dim = tokens.shape
    bands = (rows - 8 * -(-images // 8)) // images
    head = hyper_dim // HHEADS

    def owner(index):
        return jnp.where(index < images * bands, lax.div(index, bands), index - images * bands)

    same = owner(lax.broadcasted_iota(jnp.int32, (rows, rows), 0)) == owner(
        lax.broadcasted_iota(jnp.int32, (rows, rows), 1)
    )
    lane = lax.div(lax.broadcasted_iota(jnp.int32, (1, hyper_dim), 1), head)
    queries = precise_dot(tokens, query) * (1.0 / math.sqrt(head))
    keys_all = precise_dot(tokens, key)
    values_all = precise_dot(tokens, value)
    blended = None
    for place in range(HHEADS):
        chosen = (lane == place).astype(jnp.float32)
        scores = precise_dot(queries * chosen, keys_all, (1, 1))
        scores = jnp.where(same, scores, -1e30)
        highest = lax.stop_gradient(jnp.max(scores, axis=-1, keepdims=True))
        lifted = jnp.exp(scores - highest)
        weights = lifted / jnp.sum(lifted, axis=-1, keepdims=True)
        part = precise_dot(weights, values_all * chosen)
        blended = part if blended is None else blended + part
    return layer_norm(tokens + precise_dot(blended, mix), first, EPS_HYPER)


def hyper_wide(segment, expand_ref, shrink_ref, total_ref, width):
    total_ref[...] = segment

    @pl.loop(0, expand_ref.shape[1] // width)
    def _(part):
        columns = pl.ds(pl.multiple_of(part * width, width), width)
        wide = precise_dot(segment, expand_ref[:, columns])
        active = 0.5 * wide * (1.0 + lax.erf(wide * math.sqrt(0.5)))
        total_ref[...] += precise_dot(active, shrink_ref[columns, :])


def hyper_wide_back(segment, d_total, expand_ref, shrink_ref, d_segment_ref, width):
    d_segment_ref[...] = d_total

    @pl.loop(0, expand_ref.shape[1] // width)
    def _(part):
        columns = pl.ds(pl.multiple_of(part * width, width), width)
        wide = precise_dot(segment, expand_ref[:, columns])
        bell = 0.5 * (1.0 + lax.erf(wide * math.sqrt(0.5)))
        slope = bell + wide * jnp.exp(-0.5 * wide * wide) * (1.0 / math.sqrt(2.0 * math.pi))
        d_wide = precise_dot(d_total, shrink_ref[columns, :], (1, 1)) * slope
        d_segment_ref[...] += precise_dot(d_wide, expand_ref[:, columns], (1, 1))
        shrink_ref[columns, :] = precise_dot(wide * bell, d_total, (0, 0))
        expand_ref[:, columns] = precise_dot(segment, d_wide, (0, 0))


def contract_rows(left_side, right_side):
    return lax.dot_general(
        left_side, right_side, (((0,), (0,)), ((), ())), preferred_element_type=jnp.float32
    )


def contract_cols(left_side, right_side):
    return lax.dot_general(
        left_side, right_side, (((1,), (1,)), ((), ())), preferred_element_type=jnp.float32
    )


def attention_scores(queries, keys_low, usable):
    head_size = queries.shape[-1]
    scores = jnp.einsum(
        "iqhe,ikhe->ihqk", queries, keys_low, preferred_element_type=jnp.float32
    ) / math.sqrt(head_size)
    return jnp.where(usable[:, None, None, :], scores, -1e30)


def block_forward(embedded, usable, weights_full, ln1_gain, ln2_gain):
    w_qkv_full, w_out_full, w_up_full, w_down_full = weights_full
    images, slot_count, model_dim = embedded.shape
    row_count = images * slot_count
    head_count = model_dim // HD
    flat_rows = embedded.reshape(row_count, model_dim)
    normed_one = block_norm(flat_rows, ln1_gain).astype(jnp.bfloat16)
    qkv_low = jnp.dot(normed_one, w_qkv_full, preferred_element_type=jnp.float32).astype(
        jnp.bfloat16
    )
    sections = qkv_low.reshape(images, slot_count, 3, head_count, HD)
    queries = sections[:, :, 0]
    keys_low = sections[:, :, 1]
    values_low = sections[:, :, 2]
    scores = attention_scores(queries, keys_low, usable)
    highest = jnp.max(scores, axis=-1, keepdims=True)
    lifted = jnp.exp(scores - highest)
    totals = jnp.sum(lifted, axis=-1, keepdims=True)
    attn_probs = (lifted / totals).astype(jnp.bfloat16)
    log_mass = highest + jnp.log(totals)
    attended = (
        jnp.einsum("ihqk,ikhe->iqhe", attn_probs, values_low, preferred_element_type=jnp.float32)
        .astype(jnp.bfloat16)
        .reshape(row_count, model_dim)
    )
    middle = flat_rows + jnp.dot(attended, w_out_full, preferred_element_type=jnp.float32)
    normed_two = block_norm(middle, ln2_gain).astype(jnp.bfloat16)
    hidden = jnp.dot(normed_two, w_up_full, preferred_element_type=jnp.float32)
    active = exact_gelu(hidden).astype(jnp.bfloat16)
    output = middle + jnp.dot(active, w_down_full, preferred_element_type=jnp.float32)
    return (
        flat_rows,
        normed_one,
        queries,
        keys_low,
        values_low,
        log_mass,
        attended,
        middle,
        normed_two,
        hidden,
        active,
        output,
    )


def block_backward(stored, usable, grad_rows, weights_full, ln1_gain, ln2_gain):
    (
        flat_rows,
        normed_one,
        queries,
        keys_low,
        values_low,
        log_mass,
        attended,
        middle,
        normed_two,
        hidden,
        active,
        output,
    ) = stored
    w_qkv_full, w_out_full, w_up_full, w_down_full = weights_full
    images, slot_count, head_count, head_size = queries.shape
    row_count, model_dim = flat_rows.shape
    grad_low = grad_rows.astype(jnp.bfloat16)
    grad_down = contract_rows(active, grad_low)
    d_active = contract_cols(grad_low, w_down_full)
    gelu_back = jax.vjp(exact_gelu, hidden)[1]
    d_hidden = gelu_back(d_active)[0].astype(jnp.bfloat16)
    grad_up_turned = contract_rows(d_hidden, normed_two)
    d_normed_two = contract_cols(d_hidden, w_up_full)
    norm_back_two = jax.vjp(block_norm, middle, ln2_gain)[1]
    d_middle_norm, grad_gain_two = norm_back_two(d_normed_two)
    d_middle = grad_rows + d_middle_norm
    d_middle_low = d_middle.astype(jnp.bfloat16)
    grad_out_turned = contract_rows(d_middle_low, attended)
    d_attended = (
        contract_cols(d_middle_low, w_out_full)
        .astype(jnp.bfloat16)
        .reshape(images, slot_count, head_count, head_size)
    )
    scores = attention_scores(queries, keys_low, usable)
    attn_float = jnp.exp(scores - log_mass)
    attn_probs = attn_float.astype(jnp.bfloat16)
    d_values = jnp.einsum(
        "ihqk,iqhe->ikhe", attn_probs, d_attended, preferred_element_type=jnp.float32
    ).astype(jnp.bfloat16)
    d_probs = jnp.einsum(
        "iqhe,ikhe->ihqk", d_attended, values_low, preferred_element_type=jnp.float32
    )
    d_scores = (
        attn_float * (d_probs - jnp.sum(attn_float * d_probs, axis=-1, keepdims=True))
    ).astype(jnp.bfloat16)
    d_queries = (
        jnp.einsum("ihqk,ikhe->iqhe", d_scores, keys_low, preferred_element_type=jnp.float32)
        / math.sqrt(head_size)
    ).astype(jnp.bfloat16)
    d_keys = (
        jnp.einsum("ihqk,iqhe->ikhe", d_scores, queries, preferred_element_type=jnp.float32)
        / math.sqrt(head_size)
    ).astype(jnp.bfloat16)
    d_qkv = jnp.stack([d_queries, d_keys, d_values], axis=2).reshape(row_count, 3 * model_dim)
    grad_qkv_turned = contract_rows(d_qkv, normed_one)
    d_normed_one = contract_cols(d_qkv, w_qkv_full)
    norm_back_one = jax.vjp(block_norm, flat_rows, ln1_gain)[1]
    d_flat, grad_gain_one = norm_back_one(d_normed_one)
    return (
        d_middle + d_flat,
        (grad_qkv_turned, grad_out_turned, grad_up_turned, grad_down, grad_gain_one, grad_gain_two),
    )


def body(
    pixels,
    wave_table,
    wave_index,
    patch_count,
    d_out,
    gen_w,
    gen_b,
    bias_token,
    hyper_query,
    hyper_key,
    hyper_value,
    hyper_out,
    hyper_up,
    hyper_down,
    hyper_gain1,
    hyper_gain2,
    w_qkv,
    w_out,
    w_up,
    w_down,
    ln1_gain,
    ln2_gain,
):
    group_images, band_share, slot_count, pixel_count = pixels.shape[1:]
    own_images = patch_count.shape[1]
    model_dim = w_out.shape[0]
    hyper_dim = gen_w.shape[1]
    all_bands = wave_index.shape[2]
    owners = lax.axis_size("band")
    slice_pixels = pixel_count // owners
    factor = 1.0 / math.sqrt(all_bands * pixel_count)
    band_place = lax.axis_index("band")
    hyper_params = (
        bias_token,
        hyper_query,
        hyper_key,
        hyper_value,
        hyper_out,
        hyper_up,
        hyper_down,
        hyper_gain1,
        hyper_gain2,
    )
    paired = (
        band_share == 4
        and own_images == 1
        and group_images == owners
        and owners % 2 == 0
        and slice_pixels % 4 == 0
        and model_dim % 256 == 0
        and model_dim // slot_count + 1 == group_images // 2
        and model_dim % slot_count == 0
        and w_down.shape[0] * lax.axis_size("tok") % model_dim == 0
    )
    if paired:
        pixel_lined = lax.all_to_all(turn_pixels(pixels[0], owners), "band", 0, 0, tiled=True)
    else:
        pixel_turned = (
            pixels[0]
            .reshape(group_images, band_share, slot_count, owners, slice_pixels)
            .transpose(3, 0, 4, 1, 2)
        )
        pixel_blocks = lax.all_to_all(pixel_turned, "band", 0, 0, tiled=True)
    gen_part = lax.all_gather(gen_w, "tok", axis=0, tiled=True)
    gen_grid = gen_part.reshape(slice_pixels, model_dim, hyper_dim)
    weights_full = (
        lax.all_gather(w_qkv, "tok", axis=1, tiled=True),
        lax.all_gather(w_out, "tok", axis=1, tiled=True),
        lax.all_gather(w_up, "tok", axis=1, tiled=True),
        lax.all_gather(w_down, "tok", axis=0, tiled=True),
    )
    catalog = lax.broadcasted_iota(jnp.int32, (1, 1, wave_table.shape[0]), 2)
    picked = (wave_index[0][:, :, None] == catalog).astype(jnp.float32)
    lengths_all = jnp.sum(picked * wave_table, axis=-1)
    hyper_input = wave_features(lengths_all, hyper_dim)
    band_feats = hyper_layer(hyper_input, hyper_params)[0]
    band_low = band_feats.astype(jnp.bfloat16).reshape(-1, hyper_dim)
    own_input = lax.dynamic_slice_in_dim(hyper_input, band_place * own_images, own_images, 0)

    def run_hyper(params):
        return hyper_layer(own_input, params)

    (_, bias_own), hyper_back = jax.vjp(run_hyper, hyper_params)
    if paired:
        ordered = (
            band_feats.astype(jnp.bfloat16)
            .reshape(group_images // 2, 2, owners, band_share, hyper_dim)
            .transpose(0, 2, 1, 3, 4)
        )
        even_rows = ordered.reshape(-1, hyper_dim)
        odd_rows = ordered[:, :, ::-1].reshape(-1, hyper_dim)
        kernel_lined = make_kernels(
            gen_grid, even_rows, odd_rows, group_images, owners, factor
        )
        convolved = embed_parts(kernel_lined, pixel_lined, model_dim, 1)
    else:
        pixel_slices = pixel_blocks.transpose(1, 2, 0, 3, 4).reshape(
            group_images, slice_pixels * all_bands, slot_count
        )
        kernels = (
            jnp.einsum("pdc,nc->pnd", gen_grid, band_low, preferred_element_type=jnp.float32) * factor
        ).astype(jnp.bfloat16)
        kernel_grid = kernels.reshape(slice_pixels, group_images, all_bands, model_dim)
        kernel_rows = kernel_grid.transpose(1, 0, 2, 3).reshape(
            group_images, slice_pixels * all_bands, model_dim
        )
        product = jnp.einsum(
            "iks,ikd->isd", pixel_slices, kernel_rows, preferred_element_type=jnp.float32
        )
        convolved = lax.psum_scatter(
            product.reshape(group_images * slot_count, model_dim).astype(jnp.bfloat16),
            "band",
            scatter_dimension=0,
            tiled=True,
        ).astype(jnp.float32)
    bias_rows = jnp.dot(bias_own, gen_b, precision=PRECISE)
    embedded = convolved.reshape(own_images, slot_count, model_dim) + bias_rows[:, None, :]
    usable = lax.broadcasted_iota(jnp.int32, (own_images, slot_count), 1) < patch_count[0][:, None]
    stored = block_forward(embedded, usable, weights_full, ln1_gain, ln2_gain)
    row_mask = usable.reshape(-1, 1)
    layer_out = (
        jnp.where(row_mask, stored[-1], 0.0)
        .astype(jnp.bfloat16)
        .reshape(1, own_images, slot_count, model_dim)
    )
    grad_rows = jnp.where(row_mask, d_out[0].reshape(-1, model_dim).astype(jnp.float32), 0.0)
    d_embed, block_terms = block_backward(
        stored, usable, grad_rows, weights_full, ln1_gain, ln2_gain
    )
    d_embed_low = d_embed.astype(jnp.bfloat16).reshape(own_images, slot_count, model_dim)
    d_bias = jnp.sum(d_embed.reshape(own_images, slot_count, model_dim), axis=1)
    d_bias_feat = jnp.dot(d_bias, gen_b.T, precision=PRECISE)
    grad_gen_b = jnp.dot(bias_own.T, d_bias, precision=PRECISE)
    qkv_turned, out_turned, up_turned, grad_down, gain_one, gain_two = block_terms
    weight_terms = [
        term.astype(jnp.bfloat16) for term in (qkv_turned, out_turned, up_turned, grad_down)
    ]
    gain_rows = model_dim // hyper_dim
    gain_lines = [gain_one.reshape(-1, hyper_dim), gain_two.reshape(-1, hyper_dim)]
    fill = -(3 + 2 * gain_rows) % 16
    gain_lines.append(jnp.zeros((fill, hyper_dim), jnp.float32))
    if paired:
        grad_blocks, weight_sums, grad_gen_w, whole, layer_rows = tail_call(
            gen_grid,
            pixel_lined,
            kernel_lined,
            [stored[10], weights_full[3], stored[7]],
            d_embed_low.reshape(slot_count, model_dim),
            even_rows,
            odd_rows,
            weight_terms,
            own_input[0],
            bias_token[None],
            d_bias_feat,
            [
                hyper_query,
                hyper_key,
                hyper_value,
                hyper_out,
                hyper_up,
                hyper_down,
                hyper_gain1[None],
                hyper_gain2[None],
            ],
            grad_gen_b,
            jnp.concatenate([jnp.zeros((3, hyper_dim), jnp.float32)] + gain_lines),
            factor,
            2,
        )
        devices = owners * lax.axis_size("tok")
        (
            pixel_grad,
            qkv_sum,
            out_sum,
            up_sum,
            down_sum,
            query_sum,
            key_sum,
            value_sum,
            mix_sum,
            expand_sum,
            shrink_sum,
            gen_b_sum,
            line_sum,
        ) = unturn_pixels(
            grad_blocks,
            pixels.shape[1:],
            weight_sums,
            [term.shape[0] // devices for term in weight_terms],
            whole,
            [part.shape for part in hyper_params[1:7]]
            + [gen_b.shape, (3 + 2 * gain_rows + fill, hyper_dim)],
        )
        pixel_grad = pixel_grad[None]
        layer_out = jnp.where(row_mask, layer_rows, jnp.zeros_like(layer_rows)).reshape(
            1, own_images, slot_count, model_dim
        )
    else:
        d_gathered = lax.all_gather(d_embed_low, "band", axis=0, tiled=True)
        grad_slices = jnp.einsum(
            "ikd,isd->iks", kernel_rows, d_gathered, preferred_element_type=jnp.float32
        ).astype(jnp.bfloat16)
        grad_slices = grad_slices.reshape(
            group_images, slice_pixels, owners, band_share, slot_count
        ).transpose(2, 0, 1, 3, 4)
        d_kernel = jnp.einsum(
            "iks,isd->ikd", pixel_slices, d_gathered, preferred_element_type=jnp.float32
        ).astype(jnp.bfloat16)
        d_kernel = (
            d_kernel.reshape(group_images, slice_pixels, all_bands, model_dim)
            .transpose(1, 0, 2, 3)
            .reshape(slice_pixels, group_images * all_bands, model_dim)
        )
        d_band_part = (
            jnp.einsum("pnd,pdc->nc", d_kernel, gen_grid, preferred_element_type=jnp.float32) * factor
        )
        d_band_own = lax.psum_scatter(d_band_part, "band", scatter_dimension=0, tiled=True)
        gen_part_grad = (
            jnp.einsum("pnd,nc->pdc", d_kernel, band_low, preferred_element_type=jnp.float32) * factor
        )
        gen_low = gen_part_grad.reshape(-1, hyper_dim).astype(jnp.bfloat16)
        grad_slices = lax.all_to_all(grad_slices, "band", 0, 0, tiled=True)
        pixel_grad = grad_slices.transpose(1, 3, 4, 0, 2).reshape(pixels.shape)
        (
            grad_token,
            grad_query,
            grad_key,
            grad_value,
            grad_mix,
            grad_expand,
            grad_shrink,
            grad_first_gain,
            grad_second_gain,
        ) = hyper_back((d_band_own.reshape(own_images, all_bands, hyper_dim), d_bias_feat))[0]
        lines = jnp.concatenate(
            [grad_token[None], grad_first_gain[None], grad_second_gain[None]] + gain_lines
        )
        (
            qkv_sum,
            out_sum,
            up_sum,
            down_sum,
            grad_gen_w,
            query_sum,
            key_sum,
            value_sum,
            mix_sum,
            expand_sum,
            shrink_sum,
            gen_b_sum,
            line_sum,
        ) = reduce_all(
            weight_terms + [gen_low],
            [1, 0, 1, 1, 2],
            [2, 1, 2, 2, 2],
            [
                grad_query,
                grad_key,
                grad_value,
                grad_mix,
                grad_expand,
                grad_shrink,
                grad_gen_b,
                lines,
            ],
            3,
        )
    devices = owners * lax.axis_size("tok")
    place = band_place * lax.axis_size("tok") + lax.axis_index("tok")
    gain_share = model_dim // devices

    def own_gain(whole):
        return lax.dynamic_slice_in_dim(whole.reshape(-1), place * gain_share, gain_share, 0)

    return (
        layer_out,
        pixel_grad,
        grad_gen_w,
        gen_b_sum,
        line_sum[0],
        query_sum,
        key_sum,
        value_sum,
        mix_sum,
        expand_sum,
        shrink_sum,
        line_sum[1],
        line_sum[2],
        qkv_sum.T,
        out_sum.T,
        up_sum.T,
        down_sum,
        own_gain(line_sum[3 : 3 + gain_rows]),
        own_gain(line_sum[3 + gain_rows : 3 + 2 * gain_rows]),
    )


def solution(mesh):
    placed = (
        P("tok", None, "band", None, None),
        P(),
        P("tok", None, None),
        P("tok", "band"),
        P("tok", "band", None, None),
        P(("band", "tok"), None),
        P(),
        P(),
        P(),
        P(),
        P(),
        P(),
        P(),
        P(),
        P(),
        P(),
        P(None, "tok"),
        P(None, "tok"),
        P(None, "tok"),
        P("tok", None),
        P(),
        P(),
    )
    return jax.shard_map(
        body,
        mesh=mesh,
        in_specs=placed,
        out_specs=(
            P("tok", "band", None, None),
            P("tok", None, "band", None, None),
            P(("band", "tok"), None),
            P(),
            P(),
            P(),
            P(),
            P(),
            P(),
            P(),
            P(),
            P(),
            P(),
            P(None, ("band", "tok")),
            P(None, ("band", "tok")),
            P(None, ("band", "tok")),
            P(("band", "tok"), None),
            P(("band", "tok")),
            P(("band", "tok")),
        ),
        check_vma=False,
    )
```

```python
import functools
import math

import jax
import jax.numpy as jnp
from jax import lax
from jax.experimental import pallas as pl
from jax.experimental.pallas import tpu as pltpu
from jax.sharding import PartitionSpec as P

HD = 64
HHEADS = 4


EPS_BLOCK = 1e-06
EPS_HYPER = 1e-05
PRECISE = lax.Precision.HIGHEST


MESH = pl.DeviceIdType.MESH


def mesh_bits():
    tok_bits = (lax.axis_size("tok") - 1).bit_length()
    band_bits = (lax.axis_size("band") - 1).bit_length()
    dims = [("band", b) for b in reversed(range(band_bits))]
    dims += [("tok", b) for b in reversed(range(tok_bits))]
    return dims, band_bits, tok_bits


def own_bit(axis, bit):
    return lax.rem(lax.div(lax.axis_index(axis), 1 << bit), 2)


def partner_of(axis, bit):
    place = lax.axis_index(axis)
    mine = own_bit(axis, bit)
    other = place + (1 - 2 * mine) * (1 << bit)
    band, tok = lax.axis_index("band"), lax.axis_index("tok")
    return (other, tok) if axis == "band" else (band, other)


def halving_order(which, band_bits, tok_bits):
    tok = [("tok", b) for b in range(tok_bits)]
    band = [("band", b) for b in range(band_bits)]
    if which == 2:
        return tok
    if which == 0:
        return tok + band
    return tok[:1] + band[:1] + tok[1:] + band[1:]


def pick(remaining, axis_bit, value):
    place = remaining.index(axis_bit)
    return tuple([slice(None)] * place + [value])


def add_block(dest, left, right):
    lead = dest.shape[:-2]

    def one(index):
        spot = []
        for size in reversed(lead):
            spot.insert(0, lax.rem(index, size))
            index = lax.div(index, size)
        spot = tuple(spot)
        dest[spot] = (left(spot) + right(spot)).astype(dest.dtype)

    pl.loop(0, math.prod(lead))(one)


def wide_blocks(shapes, piece):
    blocks, start = [], 0
    for index, (rows, columns) in enumerate(shapes):
        for part in range(columns // 128):
            row = 0
            while row < rows:
                inside = start % piece
                size = min(rows - row, piece - inside)
                blocks.append((index, row, part, start // piece, inside, size))
                row += size
                start += size
    return blocks, start


def segment_spot(segment, count):
    return tuple((segment >> (count - 1 - bit)) & 1 for bit in range(count))


class Sums:
    def __init__(
        self, streams, sources, outputs, own, landing, send_sem, recv_sem, own_sem, buffer=None
    ):
        self.buffer = buffer
        self.streams, self.sources, self.outputs = streams, sources, outputs
        self.own, self.landing = own, landing
        self.send_sem, self.recv_sem, self.own_sem = send_sem, recv_sem, own_sem
        self.flying, self.local = {}, {}

    def part(self, stream, value):
        entry = self.streams[stream]
        spot = pick(entry["span"], entry["order"][0], value)
        spot = spot + (slice(None),) * (len(entry["span"]) - len(spot))
        rows = pl.ds(entry["start"], entry["rows"])
        return self.sources[entry["source"]].at[spot + (rows,)]

    def fetch(self, stream):
        entry = self.streams[stream]
        if entry["fetch"]:
            slot = stream % len(self.own)
            whole = (slice(None),) * (len(entry["span"]) - 1)
            target = self.own[slot].at[whole + (pl.ds(0, entry["rows"]),)]
            copy = pltpu.make_async_copy(
                self.part(stream, own_bit(*entry["order"][0])), target, self.own_sem.at[slot]
            )
            copy.start()
            self.local[stream] = (copy, target)

    def send(self, stream, stage, source):
        axis, bit = self.streams[stream]["order"][stage]
        copy = pltpu.make_async_remote_copy(
            src_ref=source,
            dst_ref=self.landing[stream][stage],
            send_sem=self.send_sem.at[stream, stage],
            recv_sem=self.recv_sem.at[stream, stage],
            device_id=partner_of(axis, bit),
            device_id_type=MESH,
        )
        copy.start()
        self.flying[stream, stage] = copy

    def begin(self, stream):
        first = self.streams[stream]["order"][0]
        self.send(stream, 0, self.part(stream, 1 - own_bit(*first)))

    def advance(self, stream, stage):
        entry = self.streams[stream]
        order, span = entry["order"], entry["span"]
        if stage >= len(order):
            return
        remaining = [d for d in span if d not in order[:stage]]
        axis_bit = order[stage]
        after = [d for d in remaining if d != axis_bit]
        self.flying[stream, stage].wait_recv()
        land = self.landing[stream][stage]
        if stage > 0:
            held = self.landing[stream][stage - 1].at[
                pick(remaining, axis_bit, own_bit(*axis_bit))
            ]
        elif stream in self.local:
            self.local[stream][0].wait()
            held = self.local[stream][1]
        else:
            held = self.part(stream, own_bit(*axis_bit))
        if stage == len(order) - 1 and entry["out"] is not None:
            total = land[...].astype(jnp.float32) + held[...].astype(jnp.float32)
            rows = pl.ds(entry["base"] + entry["start"], entry["rows"])
            if entry["fetch"]:
                self.outputs[entry["out"]][rows] = total * entry["scale"]
            else:
                buffer, sem = self.buffer
                buffer[...] = total * entry["scale"]
                copy = pltpu.make_async_copy(buffer, self.outputs[entry["out"]].at[rows], sem)
                copy.start()
                copy.wait()
        else:
            add_block(
                land,
                lambda spot: land[spot].astype(jnp.float32),
                lambda spot: held[spot].astype(jnp.float32),
            )
            if stage < len(order) - 1:
                following = order[stage + 1]
                self.send(
                    stream, stage + 1, land.at[pick(after, following, 1 - own_bit(*following))]
                )

    def drain(self):
        for copy in self.flying.values():
            copy.wait_send()


class Spread:
    def __init__(self, dims, order, whole, send_sem, recv_sem):
        self.dims, self.order, self.whole = dims, list(reversed(order)), whole
        self.send_sem, self.recv_sem = send_sem, recv_sem
        self.spot = [own_bit(*d) if d in order else slice(None) for d in dims]
        self.copies = []

    def start(self):
        step = len(self.copies)
        view = self.whole.at[tuple(self.spot)]
        copy = pltpu.make_async_remote_copy(
            src_ref=view,
            dst_ref=view,
            send_sem=self.send_sem.at[step],
            recv_sem=self.recv_sem.at[step],
            device_id=partner_of(*self.order[step]),
            device_id_type=MESH,
        )
        copy.start()
        self.copies.append(copy)

    def finish(self):
        self.copies[-1].wait()
        self.spot[self.dims.index(self.order[len(self.copies) - 1])] = slice(None)


def pack_blocks(blocks, used, packed, wide, stages):
    for index, row, part, segment, inside, size in blocks:
        packed[segment_spot(segment, stages) + (pl.ds(inside, size),)] = wide[index](
            pl.ds(row, size), pl.ds(part * 128, 128)
        ).astype(packed.dtype)
    piece = packed.shape[-2]
    while used < piece << stages:
        size = piece - used % piece
        packed[segment_spot(used // piece, stages) + (pl.ds(used % piece, size),)] = jnp.zeros(
            (size, 128), packed.dtype
        )
        used += size


def unpack_blocks(blocks, whole, wide_out, stages):
    for index, row, part, segment, inside, size in blocks:
        wide_out[index][pl.ds(row, size), pl.ds(part * 128, 128)] = whole[
            segment_spot(segment, stages) + (pl.ds(inside, size),)
        ].astype(jnp.float32)


def reduce_kernel(plan, blocks, used, *refs):
    streams, dims = plan["streams"], plan["dims"]
    count, stages = len(streams), len(dims)
    pos = plan["bulk"]
    inputs = list(refs[:pos])
    wide = refs[pos : pos + plan["wide"]]
    pos += plan["wide"]
    outputs = refs[pos : pos + plan["bulk"]]
    pos += plan["bulk"]
    wide_out = refs[pos : pos + plan["wide"]]
    pos += plan["wide"]
    own = refs[pos : pos + count - 1]
    pos += count - 1
    landing = []
    for stream in streams:
        landing.append(refs[pos : pos + len(stream["order"])])
        pos += len(stream["order"])
    packed, whole, send_sem, recv_sem, own_sem, gather_send, gather_recv = refs[pos:]
    barrier = pltpu.get_barrier_semaphore()
    for axis, bit in dims:
        pl.semaphore_signal(barrier, inc=1, device_id=partner_of(axis, bit), device_id_type=MESH)
    pl.semaphore_wait(barrier, stages)
    sums = Sums(
        streams, inputs + [packed], outputs, own, landing, send_sem, recv_sem, own_sem
    )
    for stream in range(count - 1):
        sums.begin(stream)
        sums.fetch(stream)
    pack_blocks(
        blocks, used, packed, [lambda r, c, ref=ref: ref[r, c] for ref in wide], stages
    )
    sums.begin(count - 1)
    for stage in range(stages):
        for stream in range(count):
            sums.advance(stream, stage)
    spread = Spread(dims, streams[-1]["order"], whole, gather_send, gather_recv)
    whole[tuple(spread.spot)] = landing[count - 1][stages - 1][...]
    for _ in range(stages):
        spread.start()
        spread.finish()
    unpack_blocks(blocks, whole, wide_out, stages)
    sums.drain()


def stream_entry(source, out, start, rows, order, dims, fetch, scale=1.0):
    return {
        "source": source,
        "out": out,
        "start": start,
        "rows": rows,
        "order": order,
        "span": [d for d in dims if d in order],
        "fetch": fetch,
        "base": 0,
        "scale": scale,
    }


def landing_shapes(entry, lanes):
    stages = len(entry["order"])
    return [
        pltpu.VMEM((2,) * (stages - 1 - stage) + (entry["rows"], lanes), jnp.bfloat16)
        for stage in range(stages)
    ]


def wide_plan(shapes, devices):
    used = sum(math.prod(shape) for shape in shapes) // 128
    piece = -(-used // (16 * devices)) * 16
    return wide_blocks(shapes, piece)[0], used, piece


def row_chunks(rows, chunks):
    size = -(-rows // chunks // 8) * 8
    return [(start, min(size, rows - start)) for start in range(0, rows, size)]


def reduce_all(arrays, whiches, chunks, wide, collective_id):
    dims, band_bits, tok_bits = mesh_bits()
    low, everything = jnp.bfloat16, len(dims)
    split, outs, own, landing, streams = [], [], [], [], []
    for k, array in enumerate(arrays):
        order = halving_order(whiches[k], band_bits, tok_bits)
        stages = len(order)
        rows, lanes = array.shape[0] >> stages, array.shape[1]
        split.append(array.reshape((2,) * stages + (rows, lanes)))
        outs.append(jax.ShapeDtypeStruct((rows, lanes), jnp.float32))
        for start, size in row_chunks(rows, chunks[k]):
            streams.append(stream_entry(k, k, start, size, order, dims, True))
            own.append(pltpu.VMEM((2,) * (stages - 1) + (size, lanes), low))
            landing += landing_shapes(streams[-1], lanes)
    blocks, used, piece = wide_plan([part.shape for part in wide], 1 << everything)
    order = halving_order(0, band_bits, tok_bits)
    streams.append(stream_entry(len(arrays), None, 0, piece, order, dims, False))
    landing += landing_shapes(streams[-1], 128)
    outs += [jax.ShapeDtypeStruct(part.shape, jnp.float32) for part in wide]
    count = len(streams)
    plan = {"streams": streams, "dims": dims, "bulk": len(arrays), "wide": len(wide)}
    sent = sum(a.size for a in arrays)
    space = (2,) * everything + (piece, 128)
    return pl.pallas_call(
        functools.partial(reduce_kernel, plan, blocks, used),
        out_shape=outs,
        in_specs=[pl.BlockSpec(memory_space=pl.ANY)] * len(arrays)
        + [pl.BlockSpec(memory_space=pltpu.VMEM)] * len(wide),
        out_specs=[pl.BlockSpec(memory_space=pltpu.VMEM)] * len(outs),
        scratch_shapes=own
        + landing
        + [
            pltpu.VMEM(space, low),
            pltpu.VMEM(space, low),
            pltpu.SemaphoreType.DMA((count, everything)),
            pltpu.SemaphoreType.DMA((count, everything)),
            pltpu.SemaphoreType.DMA((count,)),
            pltpu.SemaphoreType.DMA((everything,)),
            pltpu.SemaphoreType.DMA((everything,)),
        ],
        compiler_params=pltpu.CompilerParams(
            collective_id=collective_id, has_side_effects=True, vmem_limit_bytes=60 << 20
        ),
        cost_estimate=pl.CostEstimate(flops=2 * sent, bytes_accessed=40 * sent, transcendentals=0),
    )(*split, *wide)


def turn_kernel(in_ref, out_ref, lines):
    bands = in_ref.shape[1]
    halves, rows = lines.shape[:2]
    for band in range(bands):
        turned = in_ref[0, band].astype(jnp.float32).T
        for half in range(halves):
            lines[half, pl.ds(band, rows // bands, stride=bands), :] = turned[
                :, half * 128 : (half + 1) * 128
            ]
    for half in range(halves):
        out_ref[:, 0, :, pl.ds(half * 128, 128)] = (
            lines[half].astype(out_ref.dtype).reshape(*out_ref.shape[:1], -1, 128)
        )


def turn_pixels(pixels, owners):
    images, bands, slot, pixel_count = pixels.shape
    share = pixel_count // owners * bands
    return pl.pallas_call(
        turn_kernel,
        grid=(images,),
        out_shape=jax.ShapeDtypeStruct((owners, images, share, slot), pixels.dtype),
        in_specs=[pl.BlockSpec((1, bands, slot, pixel_count), lambda i: (i, 0, 0, 0))],
        out_specs=pl.BlockSpec((owners, 1, share, slot), lambda i: (0, i, 0, 0)),
        scratch_shapes=[pltpu.VMEM((slot // 128, pixel_count * bands, 128), jnp.float32)],
        compiler_params=pltpu.CompilerParams(vmem_limit_bytes=60 << 20),
    )(pixels)


def unturn_kernel(blocks, heights, *refs):
    in_ref, weight_ref, whole_ref, out_ref = refs[:4]
    weight_out = refs[4 : 4 + len(heights)]
    wide_out = refs[4 + len(heights) : -1]
    lines = refs[-1]
    bands = out_ref.shape[1]
    halves, rows = lines.shape[:2]
    for half in range(halves):
        lines[half] = (
            in_ref[:, 0, :, pl.ds(half * 128, 128)].astype(jnp.float32).reshape(rows, 128)
        )
    for band in range(bands):
        for half in range(halves):
            piece = lines[half, pl.ds(band, rows // bands, stride=bands), :]
            out_ref[0, band, pl.ds(half * 128, 128), :] = piece.T.astype(out_ref.dtype)

    @pl.when(pl.program_id(0) == 0)
    def _():
        base = 0
        for number, height in enumerate(heights):
            part = weight_ref[pl.ds(base, height), :]
            weight_out[number][...] = part
            base += height
        unpack_blocks(blocks, whole_ref, wide_out, len(whole_ref.shape) - 2)


def unturn_pixels(pixel_blocks, shape, weight_sums, heights, whole, wide_shapes):
    owners, images, share, slot = pixel_blocks.shape
    bands, pixel_count = shape[1], shape[3]
    model_dim = weight_sums.shape[1]
    blocks = wide_plan(wide_shapes, math.prod(whole.shape[:-2]))[0]

    def fixed(array_shape):
        return pl.BlockSpec(array_shape, lambda i: (0,) * len(array_shape))

    given = [(height, model_dim) for height in heights]
    given += wide_shapes
    return pl.pallas_call(
        functools.partial(unturn_kernel, blocks, heights),
        grid=(images,),
        out_shape=[jax.ShapeDtypeStruct(shape, pixel_blocks.dtype)]
        + [jax.ShapeDtypeStruct(s, jnp.float32) for s in given],
        in_specs=[
            pl.BlockSpec((owners, 1, share, slot), lambda i: (0, i, 0, 0)),
            fixed(weight_sums.shape),
            fixed(whole.shape),
        ],
        out_specs=[pl.BlockSpec((1, bands, slot, pixel_count), lambda i: (i, 0, 0, 0))]
        + [fixed(s) for s in given],
        scratch_shapes=[pltpu.VMEM((slot // 128, pixel_count * bands, 128), jnp.float32)],
        compiler_params=pltpu.CompilerParams(vmem_limit_bytes=60 << 20),
    )(pixel_blocks, weight_sums, whole)


def at_band(place):
    return (place, lax.axis_index("tok"))


def pair_place():
    band = lax.axis_index("band")
    return lax.div(band, 2), lax.rem(band, 2)


def first_half(shape):
    return lax.rem(lax.broadcasted_iota(jnp.int32, shape, len(shape) - 2), 8) < 4


def make_kernel(factor, gen_ref, even_ref, odd_ref, kern_ref):
    model_dim = gen_ref.shape[1]
    pairs, _, owners, rows, _ = kern_ref.shape
    width = 256

    @pl.loop(0, model_dim // width)
    def _(part):
        columns = pl.ds(pl.multiple_of(part * width, width), width)
        pieces = []
        for offset in range(4):
            piece = lax.dot_general(
                (even_ref, odd_ref)[offset % 2][...],
                gen_ref[offset, columns, :],
                (((1,), (1,)), ((), ())),
                preferred_element_type=jnp.float32,
            )
            pieces.append((piece * factor).reshape(pairs * owners, 8, width))
        top = first_half(pieces[0].shape)
        even, odd = [], []
        for a, b in ((pieces[0], pieces[1]), (pieces[2], pieces[3])):
            even.append(jnp.where(top, a, b))
            odd.append(pltpu.roll(jnp.where(top, b, a), 4, 1))
        for parity, both in ((0, even), (1, odd)):
            block = jnp.concatenate(both, axis=1).astype(jnp.bfloat16)
            kern_ref[:, parity, :, :, columns] = block.reshape(pairs, owners, rows, width)


def make_kernels(gen_grid, even, odd, images, owners, factor):
    pixel_share, model_dim, hyper_dim = gen_grid.shape
    fixed = pl.BlockSpec(even.shape, lambda q: (0, 0))
    return pl.pallas_call(
        functools.partial(make_kernel, factor),
        grid=(pixel_share // 4,),
        out_shape=jax.ShapeDtypeStruct(
            (images // 2, 2, owners, pixel_share * 4, model_dim), jnp.bfloat16
        ),
        in_specs=[
            pl.BlockSpec((4, model_dim, hyper_dim), lambda q: (q, 0, 0)),
            fixed,
            fixed,
        ],
        out_specs=pl.BlockSpec(
            (images // 2, 2, owners, 16, model_dim), lambda q: (0, 0, 0, q, 0)
        ),
        compiler_params=pltpu.CompilerParams(vmem_limit_bytes=60 << 20),
        cost_estimate=pl.CostEstimate(
            flops=2 * gen_grid.size * even.shape[0],
            bytes_accessed=2 * gen_grid.size + 12 * 10**6,
            transcendentals=0,
        ),
    )(gen_grid, even, odd)


def embed_kernel(
    kern_hbm,
    pix_hbm,
    out_ref,
    pix_ref,
    kern_ref,
    y_out,
    y_in,
    z_out,
    z_in,
    kept,
    load_sem,
    y_send,
    y_recv,
    z_send,
    z_recv,
):
    pairs = kern_ref.shape[0]
    depth, side = pairs, lax.rem(lax.axis_index("band"), 2)
    place = lax.div(lax.axis_index("band"), 2)

    def loads(step, parity, number):
        pair = lax.rem(place + 1 + step, depth)
        image = pair * 2 + parity
        return (
            pltpu.make_async_copy(
                kern_hbm.at[pair, parity], kern_ref.at[pair, parity], load_sem.at[0, number, step]
            ),
            pltpu.make_async_copy(
                pix_hbm.at[:, image], pix_ref.at[:, image], load_sem.at[1, number, step]
            ),
        )

    for number, parity in enumerate((1 - side, side)):

        @pl.loop(0, depth)
        def _(step):
            for load in loads(step, parity, number):
                load.start()

    barrier = pltpu.get_barrier_semaphore()
    pl.semaphore_signal(
        barrier, inc=1, device_id=at_band(place * 2 + 1 - side), device_id_type=MESH
    )
    for step in range(depth - 1):
        target = lax.rem(place + 1 + step, depth)
        pl.semaphore_signal(
            barrier, inc=1, device_id=at_band(target * 2 + side), device_id_type=MESH
        )
    pl.semaphore_wait(barrier, depth)
    width = 256

    def conv(pair, parity, store):
        slot, inner = kern_ref.shape[3], pix_ref.shape[3]
        owners = kern_ref.shape[2]
        left = pix_ref[:, pair * 2 + parity].reshape(owners * slot, inner).T

        @pl.loop(0, kern_ref.shape[4] // width)
        def _(part):
            columns = pl.ds(pl.multiple_of(part * width, width), width)
            right = kern_ref[pair, parity, :, :, columns].reshape(owners * slot, width)
            store(
                part,
                columns,
                jnp.dot(left, right, preferred_element_type=jnp.float32),
            )

    def columns_of(part):
        return pl.ds(pl.multiple_of(part * width, width), width)

    parts = kern_ref.shape[4] // width

    def y_copy(step, part):
        return pltpu.make_async_remote_copy(
            src_ref=y_out.at[step, :, columns_of(part)],
            dst_ref=y_in.at[step, :, columns_of(part)],
            send_sem=y_send.at[step, part],
            recv_sem=y_recv.at[step, part],
            device_id=at_band(place * 2 + 1 - side),
            device_id_type=MESH,
        )

    def z_copy(step, part):
        return pltpu.make_async_remote_copy(
            src_ref=z_out.at[step, :, columns_of(part)],
            dst_ref=z_in.at[step, :, columns_of(part)],
            send_sem=z_send.at[step, part],
            recv_sem=z_recv.at[step, part],
            device_id=at_band(lax.rem(place + 1 + step, depth) * 2 + side),
            device_id_type=MESH,
        )

    @pl.loop(0, depth)
    def _(step):
        def store(part, columns, value):
            y_out[step, :, columns] = value.astype(y_out.dtype)
            y_copy(step, part).start()

        for load in loads(step, 1 - side, 0):
            load.wait()
        conv(lax.rem(place + 1 + step, depth), 1 - side, store)

    @pl.loop(0, depth)
    def _(step):
        def store(part, columns, value):
            kept[:, columns] = value

        for load in loads(step, side, 1):
            load.wait()
        conv(lax.rem(place + 1 + step, depth), side, store)

        @pl.loop(0, parts)
        def _(part):
            columns = columns_of(part)
            y_copy(step, part).wait_recv()
            total = kept[:, columns] + y_in[step, :, columns].astype(jnp.float32)

            @pl.when(step < depth - 1)
            def _():
                z_out[step, :, columns] = total.astype(z_out.dtype)
                z_copy(step, part).start()

            @pl.when(step == depth - 1)
            def _():
                out_ref[:, columns] = total

    @pl.loop(0, depth - 1)
    def _(step):
        @pl.loop(0, parts)
        def _(part):
            columns = columns_of(part)
            z_copy(step, part).wait_recv()
            out_ref[:, columns] += z_in[step, :, columns].astype(jnp.float32)

    @pl.loop(0, parts)
    def _(part):
        @pl.loop(0, depth)
        def _(step):
            y_copy(step, part).wait_send()

        @pl.loop(0, depth - 1)
        def _(step):
            z_copy(step, part).wait_send()


def embed_parts(kernels, pix, model_dim, collective_id):
    owners, images, share, slot = pix.shape
    depth = owners // 2
    low = jnp.bfloat16
    return pl.pallas_call(
        embed_kernel,
        out_shape=jax.ShapeDtypeStruct((slot, model_dim), jnp.float32),
        in_specs=[pl.BlockSpec(memory_space=pl.ANY)] * 2,
        out_specs=pl.BlockSpec(memory_space=pltpu.VMEM),
        scratch_shapes=[
            pltpu.VMEM(pix.shape, low),
            pltpu.VMEM(kernels.shape, low),
            pltpu.VMEM((depth, slot, model_dim), low),
            pltpu.VMEM((depth, slot, model_dim), low),
            pltpu.VMEM((depth - 1, slot, model_dim), low),
            pltpu.VMEM((depth - 1, slot, model_dim), low),
            pltpu.VMEM((slot, model_dim), jnp.float32),
            pltpu.SemaphoreType.DMA((2, 2, depth)),
            pltpu.SemaphoreType.DMA((depth, model_dim // 256)),
            pltpu.SemaphoreType.DMA((depth, model_dim // 256)),
            pltpu.SemaphoreType.DMA((depth - 1, model_dim // 256)),
            pltpu.SemaphoreType.DMA((depth - 1, model_dim // 256)),
        ],
        compiler_params=pltpu.CompilerParams(
            collective_id=collective_id, has_side_effects=True, vmem_limit_bytes=60 << 20
        ),
        cost_estimate=pl.CostEstimate(
            flops=10**10, bytes_accessed=12 * 10**7, transcendentals=0
        ),
    )(kernels, pix)


def tail_kernel(factor, plan, *refs):
    streams, dims, blocks, used = plan["streams"], plan["dims"], plan["blocks"], plan["used"]
    count, stages = len(streams), len(dims)
    bulk = plan["bulk"]
    refs = list(refs)

    def take(number):
        taken = refs[:number]
        del refs[:number]
        return taken

    gen_hbm, pix_hbm, kern_hbm = take(3)
    active_hbm, down_hbm, middle_hbm = take(3)
    weights_in = take(bulk)
    low_ref, even_ref, odd_ref, feature_ref, token_ref, bias_grad_ref = take(6)
    params = take(8)
    gen_b_grad, gain_lines = take(2)
    (pixel_land,) = take(1)
    outputs = take(2)
    whole, layer_ref = take(2)
    gen_ref, pix_ref, kern_ref, gath, stage_ref, part_ref, part_in, wide_ref = take(8)
    expand_ref, shrink_ref = take(2)
    own = take(2)
    landing = [take(len(stream["order"])) for stream in streams]
    (packed,) = take(1)
    load_sem, near_send, far_send, relay_send, onward_send = take(5)
    block_recv, part_send, part_recv = take(3)
    send_sem, recv_sem, own_sem, gather_send, gather_recv = take(5)
    pixel_send, pixel_recv, pixel_own = take(3)
    sum_in, sum_send, sum_recv, share_send, share_recv, out_buffer, out_sem = take(7)
    layer_total, layer_sem = take(2)

    depth = kern_ref.shape[0]
    owners, share = kern_ref.shape[2], kern_ref.shape[3]
    slot, model_dim = low_ref.shape
    place, side = pair_place()
    mine = place * 2 + side
    beside = place * 2 + 1 - side
    dk_ref = kern_ref.reshape(depth, gen_ref.shape[0] // 2, 2, owners * 8, model_dim)
    tok_dims = [d for d in dims if d[0] == "tok"]
    loads = [
        pltpu.make_async_copy(gen_hbm, gen_ref, load_sem.at[0]),
        pltpu.make_async_copy(pix_hbm, pix_ref, load_sem.at[1]),
        pltpu.make_async_copy(params[4], expand_ref, load_sem.at[2]),
        pltpu.make_async_copy(params[5], shrink_ref, load_sem.at[3]),
        pltpu.make_async_copy(kern_hbm, kern_ref, load_sem.at[4]),
    ]
    for load in loads:
        load.start()
    barrier = pltpu.get_barrier_semaphore()
    for step in range(1, owners):
        pl.semaphore_signal(
            barrier,
            inc=1,
            device_id=at_band(lax.rem(mine + step, owners)),
            device_id_type=MESH,
        )
    for axis, bit in tok_dims:
        pl.semaphore_signal(barrier, inc=1, device_id=partner_of(axis, bit), device_id_type=MESH)
    pl.semaphore_wait(barrier, owners - 1 + len(tok_dims))

    def block_copy(source, block, target, sem):
        return pltpu.make_async_remote_copy(
            src_ref=source,
            dst_ref=gath.at[block],
            send_sem=sem,
            recv_sem=block_recv.at[block],
            device_id=at_band(target),
            device_id_type=MESH,
        )

    near = block_copy(low_ref, mine, beside, near_send)
    has_right, has_left = place + 1 < depth, place > 0

    def to_right():
        return block_copy(low_ref, mine, mine + 2, far_send.at[0])

    def to_left():
        return block_copy(low_ref, mine, mine - 2, far_send.at[1])

    @pl.when(has_right)
    def _():
        to_right().start()

    @pl.when(has_left)
    def _():
        to_left().start()

    near.start()
    bits = (2,) * len(tok_dims)
    segments = gen_ref.reshape(bits + (gen_ref.shape[0] * model_dim >> len(bits), gen_ref.shape[2]))
    sums = Sums(
        streams,
        weights_in + [segments, packed],
        outputs,
        own,
        landing,
        send_sem,
        recv_sem,
        own_sem,
        (out_buffer, out_sem),
    )
    heavy = [s for s in range(count) if streams[s]["source"] < bulk]
    slices = [s for s in range(count) if streams[s]["source"] == bulk]
    light = count - 1
    for stream in heavy:
        sums.begin(stream)
    for stream in heavy[:2]:
        sums.fetch(stream)
    gath[mine] = low_ref[...]
    width = 256

    def pair_at(step):
        number = step - 1
        left, right = place, depth - 1 - place
        both = jnp.minimum(left, right)
        turn = jnp.where(lax.rem(number, 2) == 0, -1, 1) * (lax.div(number, 2) + 1)
        rest = jnp.where(right > left, 1, -1) * (number - both + 1)
        offset = jnp.where(number < 2 * both, turn, rest)
        return jnp.where(step == 0, place, place + offset)

    def relay(step):
        block = pair_at(step) * 2 + side
        return block_copy(gath.at[block], block, beside, relay_send.at[step - 1])

    def onward(step, act):
        pair = pair_at(step)
        block = pair * 2 + side
        ahead = jnp.where(pair < place, mine + 2, mine - 2)

        @pl.when(jnp.where(pair < place, place + 1 < depth, place > 0))
        def _():
            act(block_copy(gath.at[block], block, ahead, onward_send.at[step - 1]))

    def pixel_copy(image, step):
        target = lax.rem(mine + step, owners)
        return pltpu.make_async_remote_copy(
            src_ref=pix_ref.at[target, image],
            dst_ref=pixel_land.at[mine, image],
            send_sem=pixel_send.at[image, step - 1],
            recv_sem=pixel_recv.at[image, step - 1],
            device_id=at_band(target),
            device_id_type=MESH,
        )

    def pixel_local(image):
        return pltpu.make_async_copy(
            pix_ref.at[mine, image], pixel_land.at[mine, image], pixel_own.at[image]
        )

    def pair_work(pair):
        for parity in range(2):
            image = pair * 2 + parity
            rows = kern_ref[pair, parity].reshape(owners * share, model_dim)
            turned = lax.dot_general(
                rows, gath[image], (((1,), (1,)), ((), ())), preferred_element_type=jnp.float32
            )
            stage_ref[parity] = turned.astype(stage_ref.dtype).reshape(owners, share, slot)

        @pl.loop(0, model_dim // width)
        def _(part):
            columns = pl.ds(pl.multiple_of(part * width, width), width)
            both = []
            for parity in range(2):
                left = pix_ref[:, pair * 2 + parity].reshape(owners * share, slot)
                both.append(
                    jnp.dot(
                        left,
                        gath[pair * 2 + parity, :, columns],
                        preferred_element_type=jnp.float32,
                    ).reshape(owners * share // 8, 8, width)
                )
            even, odd = both[0], pltpu.roll(both[1], 4, 1)
            top = first_half(even.shape)
            for parity, value in (
                (0, jnp.where(top, even, odd)),
                (1, jnp.where(top, odd, even)),
            ):
                value = value.reshape(owners, share // 8, 8, width).transpose(1, 0, 2, 3)
                value = value.reshape(share // 8, owners * 8, width)
                dk_ref[pair, :, parity, :, columns] = value.astype(dk_ref.dtype)

        for parity in range(2):
            image = pair * 2 + parity
            pix_ref[:, image] = stage_ref[parity]
            pixel_local(image).start()

    def pixel_send_pair(pair):
        for parity in range(2):

            @pl.loop(1, owners)
            def _(step):
                pixel_copy(pair * 2 + parity, step).start()

    done = 0
    for step in range(1, depth):
        block_copy(low_ref, pair_at(step) * 2 + side, beside, near_send).wait_recv()
        onward(step, lambda copy: copy.start())
        relay(step).start()
        until = len(heavy) if step >= depth - 2 else len(heavy) * step // (depth - 2)
        for stream in heavy[done:until]:
            sums.advance(stream, 0)
            if stream + 2 < len(heavy):
                sums.fetch(stream + 2)
        done = max(done, until)
    hyper_dim = feature_ref.shape[1]
    bands = feature_ref.shape[0]
    first_row = lax.broadcasted_iota(jnp.int32, (8, hyper_dim), 0) == 0
    tokens = jnp.concatenate(
        [feature_ref[...], jnp.where(first_row, token_ref[...], 0.0)], axis=0
    )
    wide_width = 512
    attention = tuple(params[number][...] for number in (0, 1, 2, 3, 6))
    segment, segment_back = jax.vjp(
        lambda t, p: hyper_attention(t, p, 1), tokens, attention
    )
    loads[2].wait()
    loads[3].wait()
    hyper_wide(segment, expand_ref, shrink_ref, wide_ref, wide_width)
    norm_back = jax.vjp(
        lambda v, g: layer_norm(v, g, EPS_HYPER), wide_ref[...], params[7][...]
    )[1]

    loads[1].wait()
    loads[4].wait()

    @pl.loop(0, depth)
    def _(step):
        pair = pair_at(step)

        @pl.when(step == depth - 1)
        def _():
            pixel_send_pair(place)

        block_copy(low_ref, pair * 2 + 1 - side, beside, near_send).wait_recv()
        pair_work(pair)

    waiting = [pair_at(step) for step in range(1, depth)]

    layer_chunks = down_hbm.shape[0] // model_dim
    high = model_dim // slot

    def layer_copies(chunk):
        half = lax.rem(chunk, 2)
        base = half * (high + 1)
        rows = pl.ds(pl.multiple_of(chunk * model_dim, model_dim), model_dim)
        copies = [
            pltpu.make_async_copy(
                active_hbm.at[:, rows], gath.at[base + high], layer_sem.at[0, half]
            ),
            pltpu.make_async_copy(
                down_hbm.at[rows].reshape(high, slot, model_dim),
                gath.at[pl.ds(base, high)],
                layer_sem.at[1, half],
            ),
        ]
        return copies, base

    def layer_output():
        for step in range(1, depth):
            relay(step).wait_send()
            onward(step, lambda copy: copy.wait_send())
        first = pltpu.make_async_copy(middle_hbm, layer_total, layer_sem.at[2, 0])
        first.start()
        for copy in layer_copies(0)[0]:
            copy.start()
        first.wait()

        @pl.loop(0, layer_chunks)
        def _(chunk):
            @pl.when(chunk + 1 < layer_chunks)
            def _():
                for copy in layer_copies(chunk + 1)[0]:
                    copy.start()

            copies, base = layer_copies(chunk)
            for copy in copies:
                copy.wait()
            layer_total[...] += jnp.dot(
                gath[base + high],
                gath[pl.ds(base, high)].reshape(model_dim, model_dim),
                preferred_element_type=jnp.float32,
            )

        layer_ref[...] = layer_total[...].astype(layer_ref.dtype)
    loads[0].wait()
    part_ref[...] = jnp.zeros_like(part_ref)

    def dk_rows(duo, parity):
        return dk_ref[:, duo, parity].reshape(depth * owners * 8, model_dim)

    @pl.loop(0, dk_ref.shape[1])
    def _(duo):
        for parity in range(2):
            part_ref[parity] += jnp.dot(
                dk_rows(duo, parity),
                gen_ref[duo * 2 + parity],
                preferred_element_type=jnp.float32,
            ).reshape(depth, owners * 8, -1)

    part_ref[...] = part_ref[...] * factor

    def part_copy(step):
        target = lax.rem(mine + step, owners)
        return pltpu.make_async_remote_copy(
            src_ref=part_ref.at[:, lax.div(target, 2)],
            dst_ref=part_in.at[step - 1],
            send_sem=part_send.at[step - 1],
            recv_sem=part_recv.at[step - 1],
            device_id=at_band(target),
            device_id_type=MESH,
        )

    copies = [part_copy(step) for step in range(1, owners)]
    for copy in copies:
        copy.start()
    pixel_send_pair(waiting.pop(0))

    @pl.loop(0, dk_ref.shape[1])
    def _(duo):
        for parity in range(2):
            weight = lax.dot_general(
                dk_rows(duo, parity),
                (even_ref, odd_ref)[parity][...],
                (((0,), (0,)), ((), ())),
                preferred_element_type=jnp.float32,
            )
            gen_ref[duo * 2 + parity] = weight.astype(gen_ref.dtype)

    for stream in slices:
        sums.begin(stream)
    early = len(heavy) // 2
    for stream in heavy[:early]:
        sums.advance(stream, 1)
    total = part_ref[:, place]
    for step, copy in enumerate(copies):
        copy.wait_recv()
        total += part_in[step]
    rows = total.shape[1]
    half = jnp.where(side == 0, 0.0, 1.0)
    even_part = total[0].reshape(owners, 8, -1)
    odd_part = total[1].reshape(owners, 8, -1)
    low_rows = even_part + pltpu.roll(odd_part, 4, 1)
    low_rows = jnp.where(side == 0, low_rows, pltpu.roll(low_rows, 4, 1))
    low_rows = low_rows.reshape(rows, -1)
    chooser = (
        lax.broadcasted_iota(jnp.int32, (bands, rows), 1)
        == lax.div(lax.broadcasted_iota(jnp.int32, (bands, rows), 0), 4) * 8
        + lax.rem(lax.broadcasted_iota(jnp.int32, (bands, rows), 0), 4)
    ).astype(jnp.float32)
    d_band = precise_dot(chooser, low_rows)
    cotangent = jnp.concatenate(
        [d_band, jnp.where(first_row, bias_grad_ref[...], 0.0)], axis=0
    )
    d_total, second_grad = norm_back(cotangent)
    hyper_wide_back(segment, d_total, expand_ref, shrink_ref, wide_ref, wide_width)
    token_grad, param_grads = segment_back(wide_ref[...])
    small = [param_grads[0], param_grads[1], param_grads[2], param_grads[3]]
    line_row = lax.broadcasted_iota(jnp.int32, gain_lines.shape, 0)
    lines = gain_lines[...]
    for row, value in enumerate((token_grad[bands : bands + 1], param_grads[4], second_grad)):
        lines = jnp.where(line_row == row, value, lines)

    def of_value(value):
        return lambda r, c: value[
            r.start : r.start + r.size, c.start : c.start + c.size
        ]

    def of_ref(ref):
        return lambda r, c: ref[r, c]

    wide = [of_value(value) for value in small]
    wide += [of_ref(expand_ref), of_ref(shrink_ref), of_ref(gen_b_grad), of_value(lines)]
    pack_blocks(blocks, used, packed, wide, stages)
    sums.begin(light)
    sums.advance(light, 0)
    for stream in slices:
        sums.advance(stream, 0)
    while len(waiting) > 1:
        pixel_send_pair(waiting.pop(0))
    sums.advance(light, len(tok_dims) - 1)
    for stream in heavy[early:]:
        sums.advance(stream, 1)
    sums.advance(light, len(tok_dims))
    piece = packed.shape[-2]
    quarter = landing[light][-1].reshape(depth, piece, 128)

    def sum_copy(step):
        target = lax.rem(place + step, depth)
        return pltpu.make_async_remote_copy(
            src_ref=quarter.at[target],
            dst_ref=sum_in.at[step - 1],
            send_sem=sum_send.at[step - 1],
            recv_sem=sum_recv.at[step - 1],
            device_id=at_band(target * 2 + side),
            device_id_type=MESH,
        )

    own_tok = tuple(own_bit(*d) for d in tok_dims)
    spread_view = whole.reshape((owners,) + bits + (piece, 128))

    def share_copy(block, target, step):
        return pltpu.make_async_remote_copy(
            src_ref=spread_view.at[(block,) + own_tok],
            dst_ref=spread_view.at[(block,) + own_tok],
            send_sem=share_send.at[step - 1],
            recv_sem=share_recv.at[step - 1],
            device_id=at_band(target),
            device_id_type=MESH,
        )

    moves = [sum_copy(step) for step in range(1, depth)]
    for copy in moves:
        copy.start()
    pixel_send_pair(waiting.pop(0))
    for stream in heavy:
        sums.advance(stream, 2)
    light_total = quarter[place].astype(jnp.float32)
    for step, copy in enumerate(moves):
        copy.wait_recv()
        light_total += sum_in[step].astype(jnp.float32)
    spread_view[(mine,) + own_tok] = light_total.astype(whole.dtype)
    shares = [
        share_copy(mine, lax.rem(place + step, depth) * 2 + side, step)
        for step in range(1, depth)
    ]
    for copy in shares:
        copy.start()
    layer_output()
    for stage in range(3, stages):
        for stream in heavy:
            sums.advance(stream, stage)
    for step in range(1, depth):
        source = lax.rem(place + depth - step, depth) * 2 + side
        share_copy(source, source, step).wait_recv()
    spread = Spread(dims, streams[light]["order"], whole, gather_send, gather_recv)
    for step in range(len(tok_dims) + 1):
        spread.start()
        if step == 0:
            for stream in slices:
                sums.advance(stream, 1)
        spread.finish()
    for copy in moves + shares:
        copy.wait_send()

    @pl.loop(0, depth * 2)
    def _(image):
        pixel_local(image).wait()

        @pl.loop(1, owners)
        def _(step):
            source = lax.rem(mine + owners - step, owners)
            pltpu.make_async_remote_copy(
                src_ref=pix_ref.at[source, image],
                dst_ref=pixel_land.at[source, image],
                send_sem=pixel_send.at[image, step - 1],
                recv_sem=pixel_recv.at[image, step - 1],
                device_id=at_band(source),
                device_id_type=MESH,
            ).wait()

    for copy in copies + [near]:
        copy.wait_send()

    @pl.when(has_right)
    def _():
        to_right().wait_send()

    @pl.when(has_left)
    def _():
        to_left().wait_send()

    sums.drain()


def tail_call(
    gen_grid,
    pix,
    kernels,
    layer_parts,
    low_own,
    even,
    odd,
    weights,
    features,
    token,
    bias_grad,
    params,
    gen_b_grad,
    gain_lines,
    factor,
    collective_id,
):
    dims, band_bits, tok_bits = mesh_bits()
    everything = len(dims)
    low = jnp.bfloat16
    owners, images, share, slot = pix.shape
    depth = owners // 2
    pixel_share, model_dim, hyper_dim = gen_grid.shape
    rows = owners * 8
    split, outs, landing, streams = [], [], [], []
    order = halving_order(0, band_bits, tok_bits)
    tallest, base = 0, 0
    for k, weight in enumerate(weights):
        height = weight.shape[0] >> everything
        split.append(weight.reshape((2,) * everything + (height, weight.shape[1])))
        for start, size in row_chunks(height, 3 if height > 32 else 1):
            streams.append(stream_entry(k, 0, start, size, order, dims, True))
            streams[-1]["base"] = base
            landing += landing_shapes(streams[-1], weight.shape[1])
            tallest = max(tallest, size)
        base += height
    outs.append(jax.ShapeDtypeStruct((base, model_dim), jnp.float32))
    bulk = len(weights)
    tok_order = halving_order(2, band_bits, tok_bits)
    height = pixel_share * model_dim >> tok_bits
    outs.append(jax.ShapeDtypeStruct((height, hyper_dim), jnp.float32))
    for start, size in row_chunks(height, 4):
        out_rows = size
        streams.append(stream_entry(bulk, 1, start, size, tok_order, dims, False, factor))
        landing += landing_shapes(streams[-1], hyper_dim)
    wide_shapes = [p.shape for p in params[:6]] + [gen_b_grad.shape, gain_lines.shape]
    blocks, used, piece = wide_plan(wide_shapes, 1 << everything)
    near_order = tok_order + [("band", 0)]
    light = stream_entry(bulk + 1, None, 0, piece, near_order, dims, False)
    light["span"] = dims
    streams.append(light)
    landing += [
        pltpu.VMEM((2,) * (everything - 1 - stage) + (piece, 128), low)
        for stage in range(len(near_order))
    ]
    count = len(streams)
    plan = {"streams": streams, "dims": dims, "bulk": bulk, "blocks": blocks, "used": used}
    space = (2,) * everything + (piece, 128)
    own = pltpu.VMEM((2,) * (everything - 1) + (tallest, model_dim), low)
    dma = pltpu.SemaphoreType.DMA
    return pl.pallas_call(
        functools.partial(tail_kernel, factor, plan),
        out_shape=[jax.ShapeDtypeStruct(pix.shape, low)]
        + outs
        + [jax.ShapeDtypeStruct(space, low), jax.ShapeDtypeStruct((slot, model_dim), low)],
        in_specs=[pl.BlockSpec(memory_space=pl.ANY)] * (6 + bulk)
        + [pl.BlockSpec(memory_space=pltpu.VMEM)] * 10
        + [pl.BlockSpec(memory_space=pl.ANY)] * 2
        + [pl.BlockSpec(memory_space=pltpu.VMEM)] * 4,
        out_specs=[pl.BlockSpec(memory_space=pl.ANY)]
        + [
            pl.BlockSpec(memory_space=pltpu.VMEM),
            pl.BlockSpec(memory_space=pl.ANY),
            pl.BlockSpec(memory_space=pltpu.VMEM),
            pl.BlockSpec(memory_space=pltpu.VMEM),
        ],
        scratch_shapes=[
            pltpu.VMEM(gen_grid.shape, low),
            pltpu.VMEM(pix.shape, low),
            pltpu.VMEM((images // 2, 2, owners, share, model_dim), low),
            pltpu.VMEM((images, slot, model_dim), low),
            pltpu.VMEM((2, owners, share, slot), low),
            pltpu.VMEM((2, depth, rows, hyper_dim), jnp.float32),
            pltpu.VMEM((owners - 1, 2, rows, hyper_dim), jnp.float32),
            pltpu.VMEM((features.shape[0] + 8, hyper_dim), jnp.float32),
            pltpu.VMEM(params[4].shape, jnp.float32),
            pltpu.VMEM(params[5].shape, jnp.float32),
            own,
            own,
        ]
        + landing
        + [
            pltpu.VMEM(space, low),
            dma((5,)),
            dma,
            dma((2,)),
            dma((depth - 1,)),
            dma((depth - 1,)),
            dma((owners,)),
            dma((owners - 1,)),
            dma((owners - 1,)),
            dma((count, everything)),
            dma((count, everything)),
            dma((2,)),
            dma((everything,)),
            dma((everything,)),
            dma((images, owners - 1)),
            dma((images, owners - 1)),
            dma((images,)),
            pltpu.VMEM((depth - 1, piece, 128), low),
            dma((depth - 1,)),
            dma((depth - 1,)),
            dma((depth - 1,)),
            dma((depth - 1,)),
            pltpu.VMEM((out_rows, hyper_dim), jnp.float32),
            dma,
            pltpu.VMEM((slot, model_dim), jnp.float32),
            dma((3, 2)),
        ],
        compiler_params=pltpu.CompilerParams(
            collective_id=collective_id, has_side_effects=True, vmem_limit_bytes=63 << 20
        ),
        cost_estimate=pl.CostEstimate(
            flops=2 * 10**10, bytes_accessed=3 * 10**8, transcendentals=0
        ),
    )(
        gen_grid,
        pix,
        kernels,
        *layer_parts,
        *split,
        low_own,
        even,
        odd,
        features,
        token,
        bias_grad,
        *params,
        gen_b_grad,
        gain_lines,
    )


def layer_norm(values, scaling, epsilon):
    center = values - jnp.mean(values, axis=-1, keepdims=True)
    spread = jnp.mean(center * center, axis=-1, keepdims=True)
    return center * lax.rsqrt(spread + epsilon) * scaling


def block_norm(values, scaling):
    return layer_norm(values, scaling, EPS_BLOCK)


def exact_gelu(values):
    return 0.5 * values * (1.0 + lax.erf(values * math.sqrt(0.5)))


def wave_features(lengths, model_dim):
    middle = model_dim // 2
    angular = 1.0 / 10000.0 ** (jnp.arange(middle, dtype=jnp.float32) / middle)
    phases = (100.0 * lengths)[..., None] * angular
    return jnp.concatenate([jnp.sin(phases), jnp.cos(phases)], axis=-1)


def hyper_layer(features, params):
    (
        bias_token,
        hyper_query,
        hyper_key,
        hyper_value,
        hyper_out,
        hyper_up,
        hyper_down,
        hyper_gain1,
        hyper_gain2,
    ) = params
    images = features.shape[0]
    model_dim = features.shape[-1]
    head_size = model_dim // HHEADS
    tokens = jnp.concatenate(
        [features, jnp.broadcast_to(bias_token, (images, 1, model_dim))], axis=1
    )
    length = tokens.shape[1]
    queries = jnp.einsum("nsc,ce->nse", tokens, hyper_query, precision=PRECISE).reshape(
        images, length, HHEADS, head_size
    )
    keys_all = jnp.einsum("nsc,ce->nse", tokens, hyper_key, precision=PRECISE).reshape(
        images, length, HHEADS, head_size
    )
    values_all = jnp.einsum("nsc,ce->nse", tokens, hyper_value, precision=PRECISE).reshape(
        images, length, HHEADS, head_size
    )
    scores = jnp.einsum("nshe,nthe->nhst", queries, keys_all, precision=PRECISE) / math.sqrt(
        head_size
    )
    weights = jax.nn.softmax(scores, axis=-1)
    blended = jnp.einsum("nhst,nthe->nshe", weights, values_all, precision=PRECISE).reshape(
        images, length, model_dim
    )
    segment_one = layer_norm(
        tokens + jnp.einsum("nse,ef->nsf", blended, hyper_out, precision=PRECISE),
        hyper_gain1,
        EPS_HYPER,
    )
    expanded = jax.nn.gelu(
        jnp.einsum("nse,ef->nsf", segment_one, hyper_up, precision=PRECISE), approximate=False
    )
    second = layer_norm(
        segment_one + jnp.einsum("nsf,fe->nse", expanded, hyper_down, precision=PRECISE),
        hyper_gain2,
        EPS_HYPER,
    )
    return (second[:, :-1, :], second[:, -1, :])


def precise_dot(left, right, contract=(1, 0)):
    return lax.dot_general(
        left,
        right,
        (((contract[0],), (contract[1],)), ((), ())),
        precision=PRECISE,
        preferred_element_type=jnp.float32,
    )


def hyper_attention(tokens, params, images):
    query, key, value, mix, first = params
    rows, hyper_dim = tokens.shape
    bands = (rows - 8 * -(-images // 8)) // images
    head = hyper_dim // HHEADS

    def owner(index):
        return jnp.where(index < images * bands, lax.div(index, bands), index - images * bands)

    same = owner(lax.broadcasted_iota(jnp.int32, (rows, rows), 0)) == owner(
        lax.broadcasted_iota(jnp.int32, (rows, rows), 1)
    )
    lane = lax.div(lax.broadcasted_iota(jnp.int32, (1, hyper_dim), 1), head)
    queries = precise_dot(tokens, query) * (1.0 / math.sqrt(head))
    keys_all = precise_dot(tokens, key)
    values_all = precise_dot(tokens, value)
    blended = None
    for place in range(HHEADS):
        chosen = (lane == place).astype(jnp.float32)
        scores = precise_dot(queries * chosen, keys_all, (1, 1))
        scores = jnp.where(same, scores, -1e30)
        highest = lax.stop_gradient(jnp.max(scores, axis=-1, keepdims=True))
        lifted = jnp.exp(scores - highest)
        weights = lifted / jnp.sum(lifted, axis=-1, keepdims=True)
        part = precise_dot(weights, values_all * chosen)
        blended = part if blended is None else blended + part
    return layer_norm(tokens + precise_dot(blended, mix), first, EPS_HYPER)


def hyper_wide(segment, expand_ref, shrink_ref, total_ref, width):
    total_ref[...] = segment

    @pl.loop(0, expand_ref.shape[1] // width)
    def _(part):
        columns = pl.ds(pl.multiple_of(part * width, width), width)
        wide = precise_dot(segment, expand_ref[:, columns])
        active = 0.5 * wide * (1.0 + lax.erf(wide * math.sqrt(0.5)))
        total_ref[...] += precise_dot(active, shrink_ref[columns, :])


def hyper_wide_back(segment, d_total, expand_ref, shrink_ref, d_segment_ref, width):
    d_segment_ref[...] = d_total

    @pl.loop(0, expand_ref.shape[1] // width)
    def _(part):
        columns = pl.ds(pl.multiple_of(part * width, width), width)
        wide = precise_dot(segment, expand_ref[:, columns])
        bell = 0.5 * (1.0 + lax.erf(wide * math.sqrt(0.5)))
        slope = bell + wide * jnp.exp(-0.5 * wide * wide) * (1.0 / math.sqrt(2.0 * math.pi))
        d_wide = precise_dot(d_total, shrink_ref[columns, :], (1, 1)) * slope
        d_segment_ref[...] += precise_dot(d_wide, expand_ref[:, columns], (1, 1))
        shrink_ref[columns, :] = precise_dot(wide * bell, d_total, (0, 0))
        expand_ref[:, columns] = precise_dot(segment, d_wide, (0, 0))


def contract_rows(left_side, right_side):
    return lax.dot_general(
        left_side, right_side, (((0,), (0,)), ((), ())), preferred_element_type=jnp.float32
    )


def contract_cols(left_side, right_side):
    return lax.dot_general(
        left_side, right_side, (((1,), (1,)), ((), ())), preferred_element_type=jnp.float32
    )


def attention_scores(queries, keys_low, usable):
    head_size = queries.shape[-1]
    scores = jnp.einsum(
        "iqhe,ikhe->ihqk", queries, keys_low, preferred_element_type=jnp.float32
    ) / math.sqrt(head_size)
    return jnp.where(usable[:, None, None, :], scores, -1e30)


def block_forward(embedded, usable, weights_full, ln1_gain, ln2_gain):
    w_qkv_full, w_out_full, w_up_full, w_down_full = weights_full
    images, slot_count, model_dim = embedded.shape
    row_count = images * slot_count
    head_count = model_dim // HD
    flat_rows = embedded.reshape(row_count, model_dim)
    normed_one = block_norm(flat_rows, ln1_gain).astype(jnp.bfloat16)
    qkv_low = jnp.dot(normed_one, w_qkv_full, preferred_element_type=jnp.float32).astype(
        jnp.bfloat16
    )
    sections = qkv_low.reshape(images, slot_count, 3, head_count, HD)
    queries = sections[:, :, 0]
    keys_low = sections[:, :, 1]
    values_low = sections[:, :, 2]
    scores = attention_scores(queries, keys_low, usable)
    highest = jnp.max(scores, axis=-1, keepdims=True)
    lifted = jnp.exp(scores - highest)
    totals = jnp.sum(lifted, axis=-1, keepdims=True)
    attn_probs = (lifted / totals).astype(jnp.bfloat16)
    log_mass = highest + jnp.log(totals)
    attended = (
        jnp.einsum("ihqk,ikhe->iqhe", attn_probs, values_low, preferred_element_type=jnp.float32)
        .astype(jnp.bfloat16)
        .reshape(row_count, model_dim)
    )
    middle = flat_rows + jnp.dot(attended, w_out_full, preferred_element_type=jnp.float32)
    normed_two = block_norm(middle, ln2_gain).astype(jnp.bfloat16)
    hidden = jnp.dot(normed_two, w_up_full, preferred_element_type=jnp.float32)
    active = exact_gelu(hidden).astype(jnp.bfloat16)
    output = middle + jnp.dot(active, w_down_full, preferred_element_type=jnp.float32)
    return (
        flat_rows,
        normed_one,
        queries,
        keys_low,
        values_low,
        log_mass,
        attended,
        middle,
        normed_two,
        hidden,
        active,
        output,
    )


def block_backward(stored, usable, grad_rows, weights_full, ln1_gain, ln2_gain):
    (
        flat_rows,
        normed_one,
        queries,
        keys_low,
        values_low,
        log_mass,
        attended,
        middle,
        normed_two,
        hidden,
        active,
        output,
    ) = stored
    w_qkv_full, w_out_full, w_up_full, w_down_full = weights_full
    images, slot_count, head_count, head_size = queries.shape
    row_count, model_dim = flat_rows.shape
    grad_low = grad_rows.astype(jnp.bfloat16)
    grad_down = contract_rows(active, grad_low)
    d_active = contract_cols(grad_low, w_down_full)
    gelu_back = jax.vjp(exact_gelu, hidden)[1]
    d_hidden = gelu_back(d_active)[0].astype(jnp.bfloat16)
    grad_up_turned = contract_rows(d_hidden, normed_two)
    d_normed_two = contract_cols(d_hidden, w_up_full)
    norm_back_two = jax.vjp(block_norm, middle, ln2_gain)[1]
    d_middle_norm, grad_gain_two = norm_back_two(d_normed_two)
    d_middle = grad_rows + d_middle_norm
    d_middle_low = d_middle.astype(jnp.bfloat16)
    grad_out_turned = contract_rows(d_middle_low, attended)
    d_attended = (
        contract_cols(d_middle_low, w_out_full)
        .astype(jnp.bfloat16)
        .reshape(images, slot_count, head_count, head_size)
    )
    scores = attention_scores(queries, keys_low, usable)
    attn_float = jnp.exp(scores - log_mass)
    attn_probs = attn_float.astype(jnp.bfloat16)
    d_values = jnp.einsum(
        "ihqk,iqhe->ikhe", attn_probs, d_attended, preferred_element_type=jnp.float32
    ).astype(jnp.bfloat16)
    d_probs = jnp.einsum(
        "iqhe,ikhe->ihqk", d_attended, values_low, preferred_element_type=jnp.float32
    )
    d_scores = (
        attn_float * (d_probs - jnp.sum(attn_float * d_probs, axis=-1, keepdims=True))
    ).astype(jnp.bfloat16)
    d_queries = (
        jnp.einsum("ihqk,ikhe->iqhe", d_scores, keys_low, preferred_element_type=jnp.float32)
        / math.sqrt(head_size)
    ).astype(jnp.bfloat16)
    d_keys = (
        jnp.einsum("ihqk,iqhe->ikhe", d_scores, queries, preferred_element_type=jnp.float32)
        / math.sqrt(head_size)
    ).astype(jnp.bfloat16)
    d_qkv = jnp.stack([d_queries, d_keys, d_values], axis=2).reshape(row_count, 3 * model_dim)
    grad_qkv_turned = contract_rows(d_qkv, normed_one)
    d_normed_one = contract_cols(d_qkv, w_qkv_full)
    norm_back_one = jax.vjp(block_norm, flat_rows, ln1_gain)[1]
    d_flat, grad_gain_one = norm_back_one(d_normed_one)
    return (
        d_middle + d_flat,
        (grad_qkv_turned, grad_out_turned, grad_up_turned, grad_down, grad_gain_one, grad_gain_two),
    )


def body(
    pixels,
    wave_table,
    wave_index,
    patch_count,
    d_out,
    gen_w,
    gen_b,
    bias_token,
    hyper_query,
    hyper_key,
    hyper_value,
    hyper_out,
    hyper_up,
    hyper_down,
    hyper_gain1,
    hyper_gain2,
    w_qkv,
    w_out,
    w_up,
    w_down,
    ln1_gain,
    ln2_gain,
):
    group_images, band_share, slot_count, pixel_count = pixels.shape[1:]
    own_images = patch_count.shape[1]
    model_dim = w_out.shape[0]
    hyper_dim = gen_w.shape[1]
    all_bands = wave_index.shape[2]
    owners = lax.axis_size("band")
    slice_pixels = pixel_count // owners
    factor = 1.0 / math.sqrt(all_bands * pixel_count)
    band_place = lax.axis_index("band")
    hyper_params = (
        bias_token,
        hyper_query,
        hyper_key,
        hyper_value,
        hyper_out,
        hyper_up,
        hyper_down,
        hyper_gain1,
        hyper_gain2,
    )
    paired = (
        band_share == 4
        and own_images == 1
        and group_images == owners
        and owners % 2 == 0
        and slice_pixels % 4 == 0
        and model_dim % 256 == 0
        and model_dim // slot_count + 1 == group_images // 2
        and model_dim % slot_count == 0
        and w_down.shape[0] * lax.axis_size("tok") % model_dim == 0
    )
    if paired:
        pixel_lined = lax.all_to_all(turn_pixels(pixels[0], owners), "band", 0, 0, tiled=True)
    else:
        pixel_turned = (
            pixels[0]
            .reshape(group_images, band_share, slot_count, owners, slice_pixels)
            .transpose(3, 0, 4, 1, 2)
        )
        pixel_blocks = lax.all_to_all(pixel_turned, "band", 0, 0, tiled=True)
    gen_part = lax.all_gather(gen_w, "tok", axis=0, tiled=True)
    gen_grid = gen_part.reshape(slice_pixels, model_dim, hyper_dim)
    weights_full = (
        lax.all_gather(w_qkv, "tok", axis=1, tiled=True),
        lax.all_gather(w_out, "tok", axis=1, tiled=True),
        lax.all_gather(w_up, "tok", axis=1, tiled=True),
        lax.all_gather(w_down, "tok", axis=0, tiled=True),
    )
    catalog = lax.broadcasted_iota(jnp.int32, (1, 1, wave_table.shape[0]), 2)
    picked = (wave_index[0][:, :, None] == catalog).astype(jnp.float32)
    lengths_all = jnp.sum(picked * wave_table, axis=-1)
    hyper_input = wave_features(lengths_all, hyper_dim)
    band_feats, bias_feats = hyper_layer(hyper_input, hyper_params)
    band_low = band_feats.astype(jnp.bfloat16).reshape(-1, hyper_dim)
    own_input = lax.dynamic_slice_in_dim(hyper_input, band_place * own_images, own_images, 0)

    def run_hyper(params):
        return hyper_layer(own_input, params)

    if paired:
        bias_own = lax.dynamic_slice_in_dim(
            bias_feats, band_place * own_images, own_images, 0
        )
    else:
        (_, bias_own), hyper_back = jax.vjp(run_hyper, hyper_params)
    if paired:
        ordered = (
            band_feats.astype(jnp.bfloat16)
            .reshape(group_images // 2, 2, owners, band_share, hyper_dim)
            .transpose(0, 2, 1, 3, 4)
        )
        even_rows = ordered.reshape(-1, hyper_dim)
        odd_rows = ordered[:, :, ::-1].reshape(-1, hyper_dim)
        kernel_lined = make_kernels(
            gen_grid, even_rows, odd_rows, group_images, owners, factor
        )
        convolved = embed_parts(kernel_lined, pixel_lined, model_dim, 1)
    else:
        pixel_slices = pixel_blocks.transpose(1, 2, 0, 3, 4).reshape(
            group_images, slice_pixels * all_bands, slot_count
        )
        kernels = (
            jnp.einsum("pdc,nc->pnd", gen_grid, band_low, preferred_element_type=jnp.float32) * factor
        ).astype(jnp.bfloat16)
        kernel_grid = kernels.reshape(slice_pixels, group_images, all_bands, model_dim)
        kernel_rows = kernel_grid.transpose(1, 0, 2, 3).reshape(
            group_images, slice_pixels * all_bands, model_dim
        )
        product = jnp.einsum(
            "iks,ikd->isd", pixel_slices, kernel_rows, preferred_element_type=jnp.float32
        )
        convolved = lax.psum_scatter(
            product.reshape(group_images * slot_count, model_dim).astype(jnp.bfloat16),
            "band",
            scatter_dimension=0,
            tiled=True,
        ).astype(jnp.float32)
    bias_rows = jnp.dot(bias_own, gen_b, precision=PRECISE)
    embedded = convolved.reshape(own_images, slot_count, model_dim) + bias_rows[:, None, :]
    usable = lax.broadcasted_iota(jnp.int32, (own_images, slot_count), 1) < patch_count[0][:, None]
    stored = block_forward(embedded, usable, weights_full, ln1_gain, ln2_gain)
    row_mask = usable.reshape(-1, 1)
    layer_out = (
        jnp.where(row_mask, stored[-1], 0.0)
        .astype(jnp.bfloat16)
        .reshape(1, own_images, slot_count, model_dim)
    )
    grad_rows = jnp.where(row_mask, d_out[0].reshape(-1, model_dim).astype(jnp.float32), 0.0)
    d_embed, block_terms = block_backward(
        stored, usable, grad_rows, weights_full, ln1_gain, ln2_gain
    )
    d_embed_low = d_embed.astype(jnp.bfloat16).reshape(own_images, slot_count, model_dim)
    d_bias = jnp.sum(d_embed.reshape(own_images, slot_count, model_dim), axis=1)
    d_bias_feat = jnp.dot(d_bias, gen_b.T, precision=PRECISE)
    grad_gen_b = jnp.dot(bias_own.T, d_bias, precision=PRECISE)
    qkv_turned, out_turned, up_turned, grad_down, gain_one, gain_two = block_terms
    weight_terms = [
        term.astype(jnp.bfloat16) for term in (qkv_turned, out_turned, up_turned, grad_down)
    ]
    gain_rows = model_dim // hyper_dim
    gain_lines = [gain_one.reshape(-1, hyper_dim), gain_two.reshape(-1, hyper_dim)]
    fill = -(3 + 2 * gain_rows) % 16
    gain_lines.append(jnp.zeros((fill, hyper_dim), jnp.float32))
    if paired:
        grad_blocks, weight_sums, grad_gen_w, whole, layer_rows = tail_call(
            gen_grid,
            pixel_lined,
            kernel_lined,
            [stored[10], weights_full[3], stored[7]],
            d_embed_low.reshape(slot_count, model_dim),
            even_rows,
            odd_rows,
            weight_terms,
            own_input[0],
            bias_token[None],
            d_bias_feat,
            [
                hyper_query,
                hyper_key,
                hyper_value,
                hyper_out,
                hyper_up,
                hyper_down,
                hyper_gain1[None],
                hyper_gain2[None],
            ],
            grad_gen_b,
            jnp.concatenate([jnp.zeros((3, hyper_dim), jnp.float32)] + gain_lines),
            factor,
            2,
        )
        devices = owners * lax.axis_size("tok")
        (
            pixel_grad,
            qkv_sum,
            out_sum,
            up_sum,
            down_sum,
            query_sum,
            key_sum,
            value_sum,
            mix_sum,
            expand_sum,
            shrink_sum,
            gen_b_sum,
            line_sum,
        ) = unturn_pixels(
            grad_blocks,
            pixels.shape[1:],
            weight_sums,
            [term.shape[0] // devices for term in weight_terms],
            whole,
            [part.shape for part in hyper_params[1:7]]
            + [gen_b.shape, (3 + 2 * gain_rows + fill, hyper_dim)],
        )
        pixel_grad = pixel_grad[None]
        layer_out = jnp.where(row_mask, layer_rows, jnp.zeros_like(layer_rows)).reshape(
            1, own_images, slot_count, model_dim
        )
    else:
        d_gathered = lax.all_gather(d_embed_low, "band", axis=0, tiled=True)
        grad_slices = jnp.einsum(
            "ikd,isd->iks", kernel_rows, d_gathered, preferred_element_type=jnp.float32
        ).astype(jnp.bfloat16)
        grad_slices = grad_slices.reshape(
            group_images, slice_pixels, owners, band_share, slot_count
        ).transpose(2, 0, 1, 3, 4)
        d_kernel = jnp.einsum(
            "iks,isd->ikd", pixel_slices, d_gathered, preferred_element_type=jnp.float32
        ).astype(jnp.bfloat16)
        d_kernel = (
            d_kernel.reshape(group_images, slice_pixels, all_bands, model_dim)
            .transpose(1, 0, 2, 3)
            .reshape(slice_pixels, group_images * all_bands, model_dim)
        )
        d_band_part = (
            jnp.einsum("pnd,pdc->nc", d_kernel, gen_grid, preferred_element_type=jnp.float32) * factor
        )
        d_band_own = lax.psum_scatter(d_band_part, "band", scatter_dimension=0, tiled=True)
        gen_part_grad = (
            jnp.einsum("pnd,nc->pdc", d_kernel, band_low, preferred_element_type=jnp.float32) * factor
        )
        gen_low = gen_part_grad.reshape(-1, hyper_dim).astype(jnp.bfloat16)
        grad_slices = lax.all_to_all(grad_slices, "band", 0, 0, tiled=True)
        pixel_grad = grad_slices.transpose(1, 3, 4, 0, 2).reshape(pixels.shape)
        (
            grad_token,
            grad_query,
            grad_key,
            grad_value,
            grad_mix,
            grad_expand,
            grad_shrink,
            grad_first_gain,
            grad_second_gain,
        ) = hyper_back((d_band_own.reshape(own_images, all_bands, hyper_dim), d_bias_feat))[0]
        lines = jnp.concatenate(
            [grad_token[None], grad_first_gain[None], grad_second_gain[None]] + gain_lines
        )
        (
            qkv_sum,
            out_sum,
            up_sum,
            down_sum,
            grad_gen_w,
            query_sum,
            key_sum,
            value_sum,
            mix_sum,
            expand_sum,
            shrink_sum,
            gen_b_sum,
            line_sum,
        ) = reduce_all(
            weight_terms + [gen_low],
            [1, 0, 1, 1, 2],
            [2, 1, 2, 2, 2],
            [
                grad_query,
                grad_key,
                grad_value,
                grad_mix,
                grad_expand,
                grad_shrink,
                grad_gen_b,
                lines,
            ],
            3,
        )
    devices = owners * lax.axis_size("tok")
    place = band_place * lax.axis_size("tok") + lax.axis_index("tok")
    gain_share = model_dim // devices

    def own_gain(whole):
        return lax.dynamic_slice_in_dim(whole.reshape(-1), place * gain_share, gain_share, 0)

    return (
        layer_out,
        pixel_grad,
        grad_gen_w,
        gen_b_sum,
        line_sum[0],
        query_sum,
        key_sum,
        value_sum,
        mix_sum,
        expand_sum,
        shrink_sum,
        line_sum[1],
        line_sum[2],
        qkv_sum.T,
        out_sum.T,
        up_sum.T,
        down_sum,
        own_gain(line_sum[3 : 3 + gain_rows]),
        own_gain(line_sum[3 + gain_rows : 3 + 2 * gain_rows]),
    )


def solution(mesh):
    placed = (
        P("tok", None, "band", None, None),
        P(),
        P("tok", None, None),
        P("tok", "band"),
        P("tok", "band", None, None),
        P(("band", "tok"), None),
        P(),
        P(),
        P(),
        P(),
        P(),
        P(),
        P(),
        P(),
        P(),
        P(),
        P(None, "tok"),
        P(None, "tok"),
        P(None, "tok"),
        P("tok", None),
        P(),
        P(),
    )
    return jax.shard_map(
        body,
        mesh=mesh,
        in_specs=placed,
        out_specs=(
            P("tok", "band", None, None),
            P("tok", None, "band", None, None),
            P(("band", "tok"), None),
            P(),
            P(),
            P(),
            P(),
            P(),
            P(),
            P(),
            P(),
            P(),
            P(),
            P(None, ("band", "tok")),
            P(None, ("band", "tok")),
            P(None, ("band", "tok")),
            P(("band", "tok"), None),
            P(("band", "tok")),
            P(("band", "tok")),
        ),
        check_vma=False,
    )
```

```python
import functools
import math

import jax
import jax.numpy as jnp
from jax import lax
from jax.experimental import pallas as pl
from jax.experimental.pallas import tpu as pltpu
from jax.sharding import PartitionSpec as P

HD = 64
HHEADS = 4


EPS_BLOCK = 1e-06
EPS_HYPER = 1e-05
PRECISE = lax.Precision.HIGHEST


MESH = pl.DeviceIdType.MESH


def mesh_bits():
    tok_bits = (lax.axis_size("tok") - 1).bit_length()
    band_bits = (lax.axis_size("band") - 1).bit_length()
    dims = [("band", b) for b in reversed(range(band_bits))]
    dims += [("tok", b) for b in reversed(range(tok_bits))]
    return dims, band_bits, tok_bits


def own_bit(axis, bit):
    return lax.rem(lax.div(lax.axis_index(axis), 1 << bit), 2)


def partner_of(axis, bit):
    place = lax.axis_index(axis)
    mine = own_bit(axis, bit)
    other = place + (1 - 2 * mine) * (1 << bit)
    band, tok = lax.axis_index("band"), lax.axis_index("tok")
    return (other, tok) if axis == "band" else (band, other)


def halving_order(which, band_bits, tok_bits):
    tok = [("tok", b) for b in range(tok_bits)]
    band = [("band", b) for b in range(band_bits)]
    if which == 2:
        return tok
    if which == 0:
        return tok + band
    return tok[:1] + band[:1] + tok[1:] + band[1:]


def pick(remaining, axis_bit, value):
    place = remaining.index(axis_bit)
    return tuple([slice(None)] * place + [value])


def add_block(dest, left, right):
    lead = dest.shape[:-2]

    def one(index):
        spot = []
        for size in reversed(lead):
            spot.insert(0, lax.rem(index, size))
            index = lax.div(index, size)
        spot = tuple(spot)
        dest[spot] = (left(spot) + right(spot)).astype(dest.dtype)

    pl.loop(0, math.prod(lead))(one)


def wide_blocks(shapes, piece):
    blocks, start = [], 0
    for index, (rows, columns) in enumerate(shapes):
        for part in range(columns // 128):
            row = 0
            while row < rows:
                inside = start % piece
                size = min(rows - row, piece - inside)
                blocks.append((index, row, part, start // piece, inside, size))
                row += size
                start += size
    return blocks, start


def segment_spot(segment, count):
    return tuple((segment >> (count - 1 - bit)) & 1 for bit in range(count))


class Sums:
    def __init__(
        self, streams, sources, outputs, own, landing, send_sem, recv_sem, own_sem, buffer=None
    ):
        self.buffer = buffer
        self.streams, self.sources, self.outputs = streams, sources, outputs
        self.own, self.landing = own, landing
        self.send_sem, self.recv_sem, self.own_sem = send_sem, recv_sem, own_sem
        self.flying, self.local = {}, {}

    def part(self, stream, value):
        entry = self.streams[stream]
        spot = pick(entry["span"], entry["order"][0], value)
        spot = spot + (slice(None),) * (len(entry["span"]) - len(spot))
        rows = pl.ds(entry["start"], entry["rows"])
        return self.sources[entry["source"]].at[spot + (rows,)]

    def fetch(self, stream):
        entry = self.streams[stream]
        if entry["fetch"]:
            slot = stream % len(self.own)
            whole = (slice(None),) * (len(entry["span"]) - 1)
            target = self.own[slot].at[whole + (pl.ds(0, entry["rows"]),)]
            copy = pltpu.make_async_copy(
                self.part(stream, own_bit(*entry["order"][0])), target, self.own_sem.at[slot]
            )
            copy.start()
            self.local[stream] = (copy, target)

    def send(self, stream, stage, source):
        axis, bit = self.streams[stream]["order"][stage]
        copy = pltpu.make_async_remote_copy(
            src_ref=source,
            dst_ref=self.landing[stream][stage],
            send_sem=self.send_sem.at[stream, stage],
            recv_sem=self.recv_sem.at[stream, stage],
            device_id=partner_of(axis, bit),
            device_id_type=MESH,
        )
        copy.start()
        self.flying[stream, stage] = copy

    def begin(self, stream):
        first = self.streams[stream]["order"][0]
        self.send(stream, 0, self.part(stream, 1 - own_bit(*first)))

    def advance(self, stream, stage):
        entry = self.streams[stream]
        order, span = entry["order"], entry["span"]
        if stage >= len(order):
            return
        remaining = [d for d in span if d not in order[:stage]]
        axis_bit = order[stage]
        after = [d for d in remaining if d != axis_bit]
        self.flying[stream, stage].wait_recv()
        land = self.landing[stream][stage]
        if stage > 0:
            held = self.landing[stream][stage - 1].at[
                pick(remaining, axis_bit, own_bit(*axis_bit))
            ]
        elif stream in self.local:
            self.local[stream][0].wait()
            held = self.local[stream][1]
        else:
            held = self.part(stream, own_bit(*axis_bit))
        if stage == len(order) - 1 and entry["out"] is not None:
            total = land[...].astype(jnp.float32) + held[...].astype(jnp.float32)
            rows = pl.ds(entry["base"] + entry["start"], entry["rows"])
            if entry["fetch"]:
                self.outputs[entry["out"]][rows] = total * entry["scale"]
            else:
                buffer, sem = self.buffer
                buffer[...] = total * entry["scale"]
                copy = pltpu.make_async_copy(buffer, self.outputs[entry["out"]].at[rows], sem)
                copy.start()
                copy.wait()
        else:
            add_block(
                land,
                lambda spot: land[spot].astype(jnp.float32),
                lambda spot: held[spot].astype(jnp.float32),
            )
            if stage < len(order) - 1:
                following = order[stage + 1]
                self.send(
                    stream, stage + 1, land.at[pick(after, following, 1 - own_bit(*following))]
                )

    def drain(self):
        for copy in self.flying.values():
            copy.wait_send()


class Spread:
    def __init__(self, dims, order, whole, send_sem, recv_sem):
        self.dims, self.order, self.whole = dims, list(reversed(order)), whole
        self.send_sem, self.recv_sem = send_sem, recv_sem
        self.spot = [own_bit(*d) if d in order else slice(None) for d in dims]
        self.copies = []

    def start(self):
        step = len(self.copies)
        view = self.whole.at[tuple(self.spot)]
        copy = pltpu.make_async_remote_copy(
            src_ref=view,
            dst_ref=view,
            send_sem=self.send_sem.at[step],
            recv_sem=self.recv_sem.at[step],
            device_id=partner_of(*self.order[step]),
            device_id_type=MESH,
        )
        copy.start()
        self.copies.append(copy)

    def finish(self):
        self.copies[-1].wait()
        self.spot[self.dims.index(self.order[len(self.copies) - 1])] = slice(None)


def pack_blocks(blocks, used, packed, wide, stages):
    for index, row, part, segment, inside, size in blocks:
        packed[segment_spot(segment, stages) + (pl.ds(inside, size),)] = wide[index](
            pl.ds(row, size), pl.ds(part * 128, 128)
        ).astype(packed.dtype)
    piece = packed.shape[-2]
    while used < piece << stages:
        size = piece - used % piece
        packed[segment_spot(used // piece, stages) + (pl.ds(used % piece, size),)] = jnp.zeros(
            (size, 128), packed.dtype
        )
        used += size


def unpack_blocks(blocks, whole, wide_out, stages):
    for index, row, part, segment, inside, size in blocks:
        wide_out[index][pl.ds(row, size), pl.ds(part * 128, 128)] = whole[
            segment_spot(segment, stages) + (pl.ds(inside, size),)
        ].astype(jnp.float32)


def reduce_kernel(plan, blocks, used, *refs):
    streams, dims = plan["streams"], plan["dims"]
    count, stages = len(streams), len(dims)
    pos = plan["bulk"]
    inputs = list(refs[:pos])
    wide = refs[pos : pos + plan["wide"]]
    pos += plan["wide"]
    outputs = refs[pos : pos + plan["bulk"]]
    pos += plan["bulk"]
    wide_out = refs[pos : pos + plan["wide"]]
    pos += plan["wide"]
    own = refs[pos : pos + count - 1]
    pos += count - 1
    landing = []
    for stream in streams:
        landing.append(refs[pos : pos + len(stream["order"])])
        pos += len(stream["order"])
    packed, whole, send_sem, recv_sem, own_sem, gather_send, gather_recv = refs[pos:]
    barrier = pltpu.get_barrier_semaphore()
    for axis, bit in dims:
        pl.semaphore_signal(barrier, inc=1, device_id=partner_of(axis, bit), device_id_type=MESH)
    pl.semaphore_wait(barrier, stages)
    sums = Sums(
        streams, inputs + [packed], outputs, own, landing, send_sem, recv_sem, own_sem
    )
    for stream in range(count - 1):
        sums.begin(stream)
        sums.fetch(stream)
    pack_blocks(
        blocks, used, packed, [lambda r, c, ref=ref: ref[r, c] for ref in wide], stages
    )
    sums.begin(count - 1)
    for stage in range(stages):
        for stream in range(count):
            sums.advance(stream, stage)
    spread = Spread(dims, streams[-1]["order"], whole, gather_send, gather_recv)
    whole[tuple(spread.spot)] = landing[count - 1][stages - 1][...]
    for _ in range(stages):
        spread.start()
        spread.finish()
    unpack_blocks(blocks, whole, wide_out, stages)
    sums.drain()


def stream_entry(source, out, start, rows, order, dims, fetch, scale=1.0):
    return {
        "source": source,
        "out": out,
        "start": start,
        "rows": rows,
        "order": order,
        "span": [d for d in dims if d in order],
        "fetch": fetch,
        "base": 0,
        "scale": scale,
    }


def landing_shapes(entry, lanes):
    stages = len(entry["order"])
    return [
        pltpu.VMEM((2,) * (stages - 1 - stage) + (entry["rows"], lanes), jnp.bfloat16)
        for stage in range(stages)
    ]


def wide_plan(shapes, devices):
    used = sum(math.prod(shape) for shape in shapes) // 128
    piece = -(-used // (16 * devices)) * 16
    return wide_blocks(shapes, piece)[0], used, piece


def row_chunks(rows, chunks):
    size = -(-rows // chunks // 8) * 8
    return [(start, min(size, rows - start)) for start in range(0, rows, size)]


def reduce_all(arrays, whiches, chunks, wide, collective_id):
    dims, band_bits, tok_bits = mesh_bits()
    low, everything = jnp.bfloat16, len(dims)
    split, outs, own, landing, streams = [], [], [], [], []
    for k, array in enumerate(arrays):
        order = halving_order(whiches[k], band_bits, tok_bits)
        stages = len(order)
        rows, lanes = array.shape[0] >> stages, array.shape[1]
        split.append(array.reshape((2,) * stages + (rows, lanes)))
        outs.append(jax.ShapeDtypeStruct((rows, lanes), jnp.float32))
        for start, size in row_chunks(rows, chunks[k]):
            streams.append(stream_entry(k, k, start, size, order, dims, True))
            own.append(pltpu.VMEM((2,) * (stages - 1) + (size, lanes), low))
            landing += landing_shapes(streams[-1], lanes)
    blocks, used, piece = wide_plan([part.shape for part in wide], 1 << everything)
    order = halving_order(0, band_bits, tok_bits)
    streams.append(stream_entry(len(arrays), None, 0, piece, order, dims, False))
    landing += landing_shapes(streams[-1], 128)
    outs += [jax.ShapeDtypeStruct(part.shape, jnp.float32) for part in wide]
    count = len(streams)
    plan = {"streams": streams, "dims": dims, "bulk": len(arrays), "wide": len(wide)}
    sent = sum(a.size for a in arrays)
    space = (2,) * everything + (piece, 128)
    return pl.pallas_call(
        functools.partial(reduce_kernel, plan, blocks, used),
        out_shape=outs,
        in_specs=[pl.BlockSpec(memory_space=pl.ANY)] * len(arrays)
        + [pl.BlockSpec(memory_space=pltpu.VMEM)] * len(wide),
        out_specs=[pl.BlockSpec(memory_space=pltpu.VMEM)] * len(outs),
        scratch_shapes=own
        + landing
        + [
            pltpu.VMEM(space, low),
            pltpu.VMEM(space, low),
            pltpu.SemaphoreType.DMA((count, everything)),
            pltpu.SemaphoreType.DMA((count, everything)),
            pltpu.SemaphoreType.DMA((count,)),
            pltpu.SemaphoreType.DMA((everything,)),
            pltpu.SemaphoreType.DMA((everything,)),
        ],
        compiler_params=pltpu.CompilerParams(
            collective_id=collective_id, has_side_effects=True, vmem_limit_bytes=60 << 20
        ),
        cost_estimate=pl.CostEstimate(flops=2 * sent, bytes_accessed=40 * sent, transcendentals=0),
    )(*split, *wide)


def turn_kernel(in_ref, out_ref, lines):
    together, bands = in_ref.shape[:2]
    halves, rows = lines.shape[:2]
    for image in range(together):
        for band in range(bands):
            turned = in_ref[image, band].astype(jnp.float32).T
            for half in range(halves):
                lines[half, pl.ds(band, rows // bands, stride=bands), :] = turned[
                    :, half * 128 : (half + 1) * 128
                ]
        for half in range(halves):
            out_ref[:, image, :, pl.ds(half * 128, 128)] = (
                lines[half].astype(out_ref.dtype).reshape(*out_ref.shape[:1], -1, 128)
            )


def turn_pixels(pixels, owners):
    images, bands, slot, pixel_count = pixels.shape
    share = pixel_count // owners * bands
    return pl.pallas_call(
        turn_kernel,
        grid=(images // 2,),
        out_shape=jax.ShapeDtypeStruct((owners, images, share, slot), pixels.dtype),
        in_specs=[pl.BlockSpec((2, bands, slot, pixel_count), lambda i: (i, 0, 0, 0))],
        out_specs=pl.BlockSpec((owners, 2, share, slot), lambda i: (0, i, 0, 0)),
        scratch_shapes=[pltpu.VMEM((slot // 128, pixel_count * bands, 128), jnp.float32)],
        compiler_params=pltpu.CompilerParams(vmem_limit_bytes=60 << 20),
    )(pixels)


def unturn_kernel(blocks, heights, *refs):
    in_ref, weight_ref, whole_ref, out_ref = refs[:4]
    weight_out = refs[4 : 4 + len(heights)]
    wide_out = refs[4 + len(heights) : -1]
    lines = refs[-1]
    bands = out_ref.shape[1]
    halves, rows = lines.shape[:2]
    for image in range(out_ref.shape[0]):
        for half in range(halves):
            lines[half] = (
                in_ref[:, image, :, pl.ds(half * 128, 128)].astype(jnp.float32).reshape(rows, 128)
            )
        for band in range(bands):
            for half in range(halves):
                piece = lines[half, pl.ds(band, rows // bands, stride=bands), :]
                out_ref[image, band, pl.ds(half * 128, 128), :] = piece.T.astype(out_ref.dtype)

    @pl.when(pl.program_id(0) == 0)
    def _():
        base = 0
        for number, height in enumerate(heights):
            part = weight_ref[pl.ds(base, height), :]
            weight_out[number][...] = part
            base += height
        unpack_blocks(blocks, whole_ref, wide_out, len(whole_ref.shape) - 2)


def unturn_pixels(pixel_blocks, shape, weight_sums, heights, whole, wide_shapes):
    owners, images, share, slot = pixel_blocks.shape
    bands, pixel_count = shape[1], shape[3]
    model_dim = weight_sums.shape[1]
    blocks = wide_plan(wide_shapes, math.prod(whole.shape[:-2]))[0]

    def fixed(array_shape):
        return pl.BlockSpec(array_shape, lambda i: (0,) * len(array_shape))

    given = [(height, model_dim) for height in heights]
    given += wide_shapes
    return pl.pallas_call(
        functools.partial(unturn_kernel, blocks, heights),
        grid=(images // 2,),
        out_shape=[jax.ShapeDtypeStruct(shape, pixel_blocks.dtype)]
        + [jax.ShapeDtypeStruct(s, jnp.float32) for s in given],
        in_specs=[
            pl.BlockSpec((owners, 2, share, slot), lambda i: (0, i, 0, 0)),
            fixed(weight_sums.shape),
            fixed(whole.shape),
        ],
        out_specs=[pl.BlockSpec((2, bands, slot, pixel_count), lambda i: (i, 0, 0, 0))]
        + [fixed(s) for s in given],
        scratch_shapes=[pltpu.VMEM((slot // 128, pixel_count * bands, 128), jnp.float32)],
        compiler_params=pltpu.CompilerParams(vmem_limit_bytes=60 << 20),
    )(pixel_blocks, weight_sums, whole)


def at_band(place):
    return (place, lax.axis_index("tok"))


def pair_place():
    band = lax.axis_index("band")
    return lax.div(band, 2), lax.rem(band, 2)


def first_half(shape):
    return lax.rem(lax.broadcasted_iota(jnp.int32, shape, len(shape) - 2), 8) < 4


def make_kernel(factor, gen_ref, even_ref, odd_ref, kern_ref):
    model_dim = gen_ref.shape[1]
    pairs, _, owners, rows, _ = kern_ref.shape
    width = 256

    @pl.loop(0, model_dim // width)
    def _(part):
        columns = pl.ds(pl.multiple_of(part * width, width), width)
        pieces = []
        for offset in range(4):
            piece = lax.dot_general(
                (even_ref, odd_ref)[offset % 2][...],
                gen_ref[offset, columns, :],
                (((1,), (1,)), ((), ())),
                preferred_element_type=jnp.float32,
            )
            pieces.append((piece * factor).reshape(pairs * owners, 8, width))
        top = first_half(pieces[0].shape)
        even, odd = [], []
        for a, b in ((pieces[0], pieces[1]), (pieces[2], pieces[3])):
            even.append(jnp.where(top, a, b))
            odd.append(pltpu.roll(jnp.where(top, b, a), 4, 1))
        for parity, both in ((0, even), (1, odd)):
            block = jnp.concatenate(both, axis=1).astype(jnp.bfloat16)
            kern_ref[:, parity, :, :, columns] = block.reshape(pairs, owners, rows, width)


def make_kernels(gen_grid, even, odd, images, owners, factor):
    pixel_share, model_dim, hyper_dim = gen_grid.shape
    fixed = pl.BlockSpec(even.shape, lambda q: (0, 0))
    return pl.pallas_call(
        functools.partial(make_kernel, factor),
        grid=(pixel_share // 4,),
        out_shape=jax.ShapeDtypeStruct(
            (images // 2, 2, owners, pixel_share * 4, model_dim), jnp.bfloat16
        ),
        in_specs=[
            pl.BlockSpec((4, model_dim, hyper_dim), lambda q: (q, 0, 0)),
            fixed,
            fixed,
        ],
        out_specs=pl.BlockSpec(
            (images // 2, 2, owners, 16, model_dim), lambda q: (0, 0, 0, q, 0)
        ),
        compiler_params=pltpu.CompilerParams(vmem_limit_bytes=60 << 20),
        cost_estimate=pl.CostEstimate(
            flops=2 * gen_grid.size * even.shape[0],
            bytes_accessed=2 * gen_grid.size + 12 * 10**6,
            transcendentals=0,
        ),
    )(gen_grid, even, odd)


def embed_kernel(
    kern_hbm,
    pix_hbm,
    out_ref,
    pix_ref,
    kern_ref,
    y_out,
    y_in,
    z_out,
    z_in,
    kept,
    load_sem,
    y_send,
    y_recv,
    z_send,
    z_recv,
):
    pairs = kern_ref.shape[0]
    depth, side = pairs, lax.rem(lax.axis_index("band"), 2)
    place = lax.div(lax.axis_index("band"), 2)

    def loads(step, parity, number):
        pair = lax.rem(place + 1 + step, depth)
        image = pair * 2 + parity
        return (
            pltpu.make_async_copy(
                kern_hbm.at[pair, parity], kern_ref.at[pair, parity], load_sem.at[0, number, step]
            ),
            pltpu.make_async_copy(
                pix_hbm.at[:, image], pix_ref.at[:, image], load_sem.at[1, number, step]
            ),
        )

    for number, parity in enumerate((1 - side, side)):

        @pl.loop(0, depth)
        def _(step):
            for load in loads(step, parity, number):
                load.start()

    barrier = pltpu.get_barrier_semaphore()
    pl.semaphore_signal(
        barrier, inc=1, device_id=at_band(place * 2 + 1 - side), device_id_type=MESH
    )
    for step in range(depth - 1):
        target = lax.rem(place + 1 + step, depth)
        pl.semaphore_signal(
            barrier, inc=1, device_id=at_band(target * 2 + side), device_id_type=MESH
        )
    pl.semaphore_wait(barrier, depth)
    width = 256

    def conv(pair, parity, store):
        slot, inner = kern_ref.shape[3], pix_ref.shape[3]
        owners = kern_ref.shape[2]
        left = pix_ref[:, pair * 2 + parity].reshape(owners * slot, inner).T

        @pl.loop(0, kern_ref.shape[4] // width)
        def _(part):
            columns = pl.ds(pl.multiple_of(part * width, width), width)
            right = kern_ref[pair, parity, :, :, columns].reshape(owners * slot, width)
            store(
                part,
                columns,
                jnp.dot(left, right, preferred_element_type=jnp.float32),
            )

    def columns_of(part):
        return pl.ds(pl.multiple_of(part * width, width), width)

    parts = kern_ref.shape[4] // width

    def y_copy(step, part):
        return pltpu.make_async_remote_copy(
            src_ref=y_out.at[step, :, columns_of(part)],
            dst_ref=y_in.at[step, :, columns_of(part)],
            send_sem=y_send.at[step, part],
            recv_sem=y_recv.at[step, part],
            device_id=at_band(place * 2 + 1 - side),
            device_id_type=MESH,
        )

    def z_copy(step, part):
        return pltpu.make_async_remote_copy(
            src_ref=z_out.at[step, :, columns_of(part)],
            dst_ref=z_in.at[step, :, columns_of(part)],
            send_sem=z_send.at[step, part],
            recv_sem=z_recv.at[step, part],
            device_id=at_band(lax.rem(place + 1 + step, depth) * 2 + side),
            device_id_type=MESH,
        )

    @pl.loop(0, depth)
    def _(step):
        def store(part, columns, value):
            y_out[step, :, columns] = value.astype(y_out.dtype)
            y_copy(step, part).start()

        for load in loads(step, 1 - side, 0):
            load.wait()
        conv(lax.rem(place + 1 + step, depth), 1 - side, store)

    @pl.loop(0, depth)
    def _(step):
        def store(part, columns, value):
            kept[:, columns] = value

        for load in loads(step, side, 1):
            load.wait()
        conv(lax.rem(place + 1 + step, depth), side, store)

        @pl.loop(0, parts)
        def _(part):
            columns = columns_of(part)
            y_copy(step, part).wait_recv()
            total = kept[:, columns] + y_in[step, :, columns].astype(jnp.float32)

            @pl.when(step < depth - 1)
            def _():
                z_out[step, :, columns] = total.astype(z_out.dtype)
                z_copy(step, part).start()

            @pl.when(step == depth - 1)
            def _():
                out_ref[:, columns] = total

    @pl.loop(0, depth - 1)
    def _(step):
        @pl.loop(0, parts)
        def _(part):
            columns = columns_of(part)
            z_copy(step, part).wait_recv()
            out_ref[:, columns] += z_in[step, :, columns].astype(jnp.float32)

    @pl.loop(0, parts)
    def _(part):
        @pl.loop(0, depth)
        def _(step):
            y_copy(step, part).wait_send()

        @pl.loop(0, depth - 1)
        def _(step):
            z_copy(step, part).wait_send()


def embed_parts(kernels, pix, model_dim, collective_id):
    owners, images, share, slot = pix.shape
    depth = owners // 2
    low = jnp.bfloat16
    return pl.pallas_call(
        embed_kernel,
        out_shape=jax.ShapeDtypeStruct((slot, model_dim), jnp.float32),
        in_specs=[pl.BlockSpec(memory_space=pl.ANY)] * 2,
        out_specs=pl.BlockSpec(memory_space=pltpu.VMEM),
        scratch_shapes=[
            pltpu.VMEM(pix.shape, low),
            pltpu.VMEM(kernels.shape, low),
            pltpu.VMEM((depth, slot, model_dim), low),
            pltpu.VMEM((depth, slot, model_dim), low),
            pltpu.VMEM((depth - 1, slot, model_dim), low),
            pltpu.VMEM((depth - 1, slot, model_dim), low),
            pltpu.VMEM((slot, model_dim), jnp.float32),
            pltpu.SemaphoreType.DMA((2, 2, depth)),
            pltpu.SemaphoreType.DMA((depth, model_dim // 256)),
            pltpu.SemaphoreType.DMA((depth, model_dim // 256)),
            pltpu.SemaphoreType.DMA((depth - 1, model_dim // 256)),
            pltpu.SemaphoreType.DMA((depth - 1, model_dim // 256)),
        ],
        compiler_params=pltpu.CompilerParams(
            collective_id=collective_id, has_side_effects=True, vmem_limit_bytes=60 << 20
        ),
        cost_estimate=pl.CostEstimate(
            flops=10**10, bytes_accessed=12 * 10**7, transcendentals=0
        ),
    )(kernels, pix)


def tail_kernel(factor, plan, *refs):
    streams, dims, blocks, used = plan["streams"], plan["dims"], plan["blocks"], plan["used"]
    count, stages = len(streams), len(dims)
    bulk = plan["bulk"]
    refs = list(refs)

    def take(number):
        taken = refs[:number]
        del refs[:number]
        return taken

    gen_hbm, pix_hbm, kern_hbm = take(3)
    active_hbm, down_hbm, middle_hbm = take(3)
    weights_in = take(bulk)
    low_ref, even_ref, odd_ref, feature_ref, token_ref, bias_grad_ref = take(6)
    params = take(8)
    gen_b_grad, gain_lines = take(2)
    (pixel_land,) = take(1)
    outputs = take(2)
    whole, layer_ref = take(2)
    gen_ref, pix_ref, kern_ref, gath, stage_ref, part_ref, part_in, wide_ref = take(8)
    expand_ref, shrink_ref = take(2)
    own = take(2)
    landing = [take(len(stream["order"])) for stream in streams]
    (packed,) = take(1)
    load_sem, near_send, far_send, relay_send, onward_send = take(5)
    block_recv, part_send, part_recv = take(3)
    send_sem, recv_sem, own_sem, gather_send, gather_recv = take(5)
    pixel_send, pixel_recv, pixel_own = take(3)
    sum_in, sum_send, sum_recv, share_send, share_recv, out_buffer, out_sem = take(7)
    layer_total, layer_sem = take(2)

    depth = kern_ref.shape[0]
    owners, share = kern_ref.shape[2], kern_ref.shape[3]
    slot, model_dim = low_ref.shape
    place, side = pair_place()
    mine = place * 2 + side
    beside = place * 2 + 1 - side
    dk_ref = kern_ref.reshape(depth, gen_ref.shape[0] // 2, 2, owners * 8, model_dim)
    tok_dims = [d for d in dims if d[0] == "tok"]
    loads = [
        pltpu.make_async_copy(gen_hbm, gen_ref, load_sem.at[0]),
        pltpu.make_async_copy(pix_hbm, pix_ref, load_sem.at[1]),
        pltpu.make_async_copy(params[4], expand_ref, load_sem.at[2]),
        pltpu.make_async_copy(params[5], shrink_ref, load_sem.at[3]),
        pltpu.make_async_copy(kern_hbm, kern_ref, load_sem.at[4]),
    ]
    for load in loads:
        load.start()
    barrier = pltpu.get_barrier_semaphore()
    for step in range(1, owners):
        pl.semaphore_signal(
            barrier,
            inc=1,
            device_id=at_band(lax.rem(mine + step, owners)),
            device_id_type=MESH,
        )
    for axis, bit in tok_dims:
        pl.semaphore_signal(barrier, inc=1, device_id=partner_of(axis, bit), device_id_type=MESH)
    pl.semaphore_wait(barrier, owners - 1 + len(tok_dims))

    def block_copy(source, block, target, sem):
        return pltpu.make_async_remote_copy(
            src_ref=source,
            dst_ref=gath.at[block],
            send_sem=sem,
            recv_sem=block_recv.at[block],
            device_id=at_band(target),
            device_id_type=MESH,
        )

    near = block_copy(low_ref, mine, beside, near_send)
    has_right, has_left = place + 1 < depth, place > 0

    def to_right():
        return block_copy(low_ref, mine, mine + 2, far_send.at[0])

    def to_left():
        return block_copy(low_ref, mine, mine - 2, far_send.at[1])

    @pl.when(has_right)
    def _():
        to_right().start()

    @pl.when(has_left)
    def _():
        to_left().start()

    near.start()
    bits = (2,) * len(tok_dims)
    segments = gen_ref.reshape(bits + (gen_ref.shape[0] * model_dim >> len(bits), gen_ref.shape[2]))
    sums = Sums(
        streams,
        weights_in + [segments, packed],
        outputs,
        own,
        landing,
        send_sem,
        recv_sem,
        own_sem,
        (out_buffer, out_sem),
    )
    heavy = [s for s in range(count) if streams[s]["source"] < bulk]
    slices = [s for s in range(count) if streams[s]["source"] == bulk]
    light = count - 1
    for stream in heavy:
        sums.begin(stream)
    for stream in heavy[:2]:
        sums.fetch(stream)
    gath[mine] = low_ref[...]
    width = 256

    def pair_at(step):
        number = step - 1
        left, right = place, depth - 1 - place
        both = jnp.minimum(left, right)
        turn = jnp.where(lax.rem(number, 2) == 0, -1, 1) * (lax.div(number, 2) + 1)
        rest = jnp.where(right > left, 1, -1) * (number - both + 1)
        offset = jnp.where(number < 2 * both, turn, rest)
        return jnp.where(step == 0, place, place + offset)

    def relay(step):
        block = pair_at(step) * 2 + side
        return block_copy(gath.at[block], block, beside, relay_send.at[step - 1])

    def onward(step, act):
        pair = pair_at(step)
        block = pair * 2 + side
        ahead = jnp.where(pair < place, mine + 2, mine - 2)

        @pl.when(jnp.where(pair < place, place + 1 < depth, place > 0))
        def _():
            act(block_copy(gath.at[block], block, ahead, onward_send.at[step - 1]))

    def pixel_copy(image, step):
        target = lax.rem(mine + step, owners)
        return pltpu.make_async_remote_copy(
            src_ref=pix_ref.at[target, image],
            dst_ref=pixel_land.at[mine, image],
            send_sem=pixel_send.at[image, step - 1],
            recv_sem=pixel_recv.at[image, step - 1],
            device_id=at_band(target),
            device_id_type=MESH,
        )

    def pixel_local(image):
        return pltpu.make_async_copy(
            pix_ref.at[mine, image], pixel_land.at[mine, image], pixel_own.at[image]
        )

    def pair_work(pair):
        for parity in range(2):
            image = pair * 2 + parity
            rows = kern_ref[pair, parity].reshape(owners * share, model_dim)
            turned = lax.dot_general(
                rows, gath[image], (((1,), (1,)), ((), ())), preferred_element_type=jnp.float32
            )
            stage_ref[parity] = turned.astype(stage_ref.dtype).reshape(owners, share, slot)

        @pl.loop(0, model_dim // width)
        def _(part):
            columns = pl.ds(pl.multiple_of(part * width, width), width)
            both = []
            for parity in range(2):
                left = pix_ref[:, pair * 2 + parity].reshape(owners * share, slot)
                both.append(
                    jnp.dot(
                        left,
                        gath[pair * 2 + parity, :, columns],
                        preferred_element_type=jnp.float32,
                    ).reshape(owners * share // 8, 8, width)
                )
            even, odd = both[0], pltpu.roll(both[1], 4, 1)
            top = first_half(even.shape)
            for parity, value in (
                (0, jnp.where(top, even, odd)),
                (1, jnp.where(top, odd, even)),
            ):
                value = value.reshape(owners, share // 8, 8, width).transpose(1, 0, 2, 3)
                value = value.reshape(share // 8, owners * 8, width)
                dk_ref[pair, :, parity, :, columns] = value.astype(dk_ref.dtype)

        for parity in range(2):
            image = pair * 2 + parity
            pix_ref[:, image] = stage_ref[parity]
            pixel_local(image).start()

    def pixel_send_pair(pair):
        for parity in range(2):

            @pl.loop(1, owners)
            def _(step):
                pixel_copy(pair * 2 + parity, step).start()

    done = 0
    for step in range(1, depth):
        block_copy(low_ref, pair_at(step) * 2 + side, beside, near_send).wait_recv()
        onward(step, lambda copy: copy.start())
        relay(step).start()
        until = len(heavy) if step >= depth - 2 else len(heavy) * step // (depth - 2)
        for stream in heavy[done:until]:
            sums.advance(stream, 0)
            if stream + 2 < len(heavy):
                sums.fetch(stream + 2)
        done = max(done, until)
    hyper_dim = feature_ref.shape[1]
    bands = feature_ref.shape[0]
    first_row = lax.broadcasted_iota(jnp.int32, (8, hyper_dim), 0) == 0
    tokens = jnp.concatenate(
        [feature_ref[...], jnp.where(first_row, token_ref[...], 0.0)], axis=0
    )
    wide_width = 512
    attention = tuple(params[number][...] for number in (0, 1, 2, 3, 6))
    segment, segment_back = jax.vjp(
        lambda t, p: hyper_attention(t, p, 1), tokens, attention
    )
    loads[2].wait()
    loads[3].wait()
    hyper_wide(segment, expand_ref, shrink_ref, wide_ref, wide_width)
    norm_back = jax.vjp(
        lambda v, g: layer_norm(v, g, EPS_HYPER), wide_ref[...], params[7][...]
    )[1]

    loads[1].wait()
    loads[4].wait()

    @pl.loop(0, depth)
    def _(step):
        pair = pair_at(step)

        @pl.when(step == depth - 1)
        def _():
            pixel_send_pair(place)

        block_copy(low_ref, pair * 2 + 1 - side, beside, near_send).wait_recv()
        pair_work(pair)

    waiting = [pair_at(step) for step in range(1, depth)]

    layer_chunks = down_hbm.shape[0] // model_dim
    high = model_dim // slot

    def layer_copies(chunk):
        half = lax.rem(chunk, 2)
        base = half * (high + 1)
        rows = pl.ds(pl.multiple_of(chunk * model_dim, model_dim), model_dim)
        copies = [
            pltpu.make_async_copy(
                active_hbm.at[:, rows], gath.at[base + high], layer_sem.at[0, half]
            ),
            pltpu.make_async_copy(
                down_hbm.at[rows].reshape(high, slot, model_dim),
                gath.at[pl.ds(base, high)],
                layer_sem.at[1, half],
            ),
        ]
        return copies, base

    def layer_output():
        for step in range(1, depth):
            relay(step).wait_send()
            onward(step, lambda copy: copy.wait_send())
        first = pltpu.make_async_copy(middle_hbm, layer_total, layer_sem.at[2, 0])
        first.start()
        for copy in layer_copies(0)[0]:
            copy.start()
        first.wait()

        @pl.loop(0, layer_chunks)
        def _(chunk):
            @pl.when(chunk + 1 < layer_chunks)
            def _():
                for copy in layer_copies(chunk + 1)[0]:
                    copy.start()

            copies, base = layer_copies(chunk)
            for copy in copies:
                copy.wait()
            layer_total[...] += jnp.dot(
                gath[base + high],
                gath[pl.ds(base, high)].reshape(model_dim, model_dim),
                preferred_element_type=jnp.float32,
            )

        layer_ref[...] = layer_total[...].astype(layer_ref.dtype)
    loads[0].wait()
    part_ref[...] = jnp.zeros_like(part_ref)

    def dk_rows(duo, parity):
        return dk_ref[:, duo, parity].reshape(depth * owners * 8, model_dim)

    @pl.loop(0, dk_ref.shape[1])
    def _(duo):
        for parity in range(2):
            part_ref[parity] += jnp.dot(
                dk_rows(duo, parity),
                gen_ref[duo * 2 + parity],
                preferred_element_type=jnp.float32,
            ).reshape(depth, owners * 8, -1)

    part_ref[...] = part_ref[...] * factor

    def part_copy(step):
        target = lax.rem(mine + step, owners)
        return pltpu.make_async_remote_copy(
            src_ref=part_ref.at[:, lax.div(target, 2)],
            dst_ref=part_in.at[step - 1],
            send_sem=part_send.at[step - 1],
            recv_sem=part_recv.at[step - 1],
            device_id=at_band(target),
            device_id_type=MESH,
        )

    copies = [part_copy(step) for step in range(1, owners)]
    for copy in copies:
        copy.start()
    pixel_send_pair(waiting.pop(0))

    @pl.loop(0, dk_ref.shape[1])
    def _(duo):
        for parity in range(2):
            weight = lax.dot_general(
                dk_rows(duo, parity),
                (even_ref, odd_ref)[parity][...],
                (((0,), (0,)), ((), ())),
                preferred_element_type=jnp.float32,
            )
            gen_ref[duo * 2 + parity] = weight.astype(gen_ref.dtype)

    for stream in slices:
        sums.begin(stream)
    early = len(heavy) // 2
    for stream in heavy[:early]:
        sums.advance(stream, 1)
    total = part_ref[:, place]
    for step, copy in enumerate(copies):
        copy.wait_recv()
        total += part_in[step]
    rows = total.shape[1]
    half = jnp.where(side == 0, 0.0, 1.0)
    even_part = total[0].reshape(owners, 8, -1)
    odd_part = total[1].reshape(owners, 8, -1)
    low_rows = even_part + pltpu.roll(odd_part, 4, 1)
    low_rows = jnp.where(side == 0, low_rows, pltpu.roll(low_rows, 4, 1))
    low_rows = low_rows.reshape(rows, -1)
    chooser = (
        lax.broadcasted_iota(jnp.int32, (bands, rows), 1)
        == lax.div(lax.broadcasted_iota(jnp.int32, (bands, rows), 0), 4) * 8
        + lax.rem(lax.broadcasted_iota(jnp.int32, (bands, rows), 0), 4)
    ).astype(jnp.float32)
    d_band = precise_dot(chooser, low_rows)
    cotangent = jnp.concatenate(
        [d_band, jnp.where(first_row, bias_grad_ref[...], 0.0)], axis=0
    )
    d_total, second_grad = norm_back(cotangent)
    hyper_wide_back(segment, d_total, expand_ref, shrink_ref, wide_ref, wide_width)
    token_grad, param_grads = segment_back(wide_ref[...])
    small = [param_grads[0], param_grads[1], param_grads[2], param_grads[3]]
    line_row = lax.broadcasted_iota(jnp.int32, gain_lines.shape, 0)
    lines = gain_lines[...]
    for row, value in enumerate((token_grad[bands : bands + 1], param_grads[4], second_grad)):
        lines = jnp.where(line_row == row, value, lines)

    def of_value(value):
        return lambda r, c: value[
            r.start : r.start + r.size, c.start : c.start + c.size
        ]

    def of_ref(ref):
        return lambda r, c: ref[r, c]

    wide = [of_value(value) for value in small]
    wide += [of_ref(expand_ref), of_ref(shrink_ref), of_ref(gen_b_grad), of_value(lines)]
    pack_blocks(blocks, used, packed, wide, stages)
    sums.begin(light)
    sums.advance(light, 0)
    for stream in slices:
        sums.advance(stream, 0)
    while len(waiting) > 1:
        pixel_send_pair(waiting.pop(0))
    sums.advance(light, len(tok_dims) - 1)
    for stream in heavy[early:]:
        sums.advance(stream, 1)
    sums.advance(light, len(tok_dims))
    piece = packed.shape[-2]
    quarter = landing[light][-1].reshape(depth, piece, 128)

    def sum_copy(step):
        target = lax.rem(place + step, depth)
        return pltpu.make_async_remote_copy(
            src_ref=quarter.at[target],
            dst_ref=sum_in.at[step - 1],
            send_sem=sum_send.at[step - 1],
            recv_sem=sum_recv.at[step - 1],
            device_id=at_band(target * 2 + side),
            device_id_type=MESH,
        )

    own_tok = tuple(own_bit(*d) for d in tok_dims)
    spread_view = whole.reshape((owners,) + bits + (piece, 128))

    def share_copy(block, target, step):
        return pltpu.make_async_remote_copy(
            src_ref=spread_view.at[(block,) + own_tok],
            dst_ref=spread_view.at[(block,) + own_tok],
            send_sem=share_send.at[step - 1],
            recv_sem=share_recv.at[step - 1],
            device_id=at_band(target),
            device_id_type=MESH,
        )

    moves = [sum_copy(step) for step in range(1, depth)]
    for copy in moves:
        copy.start()
    pixel_send_pair(waiting.pop(0))
    for stream in heavy:
        sums.advance(stream, 2)
    light_total = quarter[place].astype(jnp.float32)
    for step, copy in enumerate(moves):
        copy.wait_recv()
        light_total += sum_in[step].astype(jnp.float32)
    spread_view[(mine,) + own_tok] = light_total.astype(whole.dtype)
    shares = [
        share_copy(mine, lax.rem(place + step, depth) * 2 + side, step)
        for step in range(1, depth)
    ]
    for copy in shares:
        copy.start()
    layer_output()
    for stage in range(3, stages):
        for stream in heavy:
            sums.advance(stream, stage)
    for step in range(1, depth):
        source = lax.rem(place + depth - step, depth) * 2 + side
        share_copy(source, source, step).wait_recv()
    spread = Spread(dims, streams[light]["order"], whole, gather_send, gather_recv)
    for step in range(len(tok_dims) + 1):
        spread.start()
        if step == 0:
            for stream in slices:
                sums.advance(stream, 1)
        spread.finish()
    for copy in moves + shares:
        copy.wait_send()

    @pl.loop(0, depth * 2)
    def _(image):
        pixel_local(image).wait()

        @pl.loop(1, owners)
        def _(step):
            source = lax.rem(mine + owners - step, owners)
            pltpu.make_async_remote_copy(
                src_ref=pix_ref.at[source, image],
                dst_ref=pixel_land.at[source, image],
                send_sem=pixel_send.at[image, step - 1],
                recv_sem=pixel_recv.at[image, step - 1],
                device_id=at_band(source),
                device_id_type=MESH,
            ).wait()

    for copy in copies + [near]:
        copy.wait_send()

    @pl.when(has_right)
    def _():
        to_right().wait_send()

    @pl.when(has_left)
    def _():
        to_left().wait_send()

    sums.drain()


def tail_call(
    gen_grid,
    pix,
    kernels,
    layer_parts,
    low_own,
    even,
    odd,
    weights,
    features,
    token,
    bias_grad,
    params,
    gen_b_grad,
    gain_lines,
    factor,
    collective_id,
):
    dims, band_bits, tok_bits = mesh_bits()
    everything = len(dims)
    low = jnp.bfloat16
    owners, images, share, slot = pix.shape
    depth = owners // 2
    pixel_share, model_dim, hyper_dim = gen_grid.shape
    rows = owners * 8
    split, outs, landing, streams = [], [], [], []
    order = halving_order(0, band_bits, tok_bits)
    tallest, base = 0, 0
    for k, weight in enumerate(weights):
        height = weight.shape[0] >> everything
        split.append(weight.reshape((2,) * everything + (height, weight.shape[1])))
        for start, size in row_chunks(height, 3 if height > 32 else 1):
            streams.append(stream_entry(k, 0, start, size, order, dims, True))
            streams[-1]["base"] = base
            landing += landing_shapes(streams[-1], weight.shape[1])
            tallest = max(tallest, size)
        base += height
    outs.append(jax.ShapeDtypeStruct((base, model_dim), jnp.float32))
    bulk = len(weights)
    tok_order = halving_order(2, band_bits, tok_bits)
    height = pixel_share * model_dim >> tok_bits
    outs.append(jax.ShapeDtypeStruct((height, hyper_dim), jnp.float32))
    for start, size in row_chunks(height, 4):
        out_rows = size
        streams.append(stream_entry(bulk, 1, start, size, tok_order, dims, False, factor))
        landing += landing_shapes(streams[-1], hyper_dim)
    wide_shapes = [p.shape for p in params[:6]] + [gen_b_grad.shape, gain_lines.shape]
    blocks, used, piece = wide_plan(wide_shapes, 1 << everything)
    near_order = tok_order + [("band", 0)]
    light = stream_entry(bulk + 1, None, 0, piece, near_order, dims, False)
    light["span"] = dims
    streams.append(light)
    landing += [
        pltpu.VMEM((2,) * (everything - 1 - stage) + (piece, 128), low)
        for stage in range(len(near_order))
    ]
    count = len(streams)
    plan = {"streams": streams, "dims": dims, "bulk": bulk, "blocks": blocks, "used": used}
    space = (2,) * everything + (piece, 128)
    own = pltpu.VMEM((2,) * (everything - 1) + (tallest, model_dim), low)
    dma = pltpu.SemaphoreType.DMA
    return pl.pallas_call(
        functools.partial(tail_kernel, factor, plan),
        out_shape=[jax.ShapeDtypeStruct(pix.shape, low)]
        + outs
        + [jax.ShapeDtypeStruct(space, low), jax.ShapeDtypeStruct((slot, model_dim), low)],
        in_specs=[pl.BlockSpec(memory_space=pl.ANY)] * (6 + bulk)
        + [pl.BlockSpec(memory_space=pltpu.VMEM)] * 10
        + [pl.BlockSpec(memory_space=pl.ANY)] * 2
        + [pl.BlockSpec(memory_space=pltpu.VMEM)] * 4,
        out_specs=[pl.BlockSpec(memory_space=pl.ANY)]
        + [
            pl.BlockSpec(memory_space=pltpu.VMEM),
            pl.BlockSpec(memory_space=pl.ANY),
            pl.BlockSpec(memory_space=pltpu.VMEM),
            pl.BlockSpec(memory_space=pltpu.VMEM),
        ],
        scratch_shapes=[
            pltpu.VMEM(gen_grid.shape, low),
            pltpu.VMEM(pix.shape, low),
            pltpu.VMEM((images // 2, 2, owners, share, model_dim), low),
            pltpu.VMEM((images, slot, model_dim), low),
            pltpu.VMEM((2, owners, share, slot), low),
            pltpu.VMEM((2, depth, rows, hyper_dim), jnp.float32),
            pltpu.VMEM((owners - 1, 2, rows, hyper_dim), jnp.float32),
            pltpu.VMEM((features.shape[0] + 8, hyper_dim), jnp.float32),
            pltpu.VMEM(params[4].shape, jnp.float32),
            pltpu.VMEM(params[5].shape, jnp.float32),
            own,
            own,
        ]
        + landing
        + [
            pltpu.VMEM(space, low),
            dma((5,)),
            dma,
            dma((2,)),
            dma((depth - 1,)),
            dma((depth - 1,)),
            dma((owners,)),
            dma((owners - 1,)),
            dma((owners - 1,)),
            dma((count, everything)),
            dma((count, everything)),
            dma((2,)),
            dma((everything,)),
            dma((everything,)),
            dma((images, owners - 1)),
            dma((images, owners - 1)),
            dma((images,)),
            pltpu.VMEM((depth - 1, piece, 128), low),
            dma((depth - 1,)),
            dma((depth - 1,)),
            dma((depth - 1,)),
            dma((depth - 1,)),
            pltpu.VMEM((out_rows, hyper_dim), jnp.float32),
            dma,
            pltpu.VMEM((slot, model_dim), jnp.float32),
            dma((3, 2)),
        ],
        compiler_params=pltpu.CompilerParams(
            collective_id=collective_id, has_side_effects=True, vmem_limit_bytes=63 << 20
        ),
        cost_estimate=pl.CostEstimate(
            flops=2 * 10**10, bytes_accessed=3 * 10**8, transcendentals=0
        ),
    )(
        gen_grid,
        pix,
        kernels,
        *layer_parts,
        *split,
        low_own,
        even,
        odd,
        features,
        token,
        bias_grad,
        *params,
        gen_b_grad,
        gain_lines,
    )


def layer_norm(values, scaling, epsilon):
    center = values - jnp.mean(values, axis=-1, keepdims=True)
    spread = jnp.mean(center * center, axis=-1, keepdims=True)
    return center * lax.rsqrt(spread + epsilon) * scaling


def block_norm(values, scaling):
    return layer_norm(values, scaling, EPS_BLOCK)


def exact_gelu(values):
    return 0.5 * values * (1.0 + lax.erf(values * math.sqrt(0.5)))


def wave_features(lengths, model_dim):
    middle = model_dim // 2
    angular = 1.0 / 10000.0 ** (jnp.arange(middle, dtype=jnp.float32) / middle)
    phases = (100.0 * lengths)[..., None] * angular
    return jnp.concatenate([jnp.sin(phases), jnp.cos(phases)], axis=-1)


def hyper_layer(features, params):
    (
        bias_token,
        hyper_query,
        hyper_key,
        hyper_value,
        hyper_out,
        hyper_up,
        hyper_down,
        hyper_gain1,
        hyper_gain2,
    ) = params
    images = features.shape[0]
    model_dim = features.shape[-1]
    head_size = model_dim // HHEADS
    tokens = jnp.concatenate(
        [features, jnp.broadcast_to(bias_token, (images, 1, model_dim))], axis=1
    )
    length = tokens.shape[1]
    queries = jnp.einsum("nsc,ce->nse", tokens, hyper_query, precision=PRECISE).reshape(
        images, length, HHEADS, head_size
    )
    keys_all = jnp.einsum("nsc,ce->nse", tokens, hyper_key, precision=PRECISE).reshape(
        images, length, HHEADS, head_size
    )
    values_all = jnp.einsum("nsc,ce->nse", tokens, hyper_value, precision=PRECISE).reshape(
        images, length, HHEADS, head_size
    )
    scores = jnp.einsum("nshe,nthe->nhst", queries, keys_all, precision=PRECISE) / math.sqrt(
        head_size
    )
    weights = jax.nn.softmax(scores, axis=-1)
    blended = jnp.einsum("nhst,nthe->nshe", weights, values_all, precision=PRECISE).reshape(
        images, length, model_dim
    )
    segment_one = layer_norm(
        tokens + jnp.einsum("nse,ef->nsf", blended, hyper_out, precision=PRECISE),
        hyper_gain1,
        EPS_HYPER,
    )
    expanded = jax.nn.gelu(
        jnp.einsum("nse,ef->nsf", segment_one, hyper_up, precision=PRECISE), approximate=False
    )
    second = layer_norm(
        segment_one + jnp.einsum("nsf,fe->nse", expanded, hyper_down, precision=PRECISE),
        hyper_gain2,
        EPS_HYPER,
    )
    return (second[:, :-1, :], second[:, -1, :])


def precise_dot(left, right, contract=(1, 0)):
    return lax.dot_general(
        left,
        right,
        (((contract[0],), (contract[1],)), ((), ())),
        precision=PRECISE,
        preferred_element_type=jnp.float32,
    )


def hyper_attention(tokens, params, images):
    query, key, value, mix, first = params
    rows, hyper_dim = tokens.shape
    bands = (rows - 8 * -(-images // 8)) // images
    head = hyper_dim // HHEADS

    def owner(index):
        return jnp.where(index < images * bands, lax.div(index, bands), index - images * bands)

    same = owner(lax.broadcasted_iota(jnp.int32, (rows, rows), 0)) == owner(
        lax.broadcasted_iota(jnp.int32, (rows, rows), 1)
    )
    lane = lax.div(lax.broadcasted_iota(jnp.int32, (1, hyper_dim), 1), head)
    queries = precise_dot(tokens, query) * (1.0 / math.sqrt(head))
    keys_all = precise_dot(tokens, key)
    values_all = precise_dot(tokens, value)
    blended = None
    for place in range(HHEADS):
        chosen = (lane == place).astype(jnp.float32)
        scores = precise_dot(queries * chosen, keys_all, (1, 1))
        scores = jnp.where(same, scores, -1e30)
        highest = lax.stop_gradient(jnp.max(scores, axis=-1, keepdims=True))
        lifted = jnp.exp(scores - highest)
        weights = lifted / jnp.sum(lifted, axis=-1, keepdims=True)
        part = precise_dot(weights, values_all * chosen)
        blended = part if blended is None else blended + part
    return layer_norm(tokens + precise_dot(blended, mix), first, EPS_HYPER)


def hyper_wide(segment, expand_ref, shrink_ref, total_ref, width):
    total_ref[...] = segment

    @pl.loop(0, expand_ref.shape[1] // width)
    def _(part):
        columns = pl.ds(pl.multiple_of(part * width, width), width)
        wide = precise_dot(segment, expand_ref[:, columns])
        active = 0.5 * wide * (1.0 + lax.erf(wide * math.sqrt(0.5)))
        total_ref[...] += precise_dot(active, shrink_ref[columns, :])


def hyper_wide_back(segment, d_total, expand_ref, shrink_ref, d_segment_ref, width):
    d_segment_ref[...] = d_total

    @pl.loop(0, expand_ref.shape[1] // width)
    def _(part):
        columns = pl.ds(pl.multiple_of(part * width, width), width)
        wide = precise_dot(segment, expand_ref[:, columns])
        bell = 0.5 * (1.0 + lax.erf(wide * math.sqrt(0.5)))
        slope = bell + wide * jnp.exp(-0.5 * wide * wide) * (1.0 / math.sqrt(2.0 * math.pi))
        d_wide = precise_dot(d_total, shrink_ref[columns, :], (1, 1)) * slope
        d_segment_ref[...] += precise_dot(d_wide, expand_ref[:, columns], (1, 1))
        shrink_ref[columns, :] = precise_dot(wide * bell, d_total, (0, 0))
        expand_ref[:, columns] = precise_dot(segment, d_wide, (0, 0))


def contract_rows(left_side, right_side):
    return lax.dot_general(
        left_side, right_side, (((0,), (0,)), ((), ())), preferred_element_type=jnp.float32
    )


def contract_cols(left_side, right_side):
    return lax.dot_general(
        left_side, right_side, (((1,), (1,)), ((), ())), preferred_element_type=jnp.float32
    )


def attention_scores(queries, keys_low, usable):
    head_size = queries.shape[-1]
    scores = jnp.einsum(
        "iqhe,ikhe->ihqk", queries, keys_low, preferred_element_type=jnp.float32
    ) / math.sqrt(head_size)
    return jnp.where(usable[:, None, None, :], scores, -1e30)


def block_forward(embedded, usable, weights_full, ln1_gain, ln2_gain):
    w_qkv_full, w_out_full, w_up_full, w_down_full = weights_full
    images, slot_count, model_dim = embedded.shape
    row_count = images * slot_count
    head_count = model_dim // HD
    flat_rows = embedded.reshape(row_count, model_dim)
    normed_one = block_norm(flat_rows, ln1_gain).astype(jnp.bfloat16)
    qkv_low = jnp.dot(normed_one, w_qkv_full, preferred_element_type=jnp.float32).astype(
        jnp.bfloat16
    )
    sections = qkv_low.reshape(images, slot_count, 3, head_count, HD)
    queries = sections[:, :, 0]
    keys_low = sections[:, :, 1]
    values_low = sections[:, :, 2]
    scores = attention_scores(queries, keys_low, usable)
    highest = jnp.max(scores, axis=-1, keepdims=True)
    lifted = jnp.exp(scores - highest)
    totals = jnp.sum(lifted, axis=-1, keepdims=True)
    attn_probs = (lifted / totals).astype(jnp.bfloat16)
    log_mass = highest + jnp.log(totals)
    attended = (
        jnp.einsum("ihqk,ikhe->iqhe", attn_probs, values_low, preferred_element_type=jnp.float32)
        .astype(jnp.bfloat16)
        .reshape(row_count, model_dim)
    )
    middle = flat_rows + jnp.dot(attended, w_out_full, preferred_element_type=jnp.float32)
    normed_two = block_norm(middle, ln2_gain).astype(jnp.bfloat16)
    hidden = jnp.dot(normed_two, w_up_full, preferred_element_type=jnp.float32)
    active = exact_gelu(hidden).astype(jnp.bfloat16)
    output = middle + jnp.dot(active, w_down_full, preferred_element_type=jnp.float32)
    return (
        flat_rows,
        normed_one,
        queries,
        keys_low,
        values_low,
        log_mass,
        attended,
        middle,
        normed_two,
        hidden,
        active,
        output,
    )


def block_backward(stored, usable, grad_rows, weights_full, ln1_gain, ln2_gain):
    (
        flat_rows,
        normed_one,
        queries,
        keys_low,
        values_low,
        log_mass,
        attended,
        middle,
        normed_two,
        hidden,
        active,
        output,
    ) = stored
    w_qkv_full, w_out_full, w_up_full, w_down_full = weights_full
    images, slot_count, head_count, head_size = queries.shape
    row_count, model_dim = flat_rows.shape
    grad_low = grad_rows.astype(jnp.bfloat16)
    grad_down = contract_rows(active, grad_low)
    d_active = contract_cols(grad_low, w_down_full)
    gelu_back = jax.vjp(exact_gelu, hidden)[1]
    d_hidden = gelu_back(d_active)[0].astype(jnp.bfloat16)
    grad_up_turned = contract_rows(d_hidden, normed_two)
    d_normed_two = contract_cols(d_hidden, w_up_full)
    norm_back_two = jax.vjp(block_norm, middle, ln2_gain)[1]
    d_middle_norm, grad_gain_two = norm_back_two(d_normed_two)
    d_middle = grad_rows + d_middle_norm
    d_middle_low = d_middle.astype(jnp.bfloat16)
    grad_out_turned = contract_rows(d_middle_low, attended)
    d_attended = (
        contract_cols(d_middle_low, w_out_full)
        .astype(jnp.bfloat16)
        .reshape(images, slot_count, head_count, head_size)
    )
    scores = attention_scores(queries, keys_low, usable)
    attn_float = jnp.exp(scores - log_mass)
    attn_probs = attn_float.astype(jnp.bfloat16)
    d_values = jnp.einsum(
        "ihqk,iqhe->ikhe", attn_probs, d_attended, preferred_element_type=jnp.float32
    ).astype(jnp.bfloat16)
    d_probs = jnp.einsum(
        "iqhe,ikhe->ihqk", d_attended, values_low, preferred_element_type=jnp.float32
    )
    d_scores = (
        attn_float * (d_probs - jnp.sum(attn_float * d_probs, axis=-1, keepdims=True))
    ).astype(jnp.bfloat16)
    d_queries = (
        jnp.einsum("ihqk,ikhe->iqhe", d_scores, keys_low, preferred_element_type=jnp.float32)
        / math.sqrt(head_size)
    ).astype(jnp.bfloat16)
    d_keys = (
        jnp.einsum("ihqk,iqhe->ikhe", d_scores, queries, preferred_element_type=jnp.float32)
        / math.sqrt(head_size)
    ).astype(jnp.bfloat16)
    d_qkv = jnp.stack([d_queries, d_keys, d_values], axis=2).reshape(row_count, 3 * model_dim)
    grad_qkv_turned = contract_rows(d_qkv, normed_one)
    d_normed_one = contract_cols(d_qkv, w_qkv_full)
    norm_back_one = jax.vjp(block_norm, flat_rows, ln1_gain)[1]
    d_flat, grad_gain_one = norm_back_one(d_normed_one)
    return (
        d_middle + d_flat,
        (grad_qkv_turned, grad_out_turned, grad_up_turned, grad_down, grad_gain_one, grad_gain_two),
    )


def body(
    pixels,
    wave_table,
    wave_index,
    patch_count,
    d_out,
    gen_w,
    gen_b,
    bias_token,
    hyper_query,
    hyper_key,
    hyper_value,
    hyper_out,
    hyper_up,
    hyper_down,
    hyper_gain1,
    hyper_gain2,
    w_qkv,
    w_out,
    w_up,
    w_down,
    ln1_gain,
    ln2_gain,
):
    group_images, band_share, slot_count, pixel_count = pixels.shape[1:]
    own_images = patch_count.shape[1]
    model_dim = w_out.shape[0]
    hyper_dim = gen_w.shape[1]
    all_bands = wave_index.shape[2]
    owners = lax.axis_size("band")
    slice_pixels = pixel_count // owners
    factor = 1.0 / math.sqrt(all_bands * pixel_count)
    band_place = lax.axis_index("band")
    hyper_params = (
        bias_token,
        hyper_query,
        hyper_key,
        hyper_value,
        hyper_out,
        hyper_up,
        hyper_down,
        hyper_gain1,
        hyper_gain2,
    )
    paired = (
        band_share == 4
        and own_images == 1
        and group_images == owners
        and owners % 2 == 0
        and slice_pixels % 4 == 0
        and model_dim % 256 == 0
        and model_dim // slot_count + 1 == group_images // 2
        and model_dim % slot_count == 0
        and w_down.shape[0] * lax.axis_size("tok") % model_dim == 0
    )
    if paired:
        pixel_lined = lax.all_to_all(turn_pixels(pixels[0], owners), "band", 0, 0, tiled=True)
    else:
        pixel_turned = (
            pixels[0]
            .reshape(group_images, band_share, slot_count, owners, slice_pixels)
            .transpose(3, 0, 4, 1, 2)
        )
        pixel_blocks = lax.all_to_all(pixel_turned, "band", 0, 0, tiled=True)
    gen_part = lax.all_gather(gen_w, "tok", axis=0, tiled=True)
    gen_grid = gen_part.reshape(slice_pixels, model_dim, hyper_dim)
    weights_full = (
        lax.all_gather(w_qkv, "tok", axis=1, tiled=True),
        lax.all_gather(w_out, "tok", axis=1, tiled=True),
        lax.all_gather(w_up, "tok", axis=1, tiled=True),
        lax.all_gather(w_down, "tok", axis=0, tiled=True),
    )
    catalog = lax.broadcasted_iota(jnp.int32, (1, 1, wave_table.shape[0]), 2)
    picked = (wave_index[0][:, :, None] == catalog).astype(jnp.float32)
    lengths_all = jnp.sum(picked * wave_table, axis=-1)
    hyper_input = wave_features(lengths_all, hyper_dim)
    band_feats, bias_feats = hyper_layer(hyper_input, hyper_params)
    band_low = band_feats.astype(jnp.bfloat16).reshape(-1, hyper_dim)
    own_input = lax.dynamic_slice_in_dim(hyper_input, band_place * own_images, own_images, 0)

    def run_hyper(params):
        return hyper_layer(own_input, params)

    if paired:
        bias_own = lax.dynamic_slice_in_dim(
            bias_feats, band_place * own_images, own_images, 0
        )
    else:
        (_, bias_own), hyper_back = jax.vjp(run_hyper, hyper_params)
    if paired:
        ordered = (
            band_feats.astype(jnp.bfloat16)
            .reshape(group_images // 2, 2, owners, band_share, hyper_dim)
            .transpose(0, 2, 1, 3, 4)
        )
        even_rows = ordered.reshape(-1, hyper_dim)
        odd_rows = ordered[:, :, ::-1].reshape(-1, hyper_dim)
        kernel_lined = make_kernels(
            gen_grid, even_rows, odd_rows, group_images, owners, factor
        )
        convolved = embed_parts(kernel_lined, pixel_lined, model_dim, 1)
    else:
        pixel_slices = pixel_blocks.transpose(1, 2, 0, 3, 4).reshape(
            group_images, slice_pixels * all_bands, slot_count
        )
        kernels = (
            jnp.einsum("pdc,nc->pnd", gen_grid, band_low, preferred_element_type=jnp.float32) * factor
        ).astype(jnp.bfloat16)
        kernel_grid = kernels.reshape(slice_pixels, group_images, all_bands, model_dim)
        kernel_rows = kernel_grid.transpose(1, 0, 2, 3).reshape(
            group_images, slice_pixels * all_bands, model_dim
        )
        product = jnp.einsum(
            "iks,ikd->isd", pixel_slices, kernel_rows, preferred_element_type=jnp.float32
        )
        convolved = lax.psum_scatter(
            product.reshape(group_images * slot_count, model_dim).astype(jnp.bfloat16),
            "band",
            scatter_dimension=0,
            tiled=True,
        ).astype(jnp.float32)
    bias_rows = jnp.dot(bias_own, gen_b, precision=PRECISE)
    embedded = convolved.reshape(own_images, slot_count, model_dim) + bias_rows[:, None, :]
    usable = lax.broadcasted_iota(jnp.int32, (own_images, slot_count), 1) < patch_count[0][:, None]
    stored = block_forward(embedded, usable, weights_full, ln1_gain, ln2_gain)
    row_mask = usable.reshape(-1, 1)
    layer_out = (
        jnp.where(row_mask, stored[-1], 0.0)
        .astype(jnp.bfloat16)
        .reshape(1, own_images, slot_count, model_dim)
    )
    grad_rows = jnp.where(row_mask, d_out[0].reshape(-1, model_dim).astype(jnp.float32), 0.0)
    d_embed, block_terms = block_backward(
        stored, usable, grad_rows, weights_full, ln1_gain, ln2_gain
    )
    d_embed_low = d_embed.astype(jnp.bfloat16).reshape(own_images, slot_count, model_dim)
    d_bias = jnp.sum(d_embed.reshape(own_images, slot_count, model_dim), axis=1)
    d_bias_feat = jnp.dot(d_bias, gen_b.T, precision=PRECISE)
    grad_gen_b = jnp.dot(bias_own.T, d_bias, precision=PRECISE)
    qkv_turned, out_turned, up_turned, grad_down, gain_one, gain_two = block_terms
    weight_terms = [
        term.astype(jnp.bfloat16) for term in (qkv_turned, out_turned, up_turned, grad_down)
    ]
    gain_rows = model_dim // hyper_dim
    gain_lines = [gain_one.reshape(-1, hyper_dim), gain_two.reshape(-1, hyper_dim)]
    fill = -(3 + 2 * gain_rows) % 16
    gain_lines.append(jnp.zeros((fill, hyper_dim), jnp.float32))
    if paired:
        grad_blocks, weight_sums, grad_gen_w, whole, layer_rows = tail_call(
            gen_grid,
            pixel_lined,
            kernel_lined,
            [stored[10], weights_full[3], stored[7]],
            d_embed_low.reshape(slot_count, model_dim),
            even_rows,
            odd_rows,
            weight_terms,
            own_input[0],
            bias_token[None],
            d_bias_feat,
            [
                hyper_query,
                hyper_key,
                hyper_value,
                hyper_out,
                hyper_up,
                hyper_down,
                hyper_gain1[None],
                hyper_gain2[None],
            ],
            grad_gen_b,
            jnp.concatenate([jnp.zeros((3, hyper_dim), jnp.float32)] + gain_lines),
            factor,
            2,
        )
        devices = owners * lax.axis_size("tok")
        (
            pixel_grad,
            qkv_sum,
            out_sum,
            up_sum,
            down_sum,
            query_sum,
            key_sum,
            value_sum,
            mix_sum,
            expand_sum,
            shrink_sum,
            gen_b_sum,
            line_sum,
        ) = unturn_pixels(
            grad_blocks,
            pixels.shape[1:],
            weight_sums,
            [term.shape[0] // devices for term in weight_terms],
            whole,
            [part.shape for part in hyper_params[1:7]]
            + [gen_b.shape, (3 + 2 * gain_rows + fill, hyper_dim)],
        )
        pixel_grad = pixel_grad[None]
        layer_out = jnp.where(row_mask, layer_rows, jnp.zeros_like(layer_rows)).reshape(
            1, own_images, slot_count, model_dim
        )
    else:
        d_gathered = lax.all_gather(d_embed_low, "band", axis=0, tiled=True)
        grad_slices = jnp.einsum(
            "ikd,isd->iks", kernel_rows, d_gathered, preferred_element_type=jnp.float32
        ).astype(jnp.bfloat16)
        grad_slices = grad_slices.reshape(
            group_images, slice_pixels, owners, band_share, slot_count
        ).transpose(2, 0, 1, 3, 4)
        d_kernel = jnp.einsum(
            "iks,isd->ikd", pixel_slices, d_gathered, preferred_element_type=jnp.float32
        ).astype(jnp.bfloat16)
        d_kernel = (
            d_kernel.reshape(group_images, slice_pixels, all_bands, model_dim)
            .transpose(1, 0, 2, 3)
            .reshape(slice_pixels, group_images * all_bands, model_dim)
        )
        d_band_part = (
            jnp.einsum("pnd,pdc->nc", d_kernel, gen_grid, preferred_element_type=jnp.float32) * factor
        )
        d_band_own = lax.psum_scatter(d_band_part, "band", scatter_dimension=0, tiled=True)
        gen_part_grad = (
            jnp.einsum("pnd,nc->pdc", d_kernel, band_low, preferred_element_type=jnp.float32) * factor
        )
        gen_low = gen_part_grad.reshape(-1, hyper_dim).astype(jnp.bfloat16)
        grad_slices = lax.all_to_all(grad_slices, "band", 0, 0, tiled=True)
        pixel_grad = grad_slices.transpose(1, 3, 4, 0, 2).reshape(pixels.shape)
        (
            grad_token,
            grad_query,
            grad_key,
            grad_value,
            grad_mix,
            grad_expand,
            grad_shrink,
            grad_first_gain,
            grad_second_gain,
        ) = hyper_back((d_band_own.reshape(own_images, all_bands, hyper_dim), d_bias_feat))[0]
        lines = jnp.concatenate(
            [grad_token[None], grad_first_gain[None], grad_second_gain[None]] + gain_lines
        )
        (
            qkv_sum,
            out_sum,
            up_sum,
            down_sum,
            grad_gen_w,
            query_sum,
            key_sum,
            value_sum,
            mix_sum,
            expand_sum,
            shrink_sum,
            gen_b_sum,
            line_sum,
        ) = reduce_all(
            weight_terms + [gen_low],
            [1, 0, 1, 1, 2],
            [2, 1, 2, 2, 2],
            [
                grad_query,
                grad_key,
                grad_value,
                grad_mix,
                grad_expand,
                grad_shrink,
                grad_gen_b,
                lines,
            ],
            3,
        )
    devices = owners * lax.axis_size("tok")
    place = band_place * lax.axis_size("tok") + lax.axis_index("tok")
    gain_share = model_dim // devices

    def own_gain(whole):
        return lax.dynamic_slice_in_dim(whole.reshape(-1), place * gain_share, gain_share, 0)

    return (
        layer_out,
        pixel_grad,
        grad_gen_w,
        gen_b_sum,
        line_sum[0],
        query_sum,
        key_sum,
        value_sum,
        mix_sum,
        expand_sum,
        shrink_sum,
        line_sum[1],
        line_sum[2],
        qkv_sum.T,
        out_sum.T,
        up_sum.T,
        down_sum,
        own_gain(line_sum[3 : 3 + gain_rows]),
        own_gain(line_sum[3 + gain_rows : 3 + 2 * gain_rows]),
    )


def solution(mesh):
    placed = (
        P("tok", None, "band", None, None),
        P(),
        P("tok", None, None),
        P("tok", "band"),
        P("tok", "band", None, None),
        P(("band", "tok"), None),
        P(),
        P(),
        P(),
        P(),
        P(),
        P(),
        P(),
        P(),
        P(),
        P(),
        P(None, "tok"),
        P(None, "tok"),
        P(None, "tok"),
        P("tok", None),
        P(),
        P(),
    )
    return jax.shard_map(
        body,
        mesh=mesh,
        in_specs=placed,
        out_specs=(
            P("tok", "band", None, None),
            P("tok", None, "band", None, None),
            P(("band", "tok"), None),
            P(),
            P(),
            P(),
            P(),
            P(),
            P(),
            P(),
            P(),
            P(),
            P(),
            P(None, ("band", "tok")),
            P(None, ("band", "tok")),
            P(None, ("band", "tok")),
            P(("band", "tok"), None),
            P(("band", "tok")),
            P(("band", "tok")),
        ),
        check_vma=False,
    )
```
